256 devices in a mesh: gx: 32 (over y, x, core), gy: 8 (over z).
Axes of the slice: x: 4, y: 4, z: 8, core: 2. Of those that a mesh axis runs over, the one named last changes fastest.
Arguments:
- displacement: float32 [3, 32, 256, 1024], P(None, None, 'gx', 'gy'), may hold values from -6 to 6
- velocity: float32 [3, 32, 256, 1024], P(None, None, 'gx', 'gy'), may hold values from -6 to 6
- slopes: float32 [2, 32, 256, 1024], P(None, None, 'gx', 'gy'), may hold values from -0.5 to 0.5
- stretch: float32 [32, 256, 1024], P(None, 'gx', 'gy'), may hold values from 0.6 to 1.4
- moduli: float32 [2, 32, 256, 1024], P(None, None, 'gx', 'gy'), may hold values from 0.3 to 1
- buoyancy: float32 [32, 256, 1024], P(None, 'gx', 'gy'), may hold values from 0.5 to 1.5
- probes: float32 [4, 512, 128], P(None, 'gy'), may hold values from -0.0017089844 to 0.0017089844
Outputs:
- final_displacement: float32 [3, 32, 256, 1024], P(None, None, 'gx', 'gy')
- basis: float32 [128, 48, 128], P('gx', 'gy')
- factor: float32 [128, 128], replicated
The draws below stay inside these ranges and needn't reach their ends.
All inputs are finite; a program needn't handle non-finite values.
Results may differ from the reference program's by a relative error of at most 0.0003.
Values sent between devices are 32-bit elements; how exact they have to be, the bound alone decides.
A program may use at most 64 MiB of HBM per device.

```python
import math
import jax
import jax.numpy as jnp
from jax import lax

NZ = 32
STEPS = 4
SKETCH = 128
NX = 256
NY = 1024
ROWS = 6144


def shard_levels(stream_key, extent, shards, least, largest):
    gain = 1.0
    for dim, blocks in shards:
        heights = jax.random.uniform(jax.random.fold_in(jax.random.fold_in(stream_key, 6), dim), (blocks,), jnp.float32, least / len(shards), largest / len(shards))
        gain = gain * jnp.repeat(jnp.exp(heights), extent[dim] // blocks).reshape((-1,) + (1,) * (len(extent) - 1 - dim))
    return gain


def normal_values(own_key, extent, scale, most, split=(), kind=jnp.bfloat16):
    entries = scale * jax.random.normal(own_key, extent, jnp.float32)
    if split:
        entries = entries * shard_levels(own_key, extent, split, -0.22, 0.18)
    return jnp.clip(entries, -most, most).astype(kind)


def setup_inputs(seed: int = 0) -> dict:
    keys = jax.random.split(jax.random.key(seed), 8)
    displacement = normal_values(keys[0], (3, NZ, NX, NY), 1.0, 6.0, ((2, 32), (3, 8)), jnp.float32)
    velocity = normal_values(keys[1], (3, NZ, NX, NY), 1.0, 6.0, ((2, 32), (3, 8)), jnp.float32)
    slopes = jnp.clip(jax.random.uniform(keys[2], (2, NZ, NX, NY), jnp.float32, -0.5, 0.5) * shard_levels(keys[2], (2, NZ, NX, NY), ((2, 32), (3, 8)), -0.4, 0.0), -0.5, 0.5)
    stretch = jnp.clip(0.6 + 0.79999995 * jax.random.uniform(keys[3], (NZ, NX, NY), jnp.float32) ** shard_levels(keys[3], (NZ, NX, NY), ((1, 32), (2, 8)), -0.2, 0.2), 0.6, 1.4)
    moduli = jnp.clip(0.3 + 0.7 * jax.random.uniform(keys[4], (2, NZ, NX, NY), jnp.float32) ** shard_levels(keys[4], (2, NZ, NX, NY), ((2, 32), (3, 8)), -0.2, 0.2), 0.3, 1.0)
    buoyancy = jnp.clip(jnp.exp(math.log(1.5) - 1.0986123 * jax.random.uniform(keys[5], (NZ, NX, NY), jnp.float32) ** shard_levels(keys[5], (NZ, NX, NY), ((1, 32), (2, 8)), -0.2, 0.2)), 0.5, 1.5)
    probes = normal_values(keys[6], (STEPS, NY // 2, SKETCH), (STEPS * (NY // 2) * ROWS) ** -0.5, 0.0017089844, ((1, 8),), jnp.float32)
    return dict(displacement=displacement, velocity=velocity, slopes=slopes, stretch=stretch, moduli=moduli, buoyancy=buoyancy, probes=probes)


time_step = 0.12

def fourth(values, dimension):
    length_out = values.shape[dimension] - 4

    def segment(offset):
        return lax.slice_in_dim(values, offset, offset + length_out, axis=dimension)
    return (segment(0) - segment(4) + 8.0 * (segment(3) - segment(1))) / 12.0

def vertical(values):
    padded = jnp.pad(values, ((0, 0), (2, 2), (0, 0), (0, 0)))
    return fourth(padded, 1)

def gradient(padded, slope_x, slope_y, stretch):
    d_x = fourth(padded[:, :, :, 2:-2], 2)
    d_y = fourth(padded[:, :, 2:-2, :], 3)
    d_r = vertical(padded[:, :, 2:-2, 2:-2])
    return jnp.stack([d_x + slope_x * d_r, d_y + slope_y * d_r, stretch * d_r], axis=1)

def stresses(gradients, lame, shear):
    divergence = gradients[0, 0] + gradients[1, 1] + gradients[2, 2]
    pressure = lame * divergence
    return jnp.stack([pressure + 2.0 * shear * gradients[0, 0], pressure + 2.0 * shear * gradients[1, 1], pressure + 2.0 * shear * gradients[2, 2], shear * (gradients[0, 1] + gradients[1, 0]), shear * (gradients[0, 2] + gradients[2, 0]), shear * (gradients[1, 2] + gradients[2, 1])])

def forces(padded, slope_x, slope_y, stretch):
    d_x = fourth(padded[:, :, :, 2:-2], 2)
    d_y = fourth(padded[:, :, 2:-2, :], 3)
    d_r = vertical(padded[:, :, 2:-2, 2:-2])
    rows_x = (0, 3, 4)
    rows_y = (3, 1, 5)
    rows_z = (4, 5, 2)
    return jnp.stack([d_x[rows_x[component]] + slope_x * d_r[rows_x[component]] + d_y[rows_y[component]] + slope_y * d_r[rows_y[component]] + stretch * d_r[rows_z[component]] for component in range(3)])

def reference(displacement, velocity, slopes, stretch, moduli, buoyancy, probes):
    margin = ((0, 0), (0, 0), (2, 2), (2, 2))
    previous = displacement - time_step * velocity
    current = displacement
    sketch = jnp.zeros((NX // 2, 3 * (NZ // 2), SKETCH), jnp.float32)
    for moment in range(STEPS):
        gradients = gradient(jnp.pad(current, margin), slopes[0], slopes[1], stretch)
        stress = stresses(gradients, moduli[0], moduli[1])
        pushes = buoyancy * forces(jnp.pad(stress, margin), slopes[0], slopes[1], stretch)
        following = 2.0 * current - previous + time_step ** 2 * pushes
        velocities = (following - previous) / (2.0 * time_step)
        sampled = velocities[:, ::2, ::2, ::2]
        sketch_term = jnp.einsum('czxy,yk->xczk', sampled, probes[moment], precision=lax.Precision.HIGHEST)
        sketch = sketch + sketch_term.reshape(NX // 2, 3 * (NZ // 2), SKETCH)
        previous, current = (current, following)
    tall_block = sketch.reshape(-1, SKETCH)
    orthonormal, upper_part = jnp.linalg.qr(tall_block)
    diag_signs = jnp.sign(jnp.diagonal(upper_part))
    factor = upper_part * diag_signs[:, None]
    orthonormal = orthonormal * diag_signs[None, :]
    basis = (jnp.sqrt(jnp.float32(ROWS)) * orthonormal).reshape(sketch.shape)
    return (current, basis, factor)
```

```python
import functools
import math

import jax
import jax.numpy as jnp
from jax import lax
from jax.experimental import pallas as pl
from jax.experimental.pallas import tpu as pltpu
from jax.sharding import PartitionSpec as P

STEPS = 4
DT = 0.12
MESH = pl.DeviceIdType.MESH
HIGH = lax.Precision.HIGHEST
F32 = jnp.float32
ZP = 48
VMEM = pltpu.MemorySpace.VMEM


def lanes():
    return lax.broadcasted_iota(jnp.int32, (8, 128), 1)


def shifted(f, h, lane):
    m2 = pltpu.roll(jnp.where(lane >= 126, h, f), 2, 1)
    m1 = pltpu.roll(jnp.where(lane >= 127, h, f), 1, 1)
    p1 = pltpu.roll(jnp.where(lane < 1, h, f), 127, 1)
    p2 = pltpu.roll(jnp.where(lane < 2, h, f), 126, 1)
    return m2, m1, p1, p2


def combine(m2, m1, p1, p2):
    return (m2 - p2) + 8.0 * (p1 - m1)


def wave_kernel(
    disp, vel, slopes, stretch, moduli, buoy, probes,
    out, pieces,
    U, S, MET, RATE, PE, SK, PU, PS, HU, HS,
    send_u, recv_u, send_s, recv_s,
):
    gx, gy = lax.axis_index("gx"), lax.axis_index("gy")
    nx, ny = lax.axis_size("gx"), lax.axis_size("gy")
    left = (lax.rem(gx + nx - 1, nx), gy)
    right = (lax.rem(gx + 1, nx), gy)
    down = (gx, lax.rem(gy + ny - 1, ny))
    up = (gx, lax.rem(gy + 1, ny))
    barrier = pltpu.get_barrier_semaphore()
    for peer in (left, right, down, up):
        pl.semaphore_signal(barrier, inc=1, device_id=peer, device_id_type=MESH)

    lane = lanes()
    zero8 = jnp.zeros((8, 128), F32)

    @pl.loop(0, 12)
    def _(x):
        for s in range(2):
            for c in range(3):
                U[s, c, x, 0:8, :] = zero8
                U[s, c, x, 40:48, :] = zero8
        for c in range(6):
            S[c, x, 0:8, :] = zero8
            S[c, x, 40:48, :] = zero8

    for n in range(STEPS):
        PE[n] = jnp.zeros((128, 128), F32)
        PE[n, pl.ds(0, 64, stride=2), :] = probes[n] * (1.0 / (2.0 * DT))
    SK[...] = jnp.zeros_like(SK)

    def load(x, carry):
        packed = list(carry)
        for zb in range(4):
            rows = pl.ds(zb * 64 + x, 8, stride=8)
            zs = slice(zb * 8, zb * 8 + 8)
            zu = slice(zb * 8 + 8, zb * 8 + 16)
            MET[0, x, zs, :] = slopes[0, rows, :]
            MET[1, x, zs, :] = slopes[1, rows, :]
            MET[2, x, zs, :] = stretch[rows, :]
            MET[3, x, zs, :] = moduli[0, rows, :] * (1.0 / 12.0)
            MET[4, x, zs, :] = moduli[1, rows, :] * (1.0 / 12.0)
            MET[5, x, zs, :] = buoy[rows, :] * (DT * DT / 12.0)
            k = x * 4 + zb
            for c in range(3):
                d = disp[c, rows, :]
                U[0, c, x + 2, zu, :] = d
                U[1, c, x + 2, zu, :] = d - DT * vel[c, rows, :]
                packed[c] = jnp.where((lane >> 2) == k, pltpu.roll(d, 4 * k + 2, 1), packed[c])
        return tuple(packed)

    packed = lax.fori_loop(0, 8, load, (zero8,) * 3)
    pl.semaphore_wait(barrier, 4)

    def exchange(planes, halo_lo, halo_hi, own_lo, own_hi, packed_ref, halo_ref, send, recv):
        copies = [
            pltpu.make_async_remote_copy(
                src_ref=planes(own_lo), dst_ref=planes(halo_hi), send_sem=send.at[0], recv_sem=recv.at[0],
                device_id=left, device_id_type=MESH),
            pltpu.make_async_remote_copy(
                src_ref=planes(own_hi), dst_ref=planes(halo_lo), send_sem=send.at[1], recv_sem=recv.at[1],
                device_id=right, device_id_type=MESH),
            pltpu.make_async_remote_copy(
                src_ref=packed_ref, dst_ref=halo_ref.at[1], send_sem=send.at[2], recv_sem=recv.at[2],
                device_id=down, device_id_type=MESH),
            pltpu.make_async_remote_copy(
                src_ref=packed_ref, dst_ref=halo_ref.at[0], send_sem=send.at[3], recv_sem=recv.at[3],
                device_id=up, device_id_type=MESH),
        ]
        for copy in copies:
            copy.start()
        return copies

    low_part = (lane & 3) < 2

    def halo_of(halo_ref, c):
        lo = jnp.where(gy == 0, zero8, halo_ref[0, c])
        hi = jnp.where(gy == ny - 1, zero8, halo_ref[1, c])
        return jnp.where(low_part, lo, hi)

    def clear(planes_at):
        zeros = jnp.zeros((3, 2, 32, 128), F32)

        @pl.when(gx == 0)
        def _():
            planes_at(slice(0, 2))[...] = zeros

        @pl.when(gx == nx - 1)
        def _():
            planes_at(slice(10, 12))[...] = zeros

    for c in range(3):
        PU[c] = packed[c]

    def step(n, carry):
        cur = lax.rem(n, 2)
        old = 1 - cur

        def u_planes(xs):
            return U.at[cur, :, xs, 8:40, :]

        def s_planes(xs):
            return S.at[0:3, xs, 8:40, :]

        copies = exchange(u_planes, slice(0, 2), slice(10, 12), slice(2, 4), slice(8, 10), PU, HU, send_u, recv_u)

        @pl.when(n > 0)
        def _():
            sketch(n - 1)

        for copy in copies:
            copy.wait()
        clear(u_planes)
        halos = [halo_of(HU, c) for c in range(3)]

        def stress(x, packed):
            packed = list(packed)
            for zb in range(4):
                z0 = zb * 8
                zs = slice(z0, z0 + 8)
                zu = slice(z0 + 8, z0 + 16)
                k = x * 4 + zb
                sx, sy, st = MET[0, x, zs, :], MET[1, x, zs, :], MET[2, x, zs, :]
                lam, mu = MET[3, x, zs, :], MET[4, x, zs, :]
                g = []
                for c in range(3):
                    f = U[cur, c, x + 2, zu, :]
                    dx = combine(U[cur, c, x, zu, :], U[cur, c, x + 1, zu, :],
                                 U[cur, c, x + 3, zu, :], U[cur, c, x + 4, zu, :])
                    dr = combine(*[U[cur, c, x + 2, z0 + o:z0 + o + 8, :] for o in (6, 7, 9, 10)])
                    dy = combine(*shifted(f, pltpu.roll(halos[c], 126 - 4 * k, 1), lane))
                    g.append((dx + sx * dr, dy + sy * dr, st * dr))
                pressure = lam * (g[0][0] + g[1][1] + g[2][2])
                mu2 = mu + mu
                sxy = mu * (g[0][1] + g[1][0])
                syy = pressure + mu2 * g[1][1]
                syz = mu * (g[1][2] + g[2][1])
                S[0, x + 2, zu, :] = pressure + mu2 * g[0][0]
                S[1, x + 2, zu, :] = sxy
                S[2, x + 2, zu, :] = mu * (g[0][2] + g[2][0])
                S[3, x + 2, zu, :] = syy
                S[4, x + 2, zu, :] = syz
                S[5, x + 2, zu, :] = pressure + mu2 * g[2][2]
                here = (lane >> 2) == k
                for i, s in enumerate((sxy, syy, syz)):
                    packed[i] = jnp.where(here, pltpu.roll(s, 4 * k + 2, 1), packed[i])
            return tuple(packed)

        packed = lax.fori_loop(0, 8, stress, (zero8,) * 3)
        for i in range(3):
            PS[i] = packed[i]
        copies = exchange(s_planes, slice(0, 2), slice(10, 12), slice(2, 4), slice(8, 10), PS, HS, send_s, recv_s)
        for copy in copies:
            copy.wait()
        clear(s_planes)
        halos_s = [halo_of(HS, c) for c in range(3)]

        def forces(x, packed):
            packed = list(packed)
            for zb in range(4):
                z0 = zb * 8
                zs = slice(z0, z0 + 8)
                zu = slice(z0 + 8, z0 + 16)
                k = x * 4 + zb
                sx, sy, st, b = (MET[i, x, zs, :] for i in (0, 1, 2, 5))

                def d_x(i):
                    return combine(S[i, x, zu, :], S[i, x + 1, zu, :], S[i, x + 3, zu, :], S[i, x + 4, zu, :])

                def d_y(i, h):
                    f = S[i, x + 2, zu, :]
                    return combine(*shifted(f, pltpu.roll(h, 126 - 4 * k, 1), lane))

                dr = [combine(*[S[i, x + 2, z0 + o:z0 + o + 8, :] for o in (6, 7, 9, 10)]) for i in range(6)]
                acc = (
                    d_x(0) + sx * dr[0] + d_y(1, halos_s[0]) + sy * dr[1] + st * dr[2],
                    d_x(1) + sx * dr[1] + d_y(3, halos_s[1]) + sy * dr[3] + st * dr[4],
                    d_x(2) + sx * dr[2] + d_y(4, halos_s[2]) + sy * dr[4] + st * dr[5],
                )
                here = (lane >> 2) == k
                for c in range(3):
                    u = U[cur, c, x + 2, zu, :]
                    p = U[old, c, x + 2, zu, :]
                    fol = (u + u - p) + b * acc[c]
                    U[old, c, x + 2, zu, :] = fol
                    RATE[c, x, zs, :] = fol - p
                    packed[c] = jnp.where(here, pltpu.roll(fol, 4 * k + 2, 1), packed[c])
            return tuple(packed)

        packed = lax.fori_loop(0, 8, forces, (zero8,) * 3)
        for c in range(3):
            PU[c] = packed[c]
        return carry

    def sketch(n):
        lhs = jnp.concatenate(
            [RATE[c, 2 * xh, pl.ds(0, 16, stride=2), :] for xh in range(4) for c in range(3)], axis=0)
        SK[...] += jnp.dot(lhs, PE[n], precision=HIGH, preferred_element_type=F32)

    lax.fori_loop(0, STEPS, step, 0)
    sketch(STEPS - 1)
    for g in range(8):
        for xh in range(4):
            pieces[g, 6 * xh:6 * xh + 6, :] = SK[xh * 48 + 6 * g:xh * 48 + 6 * g + 6, :]

    final = STEPS % 2

    @pl.loop(0, 8)
    def _(x):
        for zb in range(4):
            for c in range(3):
                out[c, pl.ds(zb * 64 + x, 8, stride=8), :] = U[final, c, x + 2, zb * 8 + 8:zb * 8 + 16, :]


def wave(disp, vel, slopes, stretch, moduli, buoy, probes):
    return pl.pallas_call(
        wave_kernel,
        name="wave",
        out_shape=(jax.ShapeDtypeStruct((3, 256, 128), F32), jax.ShapeDtypeStruct((8, 24, 128), F32)),
        in_specs=[pl.BlockSpec(memory_space=VMEM)] * 7,
        out_specs=[pl.BlockSpec(memory_space=VMEM)] * 2,
        scratch_shapes=[
            pltpu.VMEM((2, 3, 12, ZP, 128), F32),
            pltpu.VMEM((6, 12, ZP, 128), F32),
            pltpu.VMEM((6, 8, 32, 128), F32),
            pltpu.VMEM((3, 8, 32, 128), F32),
            pltpu.VMEM((STEPS, 128, 128), F32),
            pltpu.VMEM((192, 128), F32),
            pltpu.VMEM((3, 8, 128), F32),
            pltpu.VMEM((3, 8, 128), F32),
            pltpu.VMEM((2, 3, 8, 128), F32),
            pltpu.VMEM((2, 3, 8, 128), F32),
            pltpu.SemaphoreType.DMA((4,)),
            pltpu.SemaphoreType.DMA((4,)),
            pltpu.SemaphoreType.DMA((4,)),
            pltpu.SemaphoreType.DMA((4,)),
        ],
        compiler_params=pltpu.CompilerParams(
            collective_id=0, has_side_effects=True, vmem_limit_bytes=32 * 1024 * 1024),
    )(disp, vel, slopes, stretch, moduli, buoy, probes)


def gram_kernel(pieces, tall, gram, RB, GL, RA, PA, RBB, GS,
                s0, r0, s1, r1, s2, r2, s3, r3):
    gx, gy = lax.axis_index("gx"), lax.axis_index("gy")
    core = lax.rem(gx, 2)
    pair = gx - core
    a_me = gy * 2 + core
    b_me = gx // 2

    def a_dev(a):
        return (pair + lax.rem(a, 2), a // 2)

    def b_dev(b):
        return (b * 2 + core, gy)

    barrier = pltpu.get_barrier_semaphore()

    @pl.loop(1, 16)
    def _(d):
        pl.semaphore_signal(barrier, inc=1, device_id=a_dev(lax.rem(a_me + d, 16)), device_id_type=MESH)
        pl.semaphore_signal(barrier, inc=1, device_id=b_dev(lax.rem(b_me + d, 16)), device_id_type=MESH)

    pl.semaphore_wait(barrier, 30)

    def copy0(g):
        return pltpu.make_async_remote_copy(
            src_ref=pieces.at[g], dst_ref=RB.at[gy], send_sem=s0.at[g], recv_sem=r0.at[gy],
            device_id=(gx, g), device_id_type=MESH)

    def wait0(g):
        return pltpu.make_async_remote_copy(
            src_ref=pieces.at[g], dst_ref=RB.at[g], send_sem=s0.at[g], recv_sem=r0.at[g],
            device_id=(gx, g), device_id_type=MESH)

    @pl.loop(1, 8)
    def _(d):
        copy0(lax.rem(gy + d, 8)).start()

    RB[gy] = pieces[gy]

    @pl.loop(1, 8)
    def _(d):
        wait0(lax.rem(gy + d, 8)).wait()

    total = RB[0]
    for g in range(1, 8):
        total = total + RB[g]
    tall[...] = total
    GL[...] = lax.dot_general(
        total, total, (((0,), (0,)), ((), ())), precision=HIGH, preferred_element_type=F32).reshape(16, 8, 128)

    def group(d, dev, me, src, dst, send, recv):
        def make(slot, peer):
            return pltpu.make_async_remote_copy(
                src_ref=src(peer), dst_ref=dst.at[slot], send_sem=send.at[peer], recv_sem=recv.at[slot],
                device_id=dev(peer), device_id_type=MESH)

        @pl.loop(1, 16)
        def _(d):
            make(me, lax.rem(me + d, 16)).start()

        def finish():
            @pl.loop(1, 16)
            def _(d):
                peer = lax.rem(me + d, 16)
                make(peer, peer).wait()

        return finish

    def summed(ref):
        parts = [ref[i] for i in range(16)]
        while len(parts) > 1:
            parts = [parts[i] + parts[i + 1] for i in range(0, len(parts), 2)]
        return parts[0]

    finish = group(0, a_dev, a_me, lambda p: GL.at[p], RA, s1, r1)
    RA[a_me] = GL[a_me]
    finish()
    part = summed(RA)
    PA[...] = part
    finish = group(0, b_dev, b_me, lambda p: PA, RBB, s2, r2)
    RBB[b_me] = part
    finish()
    whole = summed(RBB)
    GS[...] = whole
    finish = group(0, a_dev, a_me, lambda p: GS, gram, s3, r3)
    gram[a_me] = whole
    finish()


def gram_reduce(pieces):
    sem = pltpu.SemaphoreType.DMA
    return pl.pallas_call(
        gram_kernel,
        name="gram",
        out_shape=(jax.ShapeDtypeStruct((24, 128), F32), jax.ShapeDtypeStruct((16, 8, 128), F32)),
        in_specs=[pl.BlockSpec(memory_space=VMEM)],
        out_specs=[pl.BlockSpec(memory_space=VMEM)] * 2,
        scratch_shapes=[
            pltpu.VMEM((8, 24, 128), F32),
            pltpu.VMEM((16, 8, 128), F32),
            pltpu.VMEM((16, 8, 128), F32),
            pltpu.VMEM((8, 128), F32),
            pltpu.VMEM((16, 8, 128), F32),
            pltpu.VMEM((8, 128), F32),
            sem((8,)), sem((8,)), sem((16,)), sem((16,)), sem((16,)), sem((16,)), sem((16,)), sem((16,)),
        ],
        compiler_params=pltpu.CompilerParams(collective_id=1, has_side_effects=True),
    )(pieces)


def factor_kernel(scale, gram, tall, disp, basis, factor, out, sem):
    copy = pltpu.make_async_copy(disp, out, sem)
    copy.start()
    lane = lanes()
    sub = lax.broadcasted_iota(jnp.int32, (8, 128), 0)
    a = [gram[i] for i in range(16)]
    for j in range(128):
        b, s = divmod(j, 8)
        col = jnp.broadcast_to(a[b][:, j:j + 1], (8, 128))
        row = jnp.broadcast_to(a[b][s:s + 1, :], (8, 128))
        pivot = jnp.broadcast_to(col[s:s + 1, :], (8, 128))
        inv = 1.0 / pivot
        here = lane == j
        scaled = jnp.where(here, 1.0, row) * inv
        for i in range(b, 16):
            if i == b:
                if s == 7:
                    continue
                m = jnp.where(sub > s, col, 0.0)
                a[i] = jnp.where(here & (sub > s), 0.0, a[i]) - m * scaled
            else:
                m = jnp.broadcast_to(a[i][:, j:j + 1], (8, 128))
                a[i] = jnp.where(here, 0.0, a[i]) - m * scaled
    inverse = []
    for i in range(16):
        rows = sub + 8 * i
        diag = jnp.sum(jnp.where(lane == rows, a[i], 0.0), axis=1, keepdims=True)
        root = lax.rsqrt(diag)
        factor[8 * i:8 * i + 8, :] = jnp.where(lane >= rows, a[i], 0.0) * root
        inverse.append(jnp.where(lane == rows, 1.0, jnp.where(lane < rows, a[i], 0.0)) * (root * scale))
    inverse = jnp.concatenate(inverse, axis=0)
    q = lax.dot_general(
        tall[...], inverse, (((1,), (1,)), ((), ())), precision=HIGH, preferred_element_type=F32)
    for xh in range(4):
        basis[xh] = q[6 * xh:6 * xh + 6, :]
    copy.wait()


def finish(gram, tall, disp, scale):
    return pl.pallas_call(
        functools.partial(factor_kernel, scale),
        name="factor",
        out_shape=(
            jax.ShapeDtypeStruct((4, 6, 128), F32),
            jax.ShapeDtypeStruct((128, 128), F32),
            jax.ShapeDtypeStruct((3, 256, 128), F32),
        ),
        in_specs=[pl.BlockSpec(memory_space=VMEM)] * 2 + [pl.BlockSpec(memory_space=pl.ANY)],
        out_specs=[pl.BlockSpec(memory_space=VMEM)] * 2 + [pl.BlockSpec(memory_space=pl.ANY)],
        scratch_shapes=[pltpu.SemaphoreType.DMA],
    )(gram, tall, disp)


def shards(displacement, velocity, slopes, stretch, moduli, buoyancy, probes):
    moved, pieces = wave(
        displacement.reshape(3, 256, 128), velocity.reshape(3, 256, 128), slopes.reshape(2, 256, 128),
        stretch.reshape(256, 128), moduli.reshape(2, 256, 128), buoyancy.reshape(256, 128), probes)
    tall, gram = gram_reduce(pieces)
    rows = tall.shape[0] * lax.axis_size("gx") * lax.axis_size("gy")
    basis, factor, moved = finish(gram, tall, moved, math.sqrt(rows))
    return moved.reshape(3, 32, 8, 128), basis, factor


def solution(mesh):
    in_specs = (
        P(None, None, "gx", "gy"),
        P(None, None, "gx", "gy"),
        P(None, None, "gx", "gy"),
        P(None, "gx", "gy"),
        P(None, None, "gx", "gy"),
        P(None, "gx", "gy"),
        P(None, "gy", None),
    )
    out_specs = (P(None, None, "gx", "gy"), P("gx", "gy", None), P())
    return jax.shard_map(shards, mesh=mesh, in_specs=in_specs, out_specs=out_specs, check_vma=False)
```

```python
import functools
import math

import jax
import jax.numpy as jnp
from jax import lax
from jax.experimental import pallas as pl
from jax.experimental.pallas import tpu as pltpu
from jax.sharding import PartitionSpec as P

STEPS = 4
DT = 0.12
MESH = pl.DeviceIdType.MESH
HIGH = lax.Precision.HIGHEST
F32 = jnp.float32
ZP = 48
VMEM = pltpu.MemorySpace.VMEM
VMEM_LIMIT = 63 * 1024 * 1024


def lanes():
    return lax.broadcasted_iota(jnp.int32, (8, 128), 1)


def shifted(f, h, lane):
    m2 = pltpu.roll(jnp.where(lane >= 126, h, f), 2, 1)
    m1 = pltpu.roll(jnp.where(lane >= 127, h, f), 1, 1)
    p1 = pltpu.roll(jnp.where(lane < 1, h, f), 127, 1)
    p2 = pltpu.roll(jnp.where(lane < 2, h, f), 126, 1)
    return m2, m1, p1, p2


def combine(m2, m1, p1, p2):
    return (m2 - p2) + 8.0 * (p1 - m1)


def wave_kernel(
    disp_hbm, vel_hbm, slopes_hbm, stretch_hbm, moduli_hbm, buoy_hbm, probes_hbm,
    tall, gram, out,
    disp, vel, slopes, stretch, moduli, buoy, probes,
    U, S, MET, RATE, PE, SK, PU, PS, HU, HS,
    PIECES, RB, GL, RA, PA, RBB, GS,
    load_sem, out_sem, send_x, recv_x, send_y, recv_y,
    s0, r0, s1, r1, s2, r2, s3, r3,
):
    gx, gy = lax.axis_index("gx"), lax.axis_index("gy")
    nx, ny = lax.axis_size("gx"), lax.axis_size("gy")
    left = (lax.rem(gx + nx - 1, nx), gy)
    right = (lax.rem(gx + 1, nx), gy)
    down = (gx, lax.rem(gy + ny - 1, ny))
    up = (gx, lax.rem(gy + 1, ny))
    has_left, has_right = gx > 0, gx < nx - 1
    core = lax.rem(gx, 2)
    pair = gx - core
    a_me = gy * 2 + core
    b_me = gx // 2

    def a_dev(a):
        return (pair + lax.rem(a, 2), a // 2)

    def b_dev(b):
        return (b * 2 + core, gy)

    loads = [
        pltpu.make_async_copy(src, dst, load_sem.at[i])
        for i, (src, dst) in enumerate((
            (disp_hbm, disp), (vel_hbm, vel), (slopes_hbm, slopes), (stretch_hbm, stretch),
            (moduli_hbm, moduli), (buoy_hbm, buoy), (probes_hbm, probes)))
    ]
    for copy in loads:
        copy.start()

    barrier = pltpu.get_barrier_semaphore()
    for peer in (left, right):
        pl.semaphore_signal(barrier, inc=1, device_id=peer, device_id_type=MESH)

    @pl.loop(1, 16)
    def _(d):
        pl.semaphore_signal(barrier, inc=1, device_id=a_dev(lax.rem(a_me + d, 16)), device_id_type=MESH)
        pl.semaphore_signal(barrier, inc=1, device_id=b_dev(lax.rem(b_me + d, 16)), device_id_type=MESH)

    lane = lanes()
    zero8 = jnp.zeros((8, 128), F32)
    low_part = (lane & 3) < 2

    @pl.loop(0, 12)
    def _(x):
        for s in range(2):
            for c in range(3):
                U[s, c, x, 0:8, :] = zero8
                U[s, c, x, 40:48, :] = zero8
        for c in range(6):
            S[c, x, 0:8, :] = zero8
            S[c, x, 40:48, :] = zero8

    def clear(x):
        for c in range(3):
            for z0 in range(8, 40, 8):
                U[0, c, x, z0:z0 + 8, :] = zero8
                U[1, c, x, z0:z0 + 8, :] = zero8
                S[c, x, z0:z0 + 8, :] = zero8

    @pl.when(gx == 0)
    def _():
        clear(0)
        clear(1)

    @pl.when(gx == nx - 1)
    def _():
        clear(10)
        clear(11)

    def x_copy(ref, kind, side):
        if side == 0:
            return pltpu.make_async_remote_copy(
                src_ref=ref(slice(2, 4)), dst_ref=ref(slice(10, 12)), send_sem=send_x.at[kind, 0],
                recv_sem=recv_x.at[kind, 0], device_id=left, device_id_type=MESH)
        return pltpu.make_async_remote_copy(
            src_ref=ref(slice(8, 10)), dst_ref=ref(slice(0, 2)), send_sem=send_x.at[kind, 1],
            recv_sem=recv_x.at[kind, 1], device_id=right, device_id_type=MESH)

    def x_start(ref, kind):
        @pl.when(has_left)
        def _():
            x_copy(ref, kind, 0).start()

        @pl.when(has_right)
        def _():
            x_copy(ref, kind, 1).start()

    def x_wait(ref, kind):
        @pl.when(has_right)
        def _():
            x_copy(ref, kind, 0).wait_recv()
            x_copy(ref, kind, 1).wait_send()

        @pl.when(has_left)
        def _():
            x_copy(ref, kind, 1).wait_recv()
            x_copy(ref, kind, 0).wait_send()

    def y_copies(packed, halo, kind, part):
        return [
            pltpu.make_async_remote_copy(
                src_ref=packed.at[part], dst_ref=halo.at[part, 1 - d], send_sem=send_y.at[kind, part, d],
                recv_sem=recv_y.at[kind, part, d], device_id=peer, device_id_type=MESH)
            for d, peer in enumerate((down, up))
        ]

    def y_send(values, packed, halo, kind, part):
        for c in range(3):
            packed[part, c] = values[c]
        for copy in y_copies(packed, halo, kind, part):
            copy.start()

    def y_wait(packed, halo, kind, part):
        for copy in y_copies(packed, halo, kind, part):
            copy.wait()
        result = []
        for c in range(3):
            lo = jnp.where(gy == 0, zero8, halo[part, 0, c])
            hi = jnp.where(gy == ny - 1, zero8, halo[part, 1, c])
            result.append(jnp.where(low_part, lo, hi))
        return result

    def u_planes(cur):
        return lambda xs: U.at[cur, :, xs, 8:40, :]

    def s_planes(xs):
        return S.at[0:3, xs, 8:40, :]

    INNER, EDGE = 0, 1

    def plane(part, i):
        return i + 2 if part == INNER else i + 4 * (i // 2)

    loads[0].wait()

    def load_u(part):
        def body(i, carry):
            x = plane(part, i)
            packed = list(carry)
            for zb in range(4):
                rows = pl.ds(zb * 64 + x, 8, stride=8)
                k = x * 4 + zb
                for c in range(3):
                    d = disp[c, rows, :]
                    U[0, c, x + 2, zb * 8 + 8:zb * 8 + 16, :] = d
                    packed[c] = jnp.where((lane >> 2) == k, pltpu.roll(d, 4 * k + 2, 1), packed[c])
            return tuple(packed)

        return lax.fori_loop(0, 4, body, (zero8,) * 3)

    first = [load_u(INNER), load_u(EDGE)]
    pl.semaphore_wait(barrier, 32)
    x_start(u_planes(0), 0)
    for part in (INNER, EDGE):
        y_send(first[part], PU, HU, 0, part)

    for copy in loads[1:]:
        copy.wait()

    @pl.loop(0, 8)
    def _(x):
        for zb in range(4):
            rows = pl.ds(zb * 64 + x, 8, stride=8)
            zs = slice(zb * 8, zb * 8 + 8)
            zu = slice(zb * 8 + 8, zb * 8 + 16)
            MET[0, x, zs, :] = slopes[0, rows, :]
            MET[1, x, zs, :] = slopes[1, rows, :]
            MET[2, x, zs, :] = stretch[rows, :]
            MET[3, x, zs, :] = moduli[0, rows, :] * (1.0 / 12.0)
            MET[4, x, zs, :] = moduli[1, rows, :] * (1.0 / 12.0)
            MET[5, x, zs, :] = buoy[rows, :] * (DT * DT / 12.0)
            for c in range(3):
                U[1, c, x + 2, zu, :] = U[0, c, x + 2, zu, :] - DT * vel[c, rows, :]

    for n in range(STEPS):
        PE[n] = jnp.zeros((128, 128), F32)
        PE[n, pl.ds(0, 64, stride=2), :] = probes[n] * (1.0 / (2.0 * DT))
    SK[...] = jnp.zeros_like(SK)

    def sketch(n, part):
        for xh in ((1, 2) if part == INNER else (0, 3)):
            lhs = jnp.concatenate([RATE[c, 2 * xh, pl.ds(0, 16, stride=2), :] for c in range(3)], axis=0)
            rows = slice(48 * xh, 48 * xh + 48)
            SK[rows, :] += jnp.dot(lhs, PE[n], precision=HIGH, preferred_element_type=F32)

    def stress(cur, part, halos):
        def body(i, packed):
            x = plane(part, i)
            packed = list(packed)
            for zb in range(4):
                z0 = zb * 8
                zs = slice(z0, z0 + 8)
                zu = slice(z0 + 8, z0 + 16)
                k = x * 4 + zb
                sx, sy, st = MET[0, x, zs, :], MET[1, x, zs, :], MET[2, x, zs, :]
                lam, mu = MET[3, x, zs, :], MET[4, x, zs, :]
                g = []
                for c in range(3):
                    f = U[cur, c, x + 2, zu, :]
                    dx = combine(U[cur, c, x, zu, :], U[cur, c, x + 1, zu, :],
                                 U[cur, c, x + 3, zu, :], U[cur, c, x + 4, zu, :])
                    dr = combine(*[U[cur, c, x + 2, z0 + o:z0 + o + 8, :] for o in (6, 7, 9, 10)])
                    dy = combine(*shifted(f, pltpu.roll(halos[c], 126 - 4 * k, 1), lane))
                    g.append((dx + sx * dr, dy + sy * dr, st * dr))
                pressure = lam * (g[0][0] + g[1][1] + g[2][2])
                mu2 = mu + mu
                sxy = mu * (g[0][1] + g[1][0])
                syy = pressure + mu2 * g[1][1]
                syz = mu * (g[1][2] + g[2][1])
                S[0, x + 2, zu, :] = pressure + mu2 * g[0][0]
                S[1, x + 2, zu, :] = sxy
                S[2, x + 2, zu, :] = mu * (g[0][2] + g[2][0])
                S[3, x + 2, zu, :] = syy
                S[4, x + 2, zu, :] = syz
                S[5, x + 2, zu, :] = pressure + mu2 * g[2][2]
                here = (lane >> 2) == k
                for i, s in enumerate((sxy, syy, syz)):
                    packed[i] = jnp.where(here, pltpu.roll(s, 4 * k + 2, 1), packed[i])
            return tuple(packed)

        return lax.fori_loop(0, 4, body, (zero8,) * 3)

    def forces(cur, part, halos):
        old = 1 - cur

        def body(i, packed):
            x = plane(part, i)
            packed = list(packed)
            for zb in range(4):
                z0 = zb * 8
                zs = slice(z0, z0 + 8)
                zu = slice(z0 + 8, z0 + 16)
                k = x * 4 + zb
                sx, sy, st, b = (MET[i, x, zs, :] for i in (0, 1, 2, 5))

                def d_x(i):
                    return combine(S[i, x, zu, :], S[i, x + 1, zu, :], S[i, x + 3, zu, :], S[i, x + 4, zu, :])

                def d_y(i, h):
                    f = S[i, x + 2, zu, :]
                    return combine(*shifted(f, pltpu.roll(h, 126 - 4 * k, 1), lane))

                dr = [combine(*[S[i, x + 2, z0 + o:z0 + o + 8, :] for o in (6, 7, 9, 10)]) for i in range(6)]
                acc = (
                    d_x(0) + sx * dr[0] + d_y(1, halos[0]) + sy * dr[1] + st * dr[2],
                    d_x(1) + sx * dr[1] + d_y(3, halos[1]) + sy * dr[3] + st * dr[4],
                    d_x(2) + sx * dr[2] + d_y(4, halos[2]) + sy * dr[4] + st * dr[5],
                )
                here = (lane >> 2) == k
                for c in range(3):
                    u = U[cur, c, x + 2, zu, :]
                    p = U[old, c, x + 2, zu, :]
                    fol = (u + u - p) + b * acc[c]
                    U[old, c, x + 2, zu, :] = fol
                    RATE[c, x, zs, :] = fol - p
                    packed[c] = jnp.where(here, pltpu.roll(fol, 4 * k + 2, 1), packed[c])
            return tuple(packed)

        return lax.fori_loop(0, 4, body, (zero8,) * 3)

    def step(n, carry):
        cur = lax.rem(n, 2)
        more = n < STEPS - 1
        packed = stress(cur, INNER, y_wait(PU, HU, 0, INNER))
        y_send(packed, PS, HS, 1, INNER)

        @pl.when(n > 0)
        def _():
            sketch(n - 1, EDGE)

        halos = y_wait(PU, HU, 0, EDGE)
        x_wait(u_planes(cur), 0)
        packed = stress(cur, EDGE, halos)
        x_start(s_planes, 1)
        y_send(packed, PS, HS, 1, EDGE)

        packed = forces(cur, INNER, y_wait(PS, HS, 1, INNER))

        @pl.when(more)
        def _():
            y_send(packed, PU, HU, 0, INNER)

        sketch(n, INNER)
        halos = y_wait(PS, HS, 1, EDGE)
        x_wait(s_planes, 1)
        packed_edge = forces(cur, EDGE, halos)

        @pl.when(more)
        def _():
            x_start(u_planes(1 - cur), 0)
            y_send(packed_edge, PU, HU, 0, EDGE)

        return carry

    lax.fori_loop(0, STEPS, step, 0)
    sketch(STEPS - 1, EDGE)
    for g in range(8):
        for xh in range(4):
            PIECES[g, 6 * xh:6 * xh + 6, :] = SK[xh * 48 + 6 * g:xh * 48 + 6 * g + 6, :]

    def piece(g, slot):
        return pltpu.make_async_remote_copy(
            src_ref=PIECES.at[g], dst_ref=RB.at[slot], send_sem=s0.at[g], recv_sem=r0.at[slot],
            device_id=(gx, g), device_id_type=MESH)

    @pl.loop(1, 8)
    def _(d):
        piece(lax.rem(gy + d, 8), gy).start()

    RB[gy] = PIECES[gy]

    final = STEPS % 2

    @pl.loop(0, 8)
    def _(x):
        for zb in range(4):
            for c in range(3):
                disp[c, pl.ds(zb * 64 + x, 8, stride=8), :] = U[final, c, x + 2, zb * 8 + 8:zb * 8 + 16, :]

    leave = pltpu.make_async_copy(disp, out, out_sem)
    leave.start()

    @pl.loop(1, 8)
    def _(d):
        g = lax.rem(gy + d, 8)
        piece(g, g).wait()

    total = RB[0]
    for g in range(1, 8):
        total = total + RB[g]
    tall[...] = total
    GL[...] = lax.dot_general(
        total, total, (((0,), (0,)), ((), ())), precision=HIGH, preferred_element_type=F32).reshape(16, 8, 128)

    def group(dev, me, src, dst, send, recv):
        def make(slot, peer):
            return pltpu.make_async_remote_copy(
                src_ref=src(peer), dst_ref=dst.at[slot], send_sem=send.at[peer], recv_sem=recv.at[slot],
                device_id=dev(peer), device_id_type=MESH)

        @pl.loop(1, 16)
        def _(d):
            make(me, lax.rem(me + d, 16)).start()

        def finish():
            @pl.loop(1, 16)
            def _(d):
                peer = lax.rem(me + d, 16)
                make(peer, peer).wait()

        return finish

    def summed(ref):
        parts = [ref[i] for i in range(16)]
        while len(parts) > 1:
            parts = [parts[i] + parts[i + 1] for i in range(0, len(parts), 2)]
        return parts[0]

    finish = group(a_dev, a_me, lambda p: GL.at[p], RA, s1, r1)
    RA[a_me] = GL[a_me]
    finish()
    part = summed(RA)
    PA[...] = part
    finish = group(b_dev, b_me, lambda p: PA, RBB, s2, r2)
    RBB[b_me] = part
    finish()
    whole = summed(RBB)
    GS[...] = whole
    finish = group(a_dev, a_me, lambda p: GS, gram, s3, r3)
    gram[a_me] = whole
    finish()
    leave.wait()


def wave(disp, vel, slopes, stretch, moduli, buoy, probes):
    sem = pltpu.SemaphoreType.DMA
    buffers = [
        (3, 256, 128), (3, 256, 128), (2, 256, 128), (256, 128), (2, 256, 128), (256, 128), (STEPS, 64, 128),
        (2, 3, 12, ZP, 128), (6, 12, ZP, 128), (6, 8, 32, 128), (3, 8, 32, 128), (STEPS, 128, 128), (192, 128),
        (2, 3, 8, 128), (2, 3, 8, 128), (2, 2, 3, 8, 128), (2, 2, 3, 8, 128),
        (8, 24, 128), (8, 24, 128), (16, 8, 128), (16, 8, 128), (8, 128), (16, 8, 128), (8, 128),
    ]
    sems = [(7,), (), (2, 2), (2, 2), (2, 2, 2), (2, 2, 2)] + [(8,)] * 2 + [(16,)] * 6
    return pl.pallas_call(
        wave_kernel,
        name="wave",
        out_shape=(
            jax.ShapeDtypeStruct((24, 128), F32),
            jax.ShapeDtypeStruct((16, 8, 128), F32),
            jax.ShapeDtypeStruct((3, 256, 128), F32),
        ),
        in_specs=[pl.BlockSpec(memory_space=pltpu.MemorySpace.HBM)] * 7,
        out_specs=[pl.BlockSpec(memory_space=VMEM)] * 2 + [pl.BlockSpec(memory_space=pltpu.MemorySpace.HBM)],
        scratch_shapes=[pltpu.VMEM(shape, F32) for shape in buffers] + [sem(shape) for shape in sems],
        compiler_params=pltpu.CompilerParams(
            collective_id=0, has_side_effects=True, vmem_limit_bytes=VMEM_LIMIT),
    )(disp, vel, slopes, stretch, moduli, buoy, probes)


def factor_kernel(scale, gram, tall, disp, basis, factor, out, sem):
    copy = pltpu.make_async_copy(disp, out, sem)
    copy.start()
    lane = lanes()
    sub = lax.broadcasted_iota(jnp.int32, (8, 128), 0)
    a = [gram[i] for i in range(16)]
    for j in range(128):
        b, s = divmod(j, 8)
        col = jnp.broadcast_to(a[b][:, j:j + 1], (8, 128))
        row = jnp.broadcast_to(a[b][s:s + 1, :], (8, 128))
        pivot = jnp.broadcast_to(col[s:s + 1, :], (8, 128))
        inv = 1.0 / pivot
        here = lane == j
        scaled = jnp.where(here, 1.0, row) * inv
        for i in range(b, 16):
            if i == b:
                if s == 7:
                    continue
                m = jnp.where(sub > s, col, 0.0)
                a[i] = jnp.where(here & (sub > s), 0.0, a[i]) - m * scaled
            else:
                m = jnp.broadcast_to(a[i][:, j:j + 1], (8, 128))
                a[i] = jnp.where(here, 0.0, a[i]) - m * scaled
    inverse = []
    for i in range(16):
        rows = sub + 8 * i
        diag = jnp.sum(jnp.where(lane == rows, a[i], 0.0), axis=1, keepdims=True)
        root = lax.rsqrt(diag)
        factor[8 * i:8 * i + 8, :] = jnp.where(lane >= rows, a[i], 0.0) * root
        inverse.append(jnp.where(lane == rows, 1.0, jnp.where(lane < rows, a[i], 0.0)) * (root * scale))
    inverse = jnp.concatenate(inverse, axis=0)
    q = lax.dot_general(
        tall[...], inverse, (((1,), (1,)), ((), ())), precision=HIGH, preferred_element_type=F32)
    for xh in range(4):
        for r in range(6):
            basis[r, xh:xh + 1, :] = q[6 * xh + r:6 * xh + r + 1, :]
    copy.wait()


def finish(gram, tall, disp, scale):
    return pl.pallas_call(
        functools.partial(factor_kernel, scale),
        name="factor",
        out_shape=(
            jax.ShapeDtypeStruct((6, 4, 128), F32),
            jax.ShapeDtypeStruct((128, 128), F32),
            jax.ShapeDtypeStruct((3, 256, 128), F32),
        ),
        in_specs=[pl.BlockSpec(memory_space=VMEM)] * 2 + [pl.BlockSpec(memory_space=pltpu.MemorySpace.HBM)],
        out_specs=[pl.BlockSpec(memory_space=VMEM)] * 2 + [pl.BlockSpec(memory_space=pltpu.MemorySpace.HBM)],
        scratch_shapes=[pltpu.SemaphoreType.DMA],
        compiler_params=pltpu.CompilerParams(vmem_limit_bytes=VMEM_LIMIT),
    )(gram, tall, disp)


def shards(displacement, velocity, slopes, stretch, moduli, buoyancy, probes):
    tall, gram, moved = wave(
        displacement.reshape(3, 256, 128), velocity.reshape(3, 256, 128), slopes.reshape(2, 256, 128),
        stretch.reshape(256, 128), moduli.reshape(2, 256, 128), buoyancy.reshape(256, 128), probes)
    rows = tall.shape[0] * lax.axis_size("gx") * lax.axis_size("gy")
    basis, factor, moved = finish(gram, tall, moved, math.sqrt(rows))
    return moved.reshape(3, 32, 8, 128), jnp.transpose(basis, (1, 0, 2)), factor


def solution(mesh):
    in_specs = (
        P(None, None, "gx", "gy"),
        P(None, None, "gx", "gy"),
        P(None, None, "gx", "gy"),
        P(None, "gx", "gy"),
        P(None, None, "gx", "gy"),
        P(None, "gx", "gy"),
        P(None, "gy", None),
    )
    out_specs = (P(None, None, "gx", "gy"), P("gx", "gy", None), P())
    return jax.shard_map(shards, mesh=mesh, in_specs=in_specs, out_specs=out_specs, check_vma=False)
```

```python
import functools
import math

import jax
import jax.numpy as jnp
from jax import lax
from jax.experimental import pallas as pl
from jax.experimental.pallas import tpu as pltpu
from jax.sharding import PartitionSpec as P

STEPS = 4
DT = 0.12
MESH = pl.DeviceIdType.MESH
HIGH = lax.Precision.HIGHEST
F32 = jnp.float32
BF16 = jnp.bfloat16
ZP = 48
VMEM = pltpu.MemorySpace.VMEM
VMEM_LIMIT = 63 * 1024 * 1024


def lanes():
    return lax.broadcasted_iota(jnp.int32, (8, 128), 1)


def shifted(f, h, lane):
    m2 = pltpu.roll(jnp.where(lane >= 126, h, f), 2, 1)
    m1 = pltpu.roll(jnp.where(lane >= 127, h, f), 1, 1)
    p1 = pltpu.roll(jnp.where(lane < 1, h, f), 127, 1)
    p2 = pltpu.roll(jnp.where(lane < 2, h, f), 126, 1)
    return m2, m1, p1, p2


def combine(m2, m1, p1, p2):
    return (m2 - p2) + 8.0 * (p1 - m1)


def split(x):
    hi = x.astype(BF16)
    rest = x - hi.astype(F32)
    mid = rest.astype(BF16)
    return hi, mid, (rest - mid.astype(F32)).astype(BF16)


def wave_kernel(
    disp_hbm, vel_hbm, slopes_hbm, stretch_hbm, moduli_hbm, buoy_hbm, probes_hbm,
    tall, gram, out,
    disp, vel, slopes, stretch, moduli, buoy, probes,
    PE, spread, U, S, MET, RATE, SK, PU, PS, HU, HS,
    PIECES, RB, GL, RA, PA, RBB, GS,
    load_sem, out_sem, send_x, recv_x, send_y, recv_y,
    s0, r0, s1, r1, s2, r2, s3, r3,
):
    gx, gy = lax.axis_index("gx"), lax.axis_index("gy")
    nx, ny = lax.axis_size("gx"), lax.axis_size("gy")
    left = (lax.rem(gx + nx - 1, nx), gy)
    right = (lax.rem(gx + 1, nx), gy)
    down = (gx, lax.rem(gy + ny - 1, ny))
    up = (gx, lax.rem(gy + 1, ny))
    has_left, has_right = gx > 0, gx < nx - 1
    core = lax.rem(gx, 2)
    pair = gx - core
    a_me = gy * 2 + core
    b_me = gx // 2

    def a_dev(a):
        return (pair + lax.rem(a, 2), a // 2)

    def b_dev(b):
        return (b * 2 + core, gy)

    loads = [
        pltpu.make_async_copy(src, dst, load_sem.at[i])
        for i, (src, dst) in enumerate((
            (disp_hbm, disp), (vel_hbm, vel), (slopes_hbm, slopes), (stretch_hbm, stretch),
            (moduli_hbm, moduli), (buoy_hbm, buoy), (probes_hbm, probes)))
    ]
    for copy in loads:
        copy.start()

    barrier = pltpu.get_barrier_semaphore()
    for peer in (left, right):
        pl.semaphore_signal(barrier, inc=1, device_id=peer, device_id_type=MESH)

    @pl.loop(1, 16)
    def _(d):
        pl.semaphore_signal(barrier, inc=1, device_id=a_dev(lax.rem(a_me + d, 16)), device_id_type=MESH)
        pl.semaphore_signal(barrier, inc=1, device_id=b_dev(lax.rem(b_me + d, 16)), device_id_type=MESH)

    lane = lanes()
    zero8 = jnp.zeros((8, 128), F32)
    low_part = (lane & 3) < 2

    @pl.loop(0, 12)
    def _(x):
        for s in range(2):
            for c in range(3):
                U[s, c, x, 0:8, :] = zero8
                U[s, c, x, 40:48, :] = zero8
        for c in range(6):
            S[c, x, 0:8, :] = zero8
            S[c, x, 40:48, :] = zero8

    def clear(x):
        for c in range(3):
            for z0 in range(8, 40, 8):
                U[0, c, x, z0:z0 + 8, :] = zero8
                U[1, c, x, z0:z0 + 8, :] = zero8
                S[c, x, z0:z0 + 8, :] = zero8

    @pl.when(gx == 0)
    def _():
        clear(0)
        clear(1)

    @pl.when(gx == nx - 1)
    def _():
        clear(10)
        clear(11)

    def x_copy(ref, kind, side):
        if side == 0:
            return pltpu.make_async_remote_copy(
                src_ref=ref(slice(2, 4)), dst_ref=ref(slice(10, 12)), send_sem=send_x.at[kind, 0],
                recv_sem=recv_x.at[kind, 0], device_id=left, device_id_type=MESH)
        return pltpu.make_async_remote_copy(
            src_ref=ref(slice(8, 10)), dst_ref=ref(slice(0, 2)), send_sem=send_x.at[kind, 1],
            recv_sem=recv_x.at[kind, 1], device_id=right, device_id_type=MESH)

    def x_start(ref, kind):
        @pl.when(has_left)
        def _():
            x_copy(ref, kind, 0).start()

        @pl.when(has_right)
        def _():
            x_copy(ref, kind, 1).start()

    def x_wait(ref, kind):
        @pl.when(has_right)
        def _():
            x_copy(ref, kind, 0).wait_recv()
            x_copy(ref, kind, 1).wait_send()

        @pl.when(has_left)
        def _():
            x_copy(ref, kind, 1).wait_recv()
            x_copy(ref, kind, 0).wait_send()

    def y_copies(packed, halo, kind, part):
        return [
            pltpu.make_async_remote_copy(
                src_ref=packed.at[part], dst_ref=halo.at[part, 1 - d], send_sem=send_y.at[kind, part, d],
                recv_sem=recv_y.at[kind, part, d], device_id=peer, device_id_type=MESH)
            for d, peer in enumerate((down, up))
        ]

    def y_send(values, packed, halo, kind, part):
        for c in range(3):
            packed[part, c] = values[c]
        for copy in y_copies(packed, halo, kind, part):
            copy.start()

    def y_wait(packed, halo, kind, part):
        for copy in y_copies(packed, halo, kind, part):
            copy.wait()
        result = []
        for c in range(3):
            lo = jnp.where(gy == 0, zero8, halo[part, 0, c])
            hi = jnp.where(gy == ny - 1, zero8, halo[part, 1, c])
            result.append(jnp.where(low_part, lo, hi))
        return result

    def u_planes(cur):
        return lambda xs: U.at[cur, :, xs, 8:40, :]

    def s_planes(xs):
        return S.at[0:3, xs, 8:40, :]

    INNER, EDGE = 0, 1

    def plane(part, i):
        return i + 2 if part == INNER else i + 4 * (i // 2)

    loads[0].wait()

    def load_u(part):
        def body(i, carry):
            x = plane(part, i)
            packed = list(carry)
            for zb in range(4):
                rows = pl.ds(zb * 64 + x, 8, stride=8)
                k = x * 4 + zb
                for c in range(3):
                    d = disp[c, rows, :]
                    U[0, c, x + 2, zb * 8 + 8:zb * 8 + 16, :] = d
                    packed[c] = jnp.where((lane >> 2) == k, pltpu.roll(d, 4 * k + 2, 1), packed[c])
            return tuple(packed)

        return lax.fori_loop(0, 4, body, (zero8,) * 3)

    first = [load_u(INNER), load_u(EDGE)]
    pl.semaphore_wait(barrier, 32)
    x_start(u_planes(0), 0)
    for part in (INNER, EDGE):
        y_send(first[part], PU, HU, 0, part)

    for copy in loads[1:]:
        copy.wait()

    @pl.loop(0, 8)
    def _(x):
        for zb in range(4):
            rows = pl.ds(zb * 64 + x, 8, stride=8)
            zs = slice(zb * 8, zb * 8 + 8)
            zu = slice(zb * 8 + 8, zb * 8 + 16)
            MET[0, x, zs, :] = slopes[0, rows, :]
            MET[1, x, zs, :] = slopes[1, rows, :]
            MET[2, x, zs, :] = stretch[rows, :]
            MET[3, x, zs, :] = moduli[0, rows, :] * (1.0 / 12.0)
            MET[4, x, zs, :] = moduli[1, rows, :] * (1.0 / 12.0)
            MET[5, x, zs, :] = buoy[rows, :] * (DT * DT / 12.0)
            for c in range(3):
                U[1, c, x + 2, zu, :] = U[0, c, x + 2, zu, :] - DT * vel[c, rows, :]

    spread[...] = jnp.zeros((128, 128), F32)
    for n in range(STEPS):
        spread[pl.ds(0, 64, stride=2), :] = probes[n] * (1.0 / (2.0 * DT))
        hi, mid, lo = split(spread[...])
        for i, term in enumerate((hi, mid, hi, lo, mid, hi)):
            PE[n, 128 * i:128 * i + 128, :] = term
    SK[...] = jnp.zeros_like(SK)

    def sketch(n, part):
        where = (1, 2) if part == INNER else (0, 3)
        hi, mid, lo = split(jnp.concatenate(
            [RATE[c, 2 * xh, pl.ds(0, 16, stride=2), :] for xh in where for c in range(3)], axis=0))
        term = jnp.dot(
            jnp.concatenate([hi, hi, mid, hi, mid, lo], axis=1), PE[n], preferred_element_type=F32)
        for i, xh in enumerate(where):
            SK[48 * xh:48 * xh + 48, :] += term[48 * i:48 * i + 48, :]

    def over_planes(part, planes, cell, put):
        def body(i, packed):
            cells = [(plane(part, i * planes + j), zb) for j in range(planes) for zb in range(4)]
            values = [cell(x, zb) for x, zb in cells]
            packed = list(packed)
            for (x, zb), value in zip(cells, values):
                edge = put(x, zb, value)
                k = x * 4 + zb
                here = (lane >> 2) == k
                for c in range(3):
                    packed[c] = jnp.where(here, pltpu.roll(edge[c], 4 * k + 2, 1), packed[c])
            return tuple(packed)

        if planes == 4:
            return body(0, (zero8,) * 3)
        return lax.fori_loop(0, 4 // planes, body, (zero8,) * 3)

    def stress(cur, part, halos):
        def cell(x, zb):
            z0 = zb * 8
            zs, zu = slice(z0, z0 + 8), slice(z0 + 8, z0 + 16)
            k = x * 4 + zb
            sx, sy, st = MET[0, x, zs, :], MET[1, x, zs, :], MET[2, x, zs, :]
            lam, mu = MET[3, x, zs, :], MET[4, x, zs, :]
            g = []
            for c in range(3):
                f = U[cur, c, x + 2, zu, :]
                dx = combine(U[cur, c, x, zu, :], U[cur, c, x + 1, zu, :],
                             U[cur, c, x + 3, zu, :], U[cur, c, x + 4, zu, :])
                dr = combine(*[U[cur, c, x + 2, z0 + o:z0 + o + 8, :] for o in (6, 7, 9, 10)])
                dy = combine(*shifted(f, pltpu.roll(halos[c], 126 - 4 * k, 1), lane))
                g.append((dx + sx * dr, dy + sy * dr, st * dr))
            pressure = lam * (g[0][0] + g[1][1] + g[2][2])
            mu2 = mu + mu
            return (pressure + mu2 * g[0][0], mu * (g[0][1] + g[1][0]), mu * (g[0][2] + g[2][0]),
                    pressure + mu2 * g[1][1], mu * (g[1][2] + g[2][1]), pressure + mu2 * g[2][2])

        def put(x, zb, value):
            for j in range(6):
                S[j, x + 2, zb * 8 + 8:zb * 8 + 16, :] = value[j]
            return value[1], value[3], value[4]

        return over_planes(part, 2, cell, put)

    def forces(cur, part, halos):
        old = 1 - cur

        def cell(x, zb):
            z0 = zb * 8
            zs, zu = slice(z0, z0 + 8), slice(z0 + 8, z0 + 16)
            k = x * 4 + zb
            sx, sy, st, b = (MET[j, x, zs, :] for j in (0, 1, 2, 5))

            def d_x(j):
                return combine(S[j, x, zu, :], S[j, x + 1, zu, :], S[j, x + 3, zu, :], S[j, x + 4, zu, :])

            def d_y(j, h):
                return combine(*shifted(S[j, x + 2, zu, :], pltpu.roll(h, 126 - 4 * k, 1), lane))

            dr = [combine(*[S[j, x + 2, z0 + o:z0 + o + 8, :] for o in (6, 7, 9, 10)]) for j in range(6)]
            acc = (
                d_x(0) + sx * dr[0] + d_y(1, halos[0]) + sy * dr[1] + st * dr[2],
                d_x(1) + sx * dr[1] + d_y(3, halos[1]) + sy * dr[3] + st * dr[4],
                d_x(2) + sx * dr[2] + d_y(4, halos[2]) + sy * dr[4] + st * dr[5],
            )
            moved = []
            for c in range(3):
                u, p = U[cur, c, x + 2, zu, :], U[old, c, x + 2, zu, :]
                fol = (u + u - p) + b * acc[c]
                moved.append((fol, fol - p))
            return moved

        def put(x, zb, value):
            z0 = zb * 8
            for c in range(3):
                U[old, c, x + 2, z0 + 8:z0 + 16, :] = value[c][0]
                RATE[c, x, z0:z0 + 8, :] = value[c][1]
            return [v[0] for v in value]

        return over_planes(part, 2, cell, put)

    def step(n, carry):
        cur = lax.rem(n, 2)
        more = n < STEPS - 1
        packed = stress(cur, INNER, y_wait(PU, HU, 0, INNER))
        y_send(packed, PS, HS, 1, INNER)

        @pl.when(n > 0)
        def _():
            sketch(n - 1, EDGE)

        halos = y_wait(PU, HU, 0, EDGE)
        x_wait(u_planes(cur), 0)
        packed = stress(cur, EDGE, halos)
        x_start(s_planes, 1)
        y_send(packed, PS, HS, 1, EDGE)

        packed = forces(cur, INNER, y_wait(PS, HS, 1, INNER))

        @pl.when(more)
        def _():
            y_send(packed, PU, HU, 0, INNER)

        sketch(n, INNER)
        halos = y_wait(PS, HS, 1, EDGE)
        x_wait(s_planes, 1)
        packed_edge = forces(cur, EDGE, halos)

        @pl.when(more)
        def _():
            x_start(u_planes(1 - cur), 0)
            y_send(packed_edge, PU, HU, 0, EDGE)

        return carry

    lax.fori_loop(0, STEPS, step, 0)
    sketch(STEPS - 1, EDGE)
    for g in range(8):
        for xh in range(4):
            PIECES[g, 6 * xh:6 * xh + 6, :] = SK[xh * 48 + 6 * g:xh * 48 + 6 * g + 6, :]

    def piece(g, slot):
        return pltpu.make_async_remote_copy(
            src_ref=PIECES.at[g], dst_ref=RB.at[slot], send_sem=s0.at[g], recv_sem=r0.at[slot],
            device_id=(gx, g), device_id_type=MESH)

    @pl.loop(1, 8)
    def _(d):
        piece(lax.rem(gy + d, 8), gy).start()

    RB[gy] = PIECES[gy]

    final = STEPS % 2

    @pl.loop(0, 8)
    def _(x):
        for zb in range(4):
            for c in range(3):
                disp[c, pl.ds(zb * 64 + x, 8, stride=8), :] = U[final, c, x + 2, zb * 8 + 8:zb * 8 + 16, :]

    leave = pltpu.make_async_copy(disp, out, out_sem)
    leave.start()

    @pl.loop(1, 8)
    def _(d):
        g = lax.rem(gy + d, 8)
        piece(g, g).wait()

    total = RB[0]
    for g in range(1, 8):
        total = total + RB[g]
    tall[...] = total
    GL[...] = lax.dot_general(
        total, total, (((0,), (0,)), ((), ())), precision=HIGH, preferred_element_type=F32).reshape(16, 8, 128)

    def group(dev, me, src, dst, send, recv):
        def make(slot, peer):
            return pltpu.make_async_remote_copy(
                src_ref=src(peer), dst_ref=dst.at[slot], send_sem=send.at[peer], recv_sem=recv.at[slot],
                device_id=dev(peer), device_id_type=MESH)

        @pl.loop(1, 16)
        def _(d):
            make(me, lax.rem(me + d, 16)).start()

        def finish():
            @pl.loop(1, 16)
            def _(d):
                peer = lax.rem(me + d, 16)
                make(peer, peer).wait()

        return finish

    def summed(ref):
        parts = [ref[i] for i in range(16)]
        while len(parts) > 1:
            parts = [parts[i] + parts[i + 1] for i in range(0, len(parts), 2)]
        return parts[0]

    finish = group(a_dev, a_me, lambda p: GL.at[p], RA, s1, r1)
    RA[a_me] = GL[a_me]
    finish()
    part = summed(RA)
    PA[...] = part
    finish = group(b_dev, b_me, lambda p: PA, RBB, s2, r2)
    RBB[b_me] = part
    finish()
    whole = summed(RBB)
    GS[...] = whole
    finish = group(a_dev, a_me, lambda p: GS, gram, s3, r3)
    gram[a_me] = whole
    finish()
    leave.wait()


def wave(disp, vel, slopes, stretch, moduli, buoy, probes):
    sem = pltpu.SemaphoreType.DMA
    buffers = [
        (3, 256, 128), (3, 256, 128), (2, 256, 128), (256, 128), (2, 256, 128), (256, 128), (STEPS, 64, 128),
        (128, 128), (2, 3, 12, ZP, 128), (6, 12, ZP, 128), (6, 8, 32, 128), (3, 8, 32, 128), (192, 128),
        (2, 3, 8, 128), (2, 3, 8, 128), (2, 2, 3, 8, 128), (2, 2, 3, 8, 128),
        (8, 24, 128), (8, 24, 128), (16, 8, 128), (16, 8, 128), (8, 128), (16, 8, 128), (8, 128),
    ]
    sems = [(7,), (), (2, 2), (2, 2), (2, 2, 2), (2, 2, 2)] + [(8,)] * 2 + [(16,)] * 6
    return pl.pallas_call(
        wave_kernel,
        name="wave",
        out_shape=(
            jax.ShapeDtypeStruct((24, 128), F32),
            jax.ShapeDtypeStruct((16, 8, 128), F32),
            jax.ShapeDtypeStruct((3, 256, 128), F32),
        ),
        in_specs=[pl.BlockSpec(memory_space=pltpu.MemorySpace.HBM)] * 7,
        out_specs=[pl.BlockSpec(memory_space=VMEM)] * 2 + [pl.BlockSpec(memory_space=pltpu.MemorySpace.HBM)],
        scratch_shapes=[pltpu.VMEM(shape, F32) for shape in buffers[:7]]
        + [pltpu.VMEM((STEPS, 768, 128), BF16)]
        + [pltpu.VMEM(shape, F32) for shape in buffers[7:]] + [sem(shape) for shape in sems],
        compiler_params=pltpu.CompilerParams(
            collective_id=0, has_side_effects=True, vmem_limit_bytes=VMEM_LIMIT),
    )(disp, vel, slopes, stretch, moduli, buoy, probes)


def factor_kernel(scale, gram, tall, disp, basis, factor, out, stage, sem):
    enter = pltpu.make_async_copy(disp, stage, sem.at[0])
    leave = pltpu.make_async_copy(stage, out, sem.at[1])
    enter.start()
    lane = lanes()
    sub = lax.broadcasted_iota(jnp.int32, (8, 128), 0)
    a = [gram[i] for i in range(16)]
    for b in range(16):
        if b == 4:
            enter.wait()
            leave.start()
        j0 = 8 * b
        inside = (lane >= j0) & (lane < j0 + 8)
        cols = [jnp.broadcast_to(a[b][:, j0 + t:j0 + t + 1], (8, 128)) for t in range(8)]
        d = [[jnp.broadcast_to(cols[t][s:s + 1, :], (8, 128)) if t >= s else None for t in range(8)]
             for s in range(8)]
        inv = [None] * 8
        m = [[None] * 8 for _ in range(8)]
        for s in range(8):
            inv[s] = 1.0 / d[s][s]
            for t in range(s + 1, 8):
                m[s][t] = d[s][t] * inv[s]
                for q in range(t, 8):
                    d[t][q] = d[t][q] - m[s][t] * d[s][q]
        unit = [None] * 8
        fresh = a[b]
        for t in range(8):
            x = jnp.broadcast_to(a[b][t:t + 1, :], (8, 128))
            for s in range(t):
                x = jnp.where(lane == j0 + s, 0.0, x) - m[s][t] * unit[s]
            unit[t] = jnp.where(lane == j0 + t, 1.0, x)
            fresh = jnp.where(sub == t, x, fresh)
        a[b] = fresh
        below = [jnp.where((lane > j0 + t) & inside, 0.0, unit[t]) for t in range(8)]
        for i in range(b + 1, 16):
            c = [jnp.broadcast_to(a[i][:, j0 + s:j0 + s + 1], (8, 128)) for s in range(8)]
            x = jnp.where(inside, 0.0, a[i])
            for s in range(8):
                ms = c[s] * inv[s]
                for t in range(s + 1, 8):
                    c[t] = c[t] - ms * d[s][t]
                x = x - ms * below[s]
            a[i] = x
    inverse = []
    for i in range(16):
        rows = sub + 8 * i
        diag = jnp.sum(jnp.where(lane == rows, a[i], 0.0), axis=1, keepdims=True)
        root = lax.rsqrt(diag)
        factor[8 * i:8 * i + 8, :] = jnp.where(lane >= rows, a[i], 0.0) * root
        inverse.append(jnp.where(lane == rows, 1.0, jnp.where(lane < rows, a[i], 0.0)) * (root * scale))
    inverse = jnp.concatenate(inverse, axis=0)
    q = lax.dot_general(
        tall[...], inverse, (((1,), (1,)), ((), ())), precision=HIGH, preferred_element_type=F32)
    for xh in range(4):
        for r in range(6):
            basis[r, xh:xh + 1, :] = q[6 * xh + r:6 * xh + r + 1, :]
    leave.wait()


def finish(gram, tall, disp, scale):
    return pl.pallas_call(
        functools.partial(factor_kernel, scale),
        name="factor",
        out_shape=(
            jax.ShapeDtypeStruct((6, 4, 128), F32),
            jax.ShapeDtypeStruct((128, 128), F32),
            jax.ShapeDtypeStruct((3, 256, 128), F32),
        ),
        in_specs=[pl.BlockSpec(memory_space=VMEM)] * 2 + [pl.BlockSpec(memory_space=pltpu.MemorySpace.HBM)],
        out_specs=[pl.BlockSpec(memory_space=VMEM)] * 2 + [pl.BlockSpec(memory_space=pltpu.MemorySpace.HBM)],
        scratch_shapes=[pltpu.VMEM((3, 256, 128), F32), pltpu.SemaphoreType.DMA((2,))],
        compiler_params=pltpu.CompilerParams(vmem_limit_bytes=VMEM_LIMIT),
    )(gram, tall, disp)


def shards(displacement, velocity, slopes, stretch, moduli, buoyancy, probes):
    tall, gram, moved = wave(
        displacement.reshape(3, 256, 128), velocity.reshape(3, 256, 128), slopes.reshape(2, 256, 128),
        stretch.reshape(256, 128), moduli.reshape(2, 256, 128), buoyancy.reshape(256, 128), probes)
    rows = tall.shape[0] * lax.axis_size("gx") * lax.axis_size("gy")
    basis, factor, moved = finish(gram, tall, moved, math.sqrt(rows))
    return moved.reshape(3, 32, 8, 128), jnp.transpose(basis, (1, 0, 2)), factor


def solution(mesh):
    in_specs = (
        P(None, None, "gx", "gy"),
        P(None, None, "gx", "gy"),
        P(None, None, "gx", "gy"),
        P(None, "gx", "gy"),
        P(None, None, "gx", "gy"),
        P(None, "gx", "gy"),
        P(None, "gy", None),
    )
    out_specs = (P(None, None, "gx", "gy"), P("gx", "gy", None), P())
    return jax.shard_map(shards, mesh=mesh, in_specs=in_specs, out_specs=out_specs, check_vma=False)
```

```python
import functools
import math

import jax
import jax.numpy as jnp
from jax import lax
from jax.experimental import pallas as pl
from jax.experimental.pallas import tpu as pltpu
from jax.sharding import PartitionSpec as P

STEPS = 4
DT = 0.12
MESH = pl.DeviceIdType.MESH
HIGH = lax.Precision.HIGHEST
F32 = jnp.float32
BF16 = jnp.bfloat16
ZP = 48
VMEM = pltpu.MemorySpace.VMEM
VMEM_LIMIT = 63 * 1024 * 1024


def lanes():
    return lax.broadcasted_iota(jnp.int32, (8, 128), 1)


def shifted(f, h, lane):
    m2 = pltpu.roll(jnp.where(lane >= 126, h, f), 2, 1)
    m1 = pltpu.roll(jnp.where(lane >= 127, h, f), 1, 1)
    p1 = pltpu.roll(jnp.where(lane < 1, h, f), 127, 1)
    p2 = pltpu.roll(jnp.where(lane < 2, h, f), 126, 1)
    return m2, m1, p1, p2


def combine(m2, m1, p1, p2):
    return (m2 - p2) + 8.0 * (p1 - m1)


def split(x):
    hi = x.astype(BF16)
    rest = x - hi.astype(F32)
    mid = rest.astype(BF16)
    return hi, mid, (rest - mid.astype(F32)).astype(BF16)


def wave_kernel(
    disp_hbm, vel_hbm, slopes_hbm, stretch_hbm, moduli_hbm, buoy_hbm, probes_hbm,
    tall, gram, out,
    disp, vel, slopes, stretch, moduli, buoy, probes,
    PE, spread, U, S, MET, RATE, SK, PU, PS, HU, HS,
    PIECES, RB, GL, RA, PA, RBB, GS,
    load_sem, out_sem, send_x, recv_x, send_y, recv_y,
    s0, r0, s1, r1, s2, r2, s3, r3,
):
    gx, gy = lax.axis_index("gx"), lax.axis_index("gy")
    nx, ny = lax.axis_size("gx"), lax.axis_size("gy")
    left = (lax.rem(gx + nx - 1, nx), gy)
    right = (lax.rem(gx + 1, nx), gy)
    down = (gx, lax.rem(gy + ny - 1, ny))
    up = (gx, lax.rem(gy + 1, ny))
    core = lax.rem(gx, 2)
    has_off = (gx > 0) & (gx < nx - 1)
    pair = gx - core
    a_me = gy * 2 + core
    b_me = gx // 2

    def a_dev(a):
        return (pair + lax.rem(a, 2), a // 2)

    def b_dev(b):
        return (b * 2 + core, gy)

    loads = [
        pltpu.make_async_copy(src, dst, load_sem.at[i])
        for i, (src, dst) in enumerate((
            (disp_hbm, disp), (vel_hbm, vel), (slopes_hbm, slopes), (stretch_hbm, stretch),
            (moduli_hbm, moduli), (buoy_hbm, buoy), (probes_hbm, probes)))
    ]
    for copy in loads:
        copy.start()

    barrier = pltpu.get_barrier_semaphore()
    for peer in (left, right):
        pl.semaphore_signal(barrier, inc=1, device_id=peer, device_id_type=MESH)

    @pl.loop(1, 16)
    def _(d):
        pl.semaphore_signal(barrier, inc=1, device_id=a_dev(lax.rem(a_me + d, 16)), device_id_type=MESH)
        pl.semaphore_signal(barrier, inc=1, device_id=b_dev(lax.rem(b_me + d, 16)), device_id_type=MESH)

    lane = lanes()
    zero8 = jnp.zeros((8, 128), F32)
    low_part = (lane & 3) < 2

    @pl.loop(0, 12)
    def _(x):
        for s in range(2):
            for c in range(3):
                U[s, c, x, 0:8, :] = zero8
                U[s, c, x, 40:48, :] = zero8
        for c in range(6):
            S[c, x, 0:8, :] = zero8
            S[c, x, 40:48, :] = zero8

    def clear(x):
        for c in range(3):
            for z0 in range(8, 40, 8):
                U[0, c, x, z0:z0 + 8, :] = zero8
                U[1, c, x, z0:z0 + 8, :] = zero8
                S[c, x, z0:z0 + 8, :] = zero8

    @pl.when(gx == 0)
    def _():
        clear(0)
        clear(1)

    @pl.when(gx == nx - 1)
    def _():
        clear(10)
        clear(11)

    INNER, ON, OFF = 0, 1, 2

    def side(part):
        return core if part == OFF else 1 - core

    def x_copy(ref, kind, part):
        s = side(part)
        return pltpu.make_async_remote_copy(
            src_ref=ref(pl.ds(2 + 6 * s, 2)), dst_ref=ref(pl.ds(10 - 10 * s, 2)), send_sem=send_x.at[kind, part - 1],
            recv_sem=recv_x.at[kind, part - 1], device_id=(gx - 1 + 2 * s, gy), device_id_type=MESH)

    def x_start(ref, kind, part):
        if part == ON:
            x_copy(ref, kind, part).start()
        else:
            @pl.when(has_off)
            def _():
                x_copy(ref, kind, part).start()

    def x_wait(ref, kind, part):
        if part == ON:
            x_copy(ref, kind, part).wait()
        else:
            @pl.when(has_off)
            def _():
                x_copy(ref, kind, part).wait()

    def y_copies(packed, halo, kind, part):
        return [
            pltpu.make_async_remote_copy(
                src_ref=packed.at[part], dst_ref=halo.at[part, 1 - d], send_sem=send_y.at[kind, part, d],
                recv_sem=recv_y.at[kind, part, d], device_id=peer, device_id_type=MESH)
            for d, peer in enumerate((down, up))
        ]

    def y_send(values, packed, halo, kind, part):
        for c in range(3):
            packed[part, c] = values[c]
        for copy in y_copies(packed, halo, kind, part):
            copy.start()

    def y_wait(packed, halo, kind, part):
        for copy in y_copies(packed, halo, kind, part):
            copy.wait()
        result = []
        for c in range(3):
            lo = jnp.where(gy == 0, zero8, halo[part, 0, c])
            hi = jnp.where(gy == ny - 1, zero8, halo[part, 1, c])
            result.append(jnp.where(low_part, lo, hi))
        return result

    def u_planes(cur):
        return lambda xs: U.at[cur, :, xs, 8:40, :]

    def s_planes(xs):
        return S.at[0:3, xs, 8:40, :]

    def plane(part, i):
        return i + 2 if part == INNER else i + 6 * side(part)

    loads[0].wait()

    def load_u(part):
        def body(i, carry):
            x = plane(part, i)
            packed = list(carry)
            for zb in range(4):
                rows = pl.ds(zb * 64 + x, 8, stride=8)
                k = x * 4 + zb
                for c in range(3):
                    d = disp[c, rows, :]
                    U[0, c, x + 2, zb * 8 + 8:zb * 8 + 16, :] = d
                    packed[c] = jnp.where((lane >> 2) == k, pltpu.roll(d, 4 * k + 2, 1), packed[c])
            return tuple(packed)

        return lax.fori_loop(0, 4 if part == INNER else 2, body, (zero8,) * 3)

    first = [load_u(INNER), load_u(ON), load_u(OFF)]
    pl.semaphore_wait(barrier, 32)
    for part in (OFF, ON):
        x_start(u_planes(0), 0, part)
    for part in (INNER, OFF, ON):
        y_send(first[part], PU, HU, 0, part)

    for copy in loads[1:]:
        copy.wait()

    @pl.loop(0, 8)
    def _(x):
        for zb in range(4):
            rows = pl.ds(zb * 64 + x, 8, stride=8)
            zs = slice(zb * 8, zb * 8 + 8)
            zu = slice(zb * 8 + 8, zb * 8 + 16)
            MET[0, x, zs, :] = slopes[0, rows, :]
            MET[1, x, zs, :] = slopes[1, rows, :]
            MET[2, x, zs, :] = stretch[rows, :]
            MET[3, x, zs, :] = moduli[0, rows, :] * (1.0 / 12.0)
            MET[4, x, zs, :] = moduli[1, rows, :] * (1.0 / 12.0)
            MET[5, x, zs, :] = buoy[rows, :] * (DT * DT / 12.0)
            for c in range(3):
                U[1, c, x + 2, zu, :] = U[0, c, x + 2, zu, :] - DT * vel[c, rows, :]

    spread[...] = jnp.zeros((128, 128), F32)
    for n in range(STEPS):
        spread[pl.ds(0, 64, stride=2), :] = probes[n] * (1.0 / (2.0 * DT))
        hi, mid, lo = split(spread[...])
        for i, term in enumerate((hi, mid, hi, lo, mid, hi)):
            PE[n, 128 * i:128 * i + 128, :] = term
    SK[...] = jnp.zeros_like(SK)

    def sketch(n, outer):
        where = (0, 3) if outer else (1, 2)
        hi, mid, lo = split(jnp.concatenate(
            [RATE[c, 2 * xh, pl.ds(0, 16, stride=2), :] for xh in where for c in range(3)], axis=0))
        term = jnp.dot(
            jnp.concatenate([hi, hi, mid, hi, mid, lo], axis=1), PE[n], preferred_element_type=F32)
        for i, xh in enumerate(where):
            SK[48 * xh:48 * xh + 48, :] += term[48 * i:48 * i + 48, :]

    def over_planes(part, planes, cell, put):
        def body(i, packed):
            cells = [(plane(part, i * planes + j), zb) for j in range(planes) for zb in range(4)]
            values = [cell(x, zb) for x, zb in cells]
            packed = list(packed)
            for (x, zb), value in zip(cells, values):
                edge = put(x, zb, value)
                k = x * 4 + zb
                here = (lane >> 2) == k
                for c in range(3):
                    packed[c] = jnp.where(here, pltpu.roll(edge[c], 4 * k + 2, 1), packed[c])
            return tuple(packed)

        if part != INNER:
            return body(0, (zero8,) * 3)
        return lax.fori_loop(0, 4 // planes, body, (zero8,) * 3)

    def stress(cur, part, halos):
        def cell(x, zb):
            z0 = zb * 8
            zs, zu = slice(z0, z0 + 8), slice(z0 + 8, z0 + 16)
            k = x * 4 + zb
            sx, sy, st = MET[0, x, zs, :], MET[1, x, zs, :], MET[2, x, zs, :]
            lam, mu = MET[3, x, zs, :], MET[4, x, zs, :]
            g = []
            for c in range(3):
                f = U[cur, c, x + 2, zu, :]
                dx = combine(U[cur, c, x, zu, :], U[cur, c, x + 1, zu, :],
                             U[cur, c, x + 3, zu, :], U[cur, c, x + 4, zu, :])
                dr = combine(*[U[cur, c, x + 2, z0 + o:z0 + o + 8, :] for o in (6, 7, 9, 10)])
                dy = combine(*shifted(f, pltpu.roll(halos[c], 126 - 4 * k, 1), lane))
                g.append((dx + sx * dr, dy + sy * dr, st * dr))
            pressure = lam * (g[0][0] + g[1][1] + g[2][2])
            mu2 = mu + mu
            return (pressure + mu2 * g[0][0], mu * (g[0][1] + g[1][0]), mu * (g[0][2] + g[2][0]),
                    pressure + mu2 * g[1][1], mu * (g[1][2] + g[2][1]), pressure + mu2 * g[2][2])

        def put(x, zb, value):
            for j in range(6):
                S[j, x + 2, zb * 8 + 8:zb * 8 + 16, :] = value[j]
            return value[1], value[3], value[4]

        return over_planes(part, 2, cell, put)

    def forces(cur, part, halos):
        old = 1 - cur

        def cell(x, zb):
            z0 = zb * 8
            zs, zu = slice(z0, z0 + 8), slice(z0 + 8, z0 + 16)
            k = x * 4 + zb
            sx, sy, st, b = (MET[j, x, zs, :] for j in (0, 1, 2, 5))

            def d_x(j):
                return combine(S[j, x, zu, :], S[j, x + 1, zu, :], S[j, x + 3, zu, :], S[j, x + 4, zu, :])

            def d_y(j, h):
                return combine(*shifted(S[j, x + 2, zu, :], pltpu.roll(h, 126 - 4 * k, 1), lane))

            dr = [combine(*[S[j, x + 2, z0 + o:z0 + o + 8, :] for o in (6, 7, 9, 10)]) for j in range(6)]
            acc = (
                d_x(0) + sx * dr[0] + d_y(1, halos[0]) + sy * dr[1] + st * dr[2],
                d_x(1) + sx * dr[1] + d_y(3, halos[1]) + sy * dr[3] + st * dr[4],
                d_x(2) + sx * dr[2] + d_y(4, halos[2]) + sy * dr[4] + st * dr[5],
            )
            moved = []
            for c in range(3):
                u, p = U[cur, c, x + 2, zu, :], U[old, c, x + 2, zu, :]
                fol = (u + u - p) + b * acc[c]
                moved.append((fol, fol - p))
            return moved

        def put(x, zb, value):
            z0 = zb * 8
            for c in range(3):
                U[old, c, x + 2, z0 + 8:z0 + 16, :] = value[c][0]
                RATE[c, x, z0:z0 + 8, :] = value[c][1]
            return [v[0] for v in value]

        return over_planes(part, 2, cell, put)

    def step(n, carry):
        cur = lax.rem(n, 2)
        more = n < STEPS - 1
        packed = stress(cur, INNER, y_wait(PU, HU, 0, INNER))
        y_send(packed, PS, HS, 1, INNER)

        @pl.when(n > 0)
        def _():
            sketch(n - 1, True)

        for part in (ON, OFF):
            halos = y_wait(PU, HU, 0, part)
            x_wait(u_planes(cur), 0, part)
            packed = stress(cur, part, halos)
            x_start(s_planes, 1, part)
            y_send(packed, PS, HS, 1, part)

        packed = forces(cur, INNER, y_wait(PS, HS, 1, INNER))

        @pl.when(more)
        def _():
            y_send(packed, PU, HU, 0, INNER)

        sketch(n, False)
        for part in (ON, OFF):
            halos = y_wait(PS, HS, 1, part)
            x_wait(s_planes, 1, part)
            packed = forces(cur, part, halos)

            @pl.when(more)
            def _():
                x_start(u_planes(1 - cur), 0, part)
                y_send(packed, PU, HU, 0, part)

        return carry

    lax.fori_loop(0, STEPS, step, 0)
    sketch(STEPS - 1, True)
    for g in range(8):
        for xh in range(4):
            PIECES[g, 6 * xh:6 * xh + 6, :] = SK[xh * 48 + 6 * g:xh * 48 + 6 * g + 6, :]

    def far_first(i, half):
        step = (i + 1) // 2
        return half + step * (2 * lax.rem(i, 2) - 1)

    def piece(g, slot):
        return pltpu.make_async_remote_copy(
            src_ref=PIECES.at[g], dst_ref=RB.at[slot], send_sem=s0.at[g], recv_sem=r0.at[slot],
            device_id=(gx, g), device_id_type=MESH)

    @pl.loop(0, 7)
    def _(i):
        piece(lax.rem(gy + far_first(i, 4), 8), gy).start()

    RB[gy] = PIECES[gy]

    final = STEPS % 2

    @pl.loop(0, 8)
    def _(x):
        for zb in range(4):
            for c in range(3):
                disp[c, pl.ds(zb * 64 + x, 8, stride=8), :] = U[final, c, x + 2, zb * 8 + 8:zb * 8 + 16, :]

    leave = pltpu.make_async_copy(disp, out, out_sem)
    leave.start()

    @pl.loop(1, 8)
    def _(d):
        g = lax.rem(gy + d, 8)
        piece(g, g).wait()

    total = RB[0]
    for g in range(1, 8):
        total = total + RB[g]
    tall[...] = total
    hi, mid, lo = (term.astype(F32) for term in split(total))
    GL[...] = lax.dot_general(
        jnp.concatenate([hi, hi, mid, hi, mid, lo], axis=0).astype(BF16),
        jnp.concatenate([hi, mid, hi, lo, mid, hi], axis=0).astype(BF16),
        (((0,), (0,)), ((), ())), preferred_element_type=F32).reshape(16, 8, 128)

    def group(dev, me, src, dst, send, recv):
        def make(slot, peer):
            return pltpu.make_async_remote_copy(
                src_ref=src(peer), dst_ref=dst.at[slot], send_sem=send.at[peer], recv_sem=recv.at[slot],
                device_id=dev(peer), device_id_type=MESH)

        @pl.loop(0, 15)
        def _(i):
            make(me, lax.rem(me + far_first(i, 8), 16)).start()

        def finish():
            @pl.loop(1, 16)
            def _(d):
                peer = lax.rem(me + d, 16)
                make(peer, peer).wait()

        return finish

    def summed(ref):
        parts = [ref[i] for i in range(16)]
        while len(parts) > 1:
            parts = [parts[i] + parts[i + 1] for i in range(0, len(parts), 2)]
        return parts[0]

    finish = group(b_dev, b_me, lambda p: GL.at[p], RA, s1, r1)
    RA[b_me] = GL[b_me]
    finish()
    part = summed(RA)
    PA[...] = part
    finish = group(a_dev, a_me, lambda p: PA, RBB, s2, r2)
    RBB[a_me] = part
    finish()
    whole = summed(RBB)
    GS[...] = whole
    finish = group(b_dev, b_me, lambda p: GS, gram, s3, r3)
    gram[b_me] = whole
    finish()
    leave.wait()


def wave(disp, vel, slopes, stretch, moduli, buoy, probes):
    sem = pltpu.SemaphoreType.DMA
    buffers = [
        (3, 256, 128), (3, 256, 128), (2, 256, 128), (256, 128), (2, 256, 128), (256, 128), (STEPS, 64, 128),
        (128, 128), (2, 3, 12, ZP, 128), (6, 12, ZP, 128), (6, 8, 32, 128), (3, 8, 32, 128), (192, 128),
        (3, 3, 8, 128), (3, 3, 8, 128), (3, 2, 3, 8, 128), (3, 2, 3, 8, 128),
        (8, 24, 128), (8, 24, 128), (16, 8, 128), (16, 8, 128), (8, 128), (16, 8, 128), (8, 128),
    ]
    sems = [(7,), (), (2, 2), (2, 2), (2, 3, 2), (2, 3, 2)] + [(8,)] * 2 + [(16,)] * 6
    return pl.pallas_call(
        wave_kernel,
        name="wave",
        out_shape=(
            jax.ShapeDtypeStruct((24, 128), F32),
            jax.ShapeDtypeStruct((16, 8, 128), F32),
            jax.ShapeDtypeStruct((3, 256, 128), F32),
        ),
        in_specs=[pl.BlockSpec(memory_space=pltpu.MemorySpace.HBM)] * 7,
        out_specs=[pl.BlockSpec(memory_space=VMEM)] * 2 + [pl.BlockSpec(memory_space=pltpu.MemorySpace.HBM)],
        scratch_shapes=[pltpu.VMEM(shape, F32) for shape in buffers[:7]]
        + [pltpu.VMEM((STEPS, 768, 128), BF16)]
        + [pltpu.VMEM(shape, F32) for shape in buffers[7:]] + [sem(shape) for shape in sems],
        compiler_params=pltpu.CompilerParams(
            collective_id=0, has_side_effects=True, vmem_limit_bytes=VMEM_LIMIT),
    )(disp, vel, slopes, stretch, moduli, buoy, probes)


def factor_kernel(scale, gram, tall, disp, basis, factor, out, stage, sem):
    enter = pltpu.make_async_copy(disp, stage, sem.at[0])
    leave = pltpu.make_async_copy(stage, out, sem.at[1])
    enter.start()
    lane = lanes()
    sub = lax.broadcasted_iota(jnp.int32, (8, 128), 0)
    a = [gram[i] for i in range(16)]
    for b in range(16):
        if b == 4:
            enter.wait()
            leave.start()
        j0 = 8 * b
        inside = (lane >= j0) & (lane < j0 + 8)
        cols = [jnp.broadcast_to(a[b][:, j0 + t:j0 + t + 1], (8, 128)) for t in range(8)]
        d = [[jnp.broadcast_to(cols[t][s:s + 1, :], (8, 128)) if t >= s else None for t in range(8)]
             for s in range(8)]
        inv = [None] * 8
        m = [[None] * 8 for _ in range(8)]
        for s in range(8):
            inv[s] = 1.0 / d[s][s]
            for t in range(s + 1, 8):
                m[s][t] = d[s][t] * inv[s]
                for q in range(t, 8):
                    d[t][q] = d[t][q] - m[s][t] * d[s][q]
        unit = [None] * 8
        fresh = a[b]
        for t in range(8):
            x = jnp.broadcast_to(a[b][t:t + 1, :], (8, 128))
            for s in range(t):
                x = jnp.where(lane == j0 + s, 0.0, x) - m[s][t] * unit[s]
            unit[t] = jnp.where(lane == j0 + t, 1.0, x)
            fresh = jnp.where(sub == t, x, fresh)
        a[b] = fresh
        below = [jnp.where((lane > j0 + t) & inside, 0.0, unit[t]) for t in range(8)]
        for i in range(b + 1, 16):
            c = [jnp.broadcast_to(a[i][:, j0 + s:j0 + s + 1], (8, 128)) for s in range(8)]
            x = jnp.where(inside, 0.0, a[i])
            for s in range(8):
                ms = c[s] * inv[s]
                for t in range(s + 1, 8):
                    c[t] = c[t] - ms * d[s][t]
                x = x - ms * below[s]
            a[i] = x
    inverse = []
    for i in range(16):
        rows = sub + 8 * i
        diag = jnp.sum(jnp.where(lane == rows, a[i], 0.0), axis=1, keepdims=True)
        root = lax.rsqrt(diag)
        factor[8 * i:8 * i + 8, :] = jnp.where(lane >= rows, a[i], 0.0) * root
        inverse.append(jnp.where(lane == rows, 1.0, jnp.where(lane < rows, a[i], 0.0)) * (root * scale))
    inverse = jnp.concatenate(inverse, axis=0)
    q = lax.dot_general(
        tall[...], inverse, (((1,), (1,)), ((), ())), precision=HIGH, preferred_element_type=F32)
    for xh in range(4):
        for r in range(6):
            basis[r, xh:xh + 1, :] = q[6 * xh + r:6 * xh + r + 1, :]
    leave.wait()


def finish(gram, tall, disp, scale):
    return pl.pallas_call(
        functools.partial(factor_kernel, scale),
        name="factor",
        out_shape=(
            jax.ShapeDtypeStruct((6, 4, 128), F32),
            jax.ShapeDtypeStruct((128, 128), F32),
            jax.ShapeDtypeStruct((3, 256, 128), F32),
        ),
        in_specs=[pl.BlockSpec(memory_space=VMEM)] * 2 + [pl.BlockSpec(memory_space=pltpu.MemorySpace.HBM)],
        out_specs=[pl.BlockSpec(memory_space=VMEM)] * 2 + [pl.BlockSpec(memory_space=pltpu.MemorySpace.HBM)],
        scratch_shapes=[pltpu.VMEM((3, 256, 128), F32), pltpu.SemaphoreType.DMA((2,))],
        compiler_params=pltpu.CompilerParams(vmem_limit_bytes=VMEM_LIMIT),
    )(gram, tall, disp)


def shards(displacement, velocity, slopes, stretch, moduli, buoyancy, probes):
    tall, gram, moved = wave(
        displacement.reshape(3, 256, 128), velocity.reshape(3, 256, 128), slopes.reshape(2, 256, 128),
        stretch.reshape(256, 128), moduli.reshape(2, 256, 128), buoyancy.reshape(256, 128), probes)
    rows = tall.shape[0] * lax.axis_size("gx") * lax.axis_size("gy")
    basis, factor, moved = finish(gram, tall, moved, math.sqrt(rows))
    return moved.reshape(3, 32, 8, 128), jnp.transpose(basis, (1, 0, 2)), factor


def solution(mesh):
    in_specs = (
        P(None, None, "gx", "gy"),
        P(None, None, "gx", "gy"),
        P(None, None, "gx", "gy"),
        P(None, "gx", "gy"),
        P(None, None, "gx", "gy"),
        P(None, "gx", "gy"),
        P(None, "gy", None),
    )
    out_specs = (P(None, None, "gx", "gy"), P("gx", "gy", None), P())
    return jax.shard_map(shards, mesh=mesh, in_specs=in_specs, out_specs=out_specs, check_vma=False)
```

```python
import functools
import math

import jax
import jax.numpy as jnp
from jax import lax
from jax.experimental import pallas as pl
from jax.experimental.pallas import tpu as pltpu
from jax.sharding import PartitionSpec as P

STEPS = 4
DT = 0.12
MESH = pl.DeviceIdType.MESH
HIGH = lax.Precision.HIGHEST
F32 = jnp.float32
BF16 = jnp.bfloat16
ZP = 48
VMEM = pltpu.MemorySpace.VMEM
VMEM_LIMIT = 24 * 1024 * 1024


def lanes():
    return lax.broadcasted_iota(jnp.int32, (8, 128), 1)


def shifted(f, h, lane):
    m2 = pltpu.roll(jnp.where(lane >= 126, h, f), 2, 1)
    m1 = pltpu.roll(jnp.where(lane >= 127, h, f), 1, 1)
    p1 = pltpu.roll(jnp.where(lane < 1, h, f), 127, 1)
    p2 = pltpu.roll(jnp.where(lane < 2, h, f), 126, 1)
    return m2, m1, p1, p2


def combine(m2, m1, p1, p2):
    return (m2 - p2) + 8.0 * (p1 - m1)


def split(x):
    hi = x.astype(BF16)
    rest = x - hi.astype(F32)
    mid = rest.astype(BF16)
    return hi, mid, (rest - mid.astype(F32)).astype(BF16)


def wave_kernel(
    disp_hbm, vel_hbm, slopes_hbm, stretch_hbm, moduli_hbm, buoy_hbm, probes_hbm,
    tall, gram, out,
    disp, vel, slopes, stretch, moduli, buoy, probes,
    PE, spread, U, S, MET, RATE, SK, PU, PS, HU, HS,
    PIECES, RB, GL, RA, PA, RBB, GS,
    load_sem, send_x, recv_x, send_y, recv_y,
    s0, r0, s1, r1, s2, r2, s3, r3,
):
    gx, gy = lax.axis_index("gx"), lax.axis_index("gy")
    nx, ny = lax.axis_size("gx"), lax.axis_size("gy")
    left = (lax.rem(gx + nx - 1, nx), gy)
    right = (lax.rem(gx + 1, nx), gy)
    down = (gx, lax.rem(gy + ny - 1, ny))
    up = (gx, lax.rem(gy + 1, ny))
    core = lax.rem(gx, 2)
    has_off = (gx > 0) & (gx < nx - 1)
    pair = gx - core
    a_me = gy * 2 + core
    b_me = gx // 2

    def a_dev(a):
        return (pair + lax.rem(a, 2), a // 2)

    def b_dev(b):
        return (b * 2 + core, gy)

    def far_first(i, half):
        step = (i + 1) // 2
        return half + step * (2 * lax.rem(i, 2) - 1)

    loads = [
        pltpu.make_async_copy(src, dst, load_sem.at[i])
        for i, (src, dst) in enumerate((
            (disp_hbm, disp), (vel_hbm, vel), (slopes_hbm, slopes), (stretch_hbm, stretch),
            (moduli_hbm, moduli), (buoy_hbm, buoy), (probes_hbm, probes)))
    ]
    for copy in loads:
        copy.start()

    barrier = pltpu.get_barrier_semaphore()

    @pl.loop(0, 15)
    def _(i):
        d = far_first(i, 8)
        pl.semaphore_signal(barrier, inc=1, device_id=a_dev(lax.rem(a_me + d, 16)), device_id_type=MESH)
        pl.semaphore_signal(barrier, inc=1, device_id=b_dev(lax.rem(b_me + d, 16)), device_id_type=MESH)

    for peer in (left, right):
        pl.semaphore_signal(barrier, inc=1, device_id=peer, device_id_type=MESH)

    lane = lanes()
    zero8 = jnp.zeros((8, 128), F32)
    low_part = (lane & 3) < 2

    @pl.loop(0, 12)
    def _(x):
        for s in range(2):
            for c in range(3):
                U[s, c, x, 0:8, :] = zero8
                U[s, c, x, 40:48, :] = zero8
        for c in range(6):
            S[c, x, 0:8, :] = zero8
            S[c, x, 40:48, :] = zero8

    def clear(x):
        for c in range(3):
            for z0 in range(8, 40, 8):
                U[0, c, x, z0:z0 + 8, :] = zero8
                U[1, c, x, z0:z0 + 8, :] = zero8
                S[c, x, z0:z0 + 8, :] = zero8

    @pl.when(gx == 0)
    def _():
        clear(0)
        clear(1)

    @pl.when(gx == nx - 1)
    def _():
        clear(10)
        clear(11)

    INNER, ON, OFF = 0, 1, 2

    def side(part):
        return core if part == OFF else 1 - core

    def x_copy(ref, kind, part):
        s = side(part)
        return pltpu.make_async_remote_copy(
            src_ref=ref(pl.ds(2 + 6 * s, 2)), dst_ref=ref(pl.ds(10 - 10 * s, 2)), send_sem=send_x.at[kind, part - 1],
            recv_sem=recv_x.at[kind, part - 1], device_id=(gx - 1 + 2 * s, gy), device_id_type=MESH)

    def x_start(ref, kind, part):
        if part == ON:
            x_copy(ref, kind, part).start()
        else:
            @pl.when(has_off)
            def _():
                x_copy(ref, kind, part).start()

    def x_wait(ref, kind, part):
        if part == ON:
            x_copy(ref, kind, part).wait()
        else:
            @pl.when(has_off)
            def _():
                x_copy(ref, kind, part).wait()

    def y_copies(packed, halo, kind, part):
        return [
            pltpu.make_async_remote_copy(
                src_ref=packed.at[part], dst_ref=halo.at[part, 1 - d], send_sem=send_y.at[kind, part, d],
                recv_sem=recv_y.at[kind, part, d], device_id=peer, device_id_type=MESH)
            for d, peer in enumerate((down, up))
        ]

    def y_send(values, packed, halo, kind, part):
        for c in range(3):
            packed[part, c] = values[c]
        for copy in y_copies(packed, halo, kind, part):
            copy.start()

    def y_wait(packed, halo, kind, part):
        for copy in y_copies(packed, halo, kind, part):
            copy.wait()
        result = []
        for c in range(3):
            lo = jnp.where(gy == 0, zero8, halo[part, 0, c])
            hi = jnp.where(gy == ny - 1, zero8, halo[part, 1, c])
            result.append(jnp.where(low_part, lo, hi))
        return result

    def u_planes(cur):
        return lambda xs: U.at[cur, :, xs, 8:40, :]

    def s_planes(xs):
        return S.at[0:3, xs, 8:40, :]

    def plane(part, i):
        return i + 2 if part == INNER else i + 6 * side(part)

    loads[0].wait()

    def load_u(part):
        def body(i, carry):
            x = plane(part, i)
            packed = list(carry)
            for zb in range(4):
                rows = pl.ds(zb * 64 + x, 8, stride=8)
                k = x * 4 + zb
                for c in range(3):
                    d = disp[c, rows, :]
                    U[0, c, x + 2, zb * 8 + 8:zb * 8 + 16, :] = d
                    packed[c] = jnp.where((lane >> 2) == k, pltpu.roll(d, 4 * k + 2, 1), packed[c])
            return tuple(packed)

        return lax.fori_loop(0, 4 if part == INNER else 2, body, (zero8,) * 3)

    first = [load_u(INNER), load_u(ON), load_u(OFF)]
    pl.semaphore_wait(barrier, 32)
    for part in (OFF, ON):
        x_start(u_planes(0), 0, part)
    for part in (INNER, OFF, ON):
        y_send(first[part], PU, HU, 0, part)

    for copy in loads[1:]:
        copy.wait()

    @pl.loop(0, 8)
    def _(x):
        for zb in range(4):
            rows = pl.ds(zb * 64 + x, 8, stride=8)
            zs = slice(zb * 8, zb * 8 + 8)
            zu = slice(zb * 8 + 8, zb * 8 + 16)
            MET[0, x, zs, :] = slopes[0, rows, :]
            MET[1, x, zs, :] = slopes[1, rows, :]
            MET[2, x, zs, :] = stretch[rows, :]
            MET[3, x, zs, :] = moduli[0, rows, :] * (1.0 / 12.0)
            MET[4, x, zs, :] = moduli[1, rows, :] * (1.0 / 12.0)
            MET[5, x, zs, :] = buoy[rows, :] * (DT * DT / 12.0)
            for c in range(3):
                U[1, c, x + 2, zu, :] = U[0, c, x + 2, zu, :] - DT * vel[c, rows, :]

    spread[...] = jnp.zeros((128, 128), F32)
    for n in range(STEPS):
        spread[pl.ds(0, 64, stride=2), :] = probes[n] * (1.0 / (2.0 * DT))
        hi, mid, lo = split(spread[...])
        for i, term in enumerate((hi, mid, hi, lo, mid, hi)):
            PE[n, 128 * i:128 * i + 128, :] = term
    SK[...] = jnp.zeros_like(SK)

    def sketch(n, outer):
        where = (0, 3) if outer else (1, 2)
        hi, mid, lo = split(jnp.concatenate(
            [RATE[c, 2 * xh, pl.ds(0, 16, stride=2), :] for xh in where for c in range(3)], axis=0))
        term = jnp.dot(
            jnp.concatenate([hi, hi, mid, hi, mid, lo], axis=1), PE[n], preferred_element_type=F32)
        for i, xh in enumerate(where):
            SK[48 * xh:48 * xh + 48, :] += term[48 * i:48 * i + 48, :]

    def over_planes(part, planes, cell, put):
        def body(i, packed):
            cells = [(plane(part, i * planes + j), zb) for j in range(planes) for zb in range(4)]
            values = [cell(x, zb) for x, zb in cells]
            packed = list(packed)
            for (x, zb), value in zip(cells, values):
                edge = put(x, zb, value)
                k = x * 4 + zb
                here = (lane >> 2) == k
                for c in range(3):
                    packed[c] = jnp.where(here, pltpu.roll(edge[c], 4 * k + 2, 1), packed[c])
            return tuple(packed)

        if part != INNER:
            return body(0, (zero8,) * 3)
        return lax.fori_loop(0, 4 // planes, body, (zero8,) * 3)

    def stress(cur, part, halos):
        def cell(x, zb):
            z0 = zb * 8
            zs, zu = slice(z0, z0 + 8), slice(z0 + 8, z0 + 16)
            k = x * 4 + zb
            sx, sy, st = MET[0, x, zs, :], MET[1, x, zs, :], MET[2, x, zs, :]
            lam, mu = MET[3, x, zs, :], MET[4, x, zs, :]
            g = []
            for c in range(3):
                f = U[cur, c, x + 2, zu, :]
                dx = combine(U[cur, c, x, zu, :], U[cur, c, x + 1, zu, :],
                             U[cur, c, x + 3, zu, :], U[cur, c, x + 4, zu, :])
                dr = combine(*[U[cur, c, x + 2, z0 + o:z0 + o + 8, :] for o in (6, 7, 9, 10)])
                dy = combine(*shifted(f, pltpu.roll(halos[c], 126 - 4 * k, 1), lane))
                g.append((dx + sx * dr, dy + sy * dr, st * dr))
            pressure = lam * (g[0][0] + g[1][1] + g[2][2])
            mu2 = mu + mu
            return (pressure + mu2 * g[0][0], mu * (g[0][1] + g[1][0]), mu * (g[0][2] + g[2][0]),
                    pressure + mu2 * g[1][1], mu * (g[1][2] + g[2][1]), pressure + mu2 * g[2][2])

        def put(x, zb, value):
            for j in range(6):
                S[j, x + 2, zb * 8 + 8:zb * 8 + 16, :] = value[j]
            return value[1], value[3], value[4]

        return over_planes(part, 2, cell, put)

    def forces(cur, part, halos):
        old = 1 - cur

        def cell(x, zb):
            z0 = zb * 8
            zs, zu = slice(z0, z0 + 8), slice(z0 + 8, z0 + 16)
            k = x * 4 + zb
            sx, sy, st, b = (MET[j, x, zs, :] for j in (0, 1, 2, 5))

            def d_x(j):
                return combine(S[j, x, zu, :], S[j, x + 1, zu, :], S[j, x + 3, zu, :], S[j, x + 4, zu, :])

            def d_y(j, h):
                return combine(*shifted(S[j, x + 2, zu, :], pltpu.roll(h, 126 - 4 * k, 1), lane))

            dr = [combine(*[S[j, x + 2, z0 + o:z0 + o + 8, :] for o in (6, 7, 9, 10)]) for j in range(6)]
            acc = (
                d_x(0) + sx * dr[0] + d_y(1, halos[0]) + sy * dr[1] + st * dr[2],
                d_x(1) + sx * dr[1] + d_y(3, halos[1]) + sy * dr[3] + st * dr[4],
                d_x(2) + sx * dr[2] + d_y(4, halos[2]) + sy * dr[4] + st * dr[5],
            )
            moved = []
            for c in range(3):
                u, p = U[cur, c, x + 2, zu, :], U[old, c, x + 2, zu, :]
                fol = (u + u - p) + b * acc[c]
                moved.append((fol, fol - p))
            return moved

        def put(x, zb, value):
            z0 = zb * 8
            for c in range(3):
                U[old, c, x + 2, z0 + 8:z0 + 16, :] = value[c][0]
                RATE[c, x, z0:z0 + 8, :] = value[c][1]
            return [v[0] for v in value]

        return over_planes(part, 2, cell, put)

    def step(n, carry):
        cur = lax.rem(n, 2)
        more = n < STEPS - 1
        packed = stress(cur, INNER, y_wait(PU, HU, 0, INNER))
        y_send(packed, PS, HS, 1, INNER)

        @pl.when(n > 0)
        def _():
            sketch(n - 1, True)

        for part in (ON, OFF):
            halos = y_wait(PU, HU, 0, part)
            x_wait(u_planes(cur), 0, part)
            packed = stress(cur, part, halos)
            x_start(s_planes, 1, part)
            y_send(packed, PS, HS, 1, part)

        packed = forces(cur, INNER, y_wait(PS, HS, 1, INNER))

        @pl.when(more)
        def _():
            y_send(packed, PU, HU, 0, INNER)

        sketch(n, False)
        for part in (ON, OFF):
            halos = y_wait(PS, HS, 1, part)
            x_wait(s_planes, 1, part)
            packed = forces(cur, part, halos)

            @pl.when(more)
            def _():
                x_start(u_planes(1 - cur), 0, part)
                y_send(packed, PU, HU, 0, part)

        return carry

    lax.fori_loop(0, STEPS, step, 0)
    sketch(STEPS - 1, True)
    for g in range(8):
        for xh in range(4):
            PIECES[g, 6 * xh:6 * xh + 6, :] = SK[xh * 48 + 6 * g:xh * 48 + 6 * g + 6, :]

    def piece(g, slot):
        return pltpu.make_async_remote_copy(
            src_ref=PIECES.at[g], dst_ref=RB.at[slot], send_sem=s0.at[g], recv_sem=r0.at[slot],
            device_id=(gx, g), device_id_type=MESH)

    @pl.loop(0, 7)
    def _(i):
        piece(lax.rem(gy + far_first(i, 4), 8), gy).start()

    RB[gy] = PIECES[gy]

    final = STEPS % 2

    @pl.loop(0, 8)
    def _(x):
        for zb in range(4):
            for c in range(3):
                out[c, pl.ds(zb * 64 + x, 8, stride=8), :] = U[final, c, x + 2, zb * 8 + 8:zb * 8 + 16, :]

    @pl.loop(1, 8)
    def _(d):
        g = lax.rem(gy + d, 8)
        piece(g, g).wait()

    total = RB[0]
    for g in range(1, 8):
        total = total + RB[g]
    tall[...] = total
    hi, mid, lo = (term.astype(F32) for term in split(total))
    GL[...] = lax.dot_general(
        jnp.concatenate([hi, hi, mid, hi, mid, lo], axis=0).astype(BF16),
        jnp.concatenate([hi, mid, hi, lo, mid, hi], axis=0).astype(BF16),
        (((0,), (0,)), ((), ())), preferred_element_type=F32).reshape(16, 8, 128)

    def group(dev, me, src, dst, send, recv):
        def make(slot, peer):
            return pltpu.make_async_remote_copy(
                src_ref=src(peer), dst_ref=dst.at[slot], send_sem=send.at[peer], recv_sem=recv.at[slot],
                device_id=dev(peer), device_id_type=MESH)

        @pl.loop(0, 15)
        def _(i):
            make(me, lax.rem(me + far_first(i, 8), 16)).start()

        def finish():
            @pl.loop(1, 16)
            def _(d):
                peer = lax.rem(me + d, 16)
                make(peer, peer).wait()

        return finish

    def summed(ref):
        parts = [ref[i] for i in range(16)]
        while len(parts) > 1:
            parts = [parts[i] + parts[i + 1] for i in range(0, len(parts), 2)]
        return parts[0]

    finish = group(b_dev, b_me, lambda p: GL.at[p], RA, s1, r1)
    RA[b_me] = GL[b_me]
    finish()
    part = summed(RA)
    PA[...] = part
    finish = group(a_dev, a_me, lambda p: PA, RBB, s2, r2)
    RBB[a_me] = part
    finish()
    whole = summed(RBB)
    GS[...] = whole
    finish = group(b_dev, b_me, lambda p: GS, gram, s3, r3)
    gram[b_me] = whole
    finish()


def wave(disp, vel, slopes, stretch, moduli, buoy, probes):
    sem = pltpu.SemaphoreType.DMA
    buffers = [
        (3, 256, 128), (3, 256, 128), (2, 256, 128), (256, 128), (2, 256, 128), (256, 128), (STEPS, 64, 128),
        (128, 128), (2, 3, 12, ZP, 128), (6, 12, ZP, 128), (6, 8, 32, 128), (3, 8, 32, 128), (192, 128),
        (3, 3, 8, 128), (3, 3, 8, 128), (3, 2, 3, 8, 128), (3, 2, 3, 8, 128),
        (8, 24, 128), (8, 24, 128), (16, 8, 128), (16, 8, 128), (8, 128), (16, 8, 128), (8, 128),
    ]
    sems = [(7,), (2, 2), (2, 2), (2, 3, 2), (2, 3, 2)] + [(8,)] * 2 + [(16,)] * 6
    return pl.pallas_call(
        wave_kernel,
        name="wave",
        out_shape=(
            jax.ShapeDtypeStruct((24, 128), F32),
            jax.ShapeDtypeStruct((16, 8, 128), F32),
            jax.ShapeDtypeStruct((3, 256, 128), F32),
        ),
        in_specs=[pl.BlockSpec(memory_space=pltpu.MemorySpace.HBM)] * 7,
        out_specs=[pl.BlockSpec(memory_space=VMEM)] * 3,
        scratch_shapes=[pltpu.VMEM(shape, F32) for shape in buffers[:7]]
        + [pltpu.VMEM((STEPS, 768, 128), BF16)]
        + [pltpu.VMEM(shape, F32) for shape in buffers[7:]] + [sem(shape) for shape in sems],
        compiler_params=pltpu.CompilerParams(
            collective_id=0, has_side_effects=True, vmem_limit_bytes=VMEM_LIMIT),
    )(*[pltpu.with_memory_space_constraint(x, pltpu.MemorySpace.HBM)
        for x in (disp, vel, slopes, stretch, moduli, buoy, probes)])


def factor_kernel(scale, gram, tall, disp, basis, factor, out, sem):
    leave = pltpu.make_async_copy(disp, out, sem)
    leave.start()
    lane = lanes()
    sub = lax.broadcasted_iota(jnp.int32, (8, 128), 0)
    a = [gram[i] for i in range(16)]
    for b in range(16):
        j0 = 8 * b
        inside = (lane >= j0) & (lane < j0 + 8)
        cols = [jnp.broadcast_to(a[b][:, j0 + t:j0 + t + 1], (8, 128)) for t in range(8)]
        d = [[jnp.broadcast_to(cols[t][s:s + 1, :], (8, 128)) if t >= s else None for t in range(8)]
             for s in range(8)]
        inv = [None] * 8
        m = [[None] * 8 for _ in range(8)]
        for s in range(8):
            inv[s] = 1.0 / d[s][s]
            for t in range(s + 1, 8):
                m[s][t] = d[s][t] * inv[s]
                for q in range(t, 8):
                    d[t][q] = d[t][q] - m[s][t] * d[s][q]
        unit = [None] * 8
        fresh = a[b]
        for t in range(8):
            x = jnp.broadcast_to(a[b][t:t + 1, :], (8, 128))
            for s in range(t):
                x = jnp.where(lane == j0 + s, 0.0, x) - m[s][t] * unit[s]
            unit[t] = jnp.where(lane == j0 + t, 1.0, x)
            fresh = jnp.where(sub == t, x, fresh)
        a[b] = fresh
        below = [jnp.where((lane > j0 + t) & inside, 0.0, unit[t]) for t in range(8)]
        for i in range(b + 1, 16):
            c = [jnp.broadcast_to(a[i][:, j0 + s:j0 + s + 1], (8, 128)) for s in range(8)]
            x = jnp.where(inside, 0.0, a[i])
            for s in range(8):
                ms = c[s] * inv[s]
                for t in range(s + 1, 8):
                    c[t] = c[t] - ms * d[s][t]
                x = x - ms * below[s]
            a[i] = x
    inverse = []
    for i in range(16):
        rows = sub + 8 * i
        diag = jnp.sum(jnp.where(lane == rows, a[i], 0.0), axis=1, keepdims=True)
        root = lax.rsqrt(diag)
        factor[8 * i:8 * i + 8, :] = jnp.where(lane >= rows, a[i], 0.0) * root
        inverse.append(jnp.where(lane == rows, 1.0, jnp.where(lane < rows, a[i], 0.0)) * (root * scale))
    inverse = jnp.concatenate(inverse, axis=0)
    q = lax.dot_general(
        tall[...], inverse, (((1,), (1,)), ((), ())), precision=HIGH, preferred_element_type=F32)
    for xh in range(4):
        for r in range(6):
            basis[r, xh:xh + 1, :] = q[6 * xh + r:6 * xh + r + 1, :]
    leave.wait()


def finish(gram, tall, disp, scale):
    return pl.pallas_call(
        functools.partial(factor_kernel, scale),
        name="factor",
        out_shape=(
            jax.ShapeDtypeStruct((6, 4, 128), F32),
            jax.ShapeDtypeStruct((128, 128), F32),
            jax.ShapeDtypeStruct((3, 256, 128), F32),
        ),
        in_specs=[pl.BlockSpec(memory_space=VMEM)] * 3,
        out_specs=[pl.BlockSpec(memory_space=VMEM)] * 2 + [pl.BlockSpec(memory_space=pltpu.MemorySpace.HBM)],
        scratch_shapes=[pltpu.SemaphoreType.DMA],
        compiler_params=pltpu.CompilerParams(vmem_limit_bytes=VMEM_LIMIT),
    )(gram, tall, disp)


def shards(displacement, velocity, slopes, stretch, moduli, buoyancy, probes):
    tall, gram, moved = wave(
        displacement.reshape(3, 256, 128), velocity.reshape(3, 256, 128), slopes.reshape(2, 256, 128),
        stretch.reshape(256, 128), moduli.reshape(2, 256, 128), buoyancy.reshape(256, 128), probes)
    rows = tall.shape[0] * lax.axis_size("gx") * lax.axis_size("gy")
    basis, factor, moved = finish(gram, tall, moved, math.sqrt(rows))
    return moved.reshape(3, 32, 8, 128), jnp.transpose(basis, (1, 0, 2)), factor


def solution(mesh):
    in_specs = (
        P(None, None, "gx", "gy"),
        P(None, None, "gx", "gy"),
        P(None, None, "gx", "gy"),
        P(None, "gx", "gy"),
        P(None, None, "gx", "gy"),
        P(None, "gx", "gy"),
        P(None, "gy", None),
    )
    out_specs = (P(None, None, "gx", "gy"), P("gx", "gy", None), P())
    return jax.shard_map(shards, mesh=mesh, in_specs=in_specs, out_specs=out_specs, check_vma=False)
```

```python
import functools
import math

import jax
import jax.numpy as jnp
from jax import lax
from jax.experimental import pallas as pl
from jax.experimental.pallas import tpu as pltpu
from jax.sharding import PartitionSpec as P

STEPS = 4
DT = 0.12
MESH = pl.DeviceIdType.MESH
HIGH = lax.Precision.HIGHEST
F32 = jnp.float32
BF16 = jnp.bfloat16
ZP = 48
VMEM = pltpu.MemorySpace.VMEM
VMEM_LIMIT = 24 * 1024 * 1024


def lanes():
    return lax.broadcasted_iota(jnp.int32, (8, 128), 1)


def shifted(f, h, lane):
    m2 = pltpu.roll(jnp.where(lane >= 126, h, f), 2, 1)
    m1 = pltpu.roll(jnp.where(lane >= 127, h, f), 1, 1)
    p1 = pltpu.roll(jnp.where(lane < 1, h, f), 127, 1)
    p2 = pltpu.roll(jnp.where(lane < 2, h, f), 126, 1)
    return m2, m1, p1, p2


def combine(m2, m1, p1, p2):
    return (m2 - p2) + 8.0 * (p1 - m1)


def split(x):
    hi = x.astype(BF16)
    rest = x - hi.astype(F32)
    mid = rest.astype(BF16)
    return hi, mid, (rest - mid.astype(F32)).astype(BF16)


def wave_kernel(
    disp_hbm, vel_hbm, slopes_hbm, stretch_hbm, moduli_hbm, buoy_hbm, probes_hbm,
    tall, gram, out,
    disp, vel, slopes, stretch, moduli, buoy, probes,
    PE, spread, U, S, MET, RATE, SK, PU, PS, HU, HS,
    SA, AH, MH, PIECES, RB, GL, RA, PA, RBB, GS,
    load_sem, send_u, recv_u, send_s, recv_s, send_y, recv_y, send_a, recv_a, moduli_sem,
    s0, r0, s1, r1, s2, r2, s3, r3,
):
    gx, gy = lax.axis_index("gx"), lax.axis_index("gy")
    nx, ny = lax.axis_size("gx"), lax.axis_size("gy")
    left = (lax.rem(gx + nx - 1, nx), gy)
    right = (lax.rem(gx + 1, nx), gy)
    down = (gx, lax.rem(gy + ny - 1, ny))
    up = (gx, lax.rem(gy + 1, ny))
    core = lax.rem(gx, 2)
    has_off = (gx > 0) & (gx < nx - 1)
    pair = gx - core
    a_me = gy * 2 + core
    b_me = gx // 2

    def a_dev(a):
        return (pair + lax.rem(a, 2), a // 2)

    def b_dev(b):
        return (b * 2 + core, gy)

    def far_first(i, half):
        step = (i + 1) // 2
        return half + step * (2 * lax.rem(i, 2) - 1)

    loads = [
        pltpu.make_async_copy(src, dst, load_sem.at[i])
        for i, (src, dst) in enumerate((
            (disp_hbm, disp), (vel_hbm, vel), (slopes_hbm, slopes), (stretch_hbm, stretch),
            (moduli_hbm, moduli), (buoy_hbm, buoy), (probes_hbm, probes)))
    ]
    for copy in loads:
        copy.start()

    barrier = pltpu.get_barrier_semaphore()

    @pl.loop(0, 15)
    def _(i):
        d = far_first(i, 8)
        pl.semaphore_signal(barrier, inc=1, device_id=a_dev(lax.rem(a_me + d, 16)), device_id_type=MESH)
        pl.semaphore_signal(barrier, inc=1, device_id=b_dev(lax.rem(b_me + d, 16)), device_id_type=MESH)

    for peer in (left, right):
        pl.semaphore_signal(barrier, inc=1, device_id=peer, device_id_type=MESH)

    lane = lanes()
    zero8 = jnp.zeros((8, 128), F32)
    low_part = (lane & 3) < 2

    @pl.loop(0, 12)
    def _(x):
        for s in range(2):
            for c in range(3):
                U[s, c, x, 0:8, :] = zero8
                U[s, c, x, 40:48, :] = zero8
        for c in range(6):
            S[c, x, 0:8, :] = zero8
            S[c, x, 40:48, :] = zero8

    @pl.when(jnp.logical_not(has_off))
    def _():
        for i in range(2):
            for z0 in range(0, 32, 8):
                for c in range(3):
                    AH[0, c, i, z0:z0 + 8, :] = zero8
                    AH[1, c, i, z0:z0 + 8, :] = zero8
                for c in range(2):
                    MH[c, i, z0:z0 + 8, :] = zero8

    def clear(x):
        for c in range(3):
            for z0 in range(8, 40, 8):
                U[0, c, x, z0:z0 + 8, :] = zero8
                U[1, c, x, z0:z0 + 8, :] = zero8
                S[c, x, z0:z0 + 8, :] = zero8

    @pl.when(gx == 0)
    def _():
        clear(0)
        clear(1)

    @pl.when(gx == nx - 1)
    def _():
        clear(10)
        clear(11)

    INNER, ON, OFF = 0, 1, 2

    def side(part):
        return core if part == OFF else 1 - core

    def u_copy(cur, part):
        s = side(part)
        index = 2 * cur + part - 1
        return pltpu.make_async_remote_copy(
            src_ref=U.at[cur, :, pl.ds(2 + 6 * s, 2), 8:40, :], dst_ref=U.at[cur, :, pl.ds(10 - 10 * s, 2), 8:40, :],
            send_sem=send_u.at[index], recv_sem=recv_u.at[index],
            device_id=(gx - 1 + 2 * s, gy), device_id_type=MESH)

    def s_copy():
        s = side(ON)
        return pltpu.make_async_remote_copy(
            src_ref=S.at[0:3, pl.ds(2 + 6 * s, 2), 8:40, :], dst_ref=S.at[0:3, pl.ds(10 - 10 * s, 2), 8:40, :],
            send_sem=send_s, recv_sem=recv_s, device_id=(gx - 1 + 2 * s, gy), device_id_type=MESH)

    def far_copy(src, dst, send, recv):
        return pltpu.make_async_remote_copy(
            src_ref=src, dst_ref=dst, send_sem=send, recv_sem=recv,
            device_id=(gx - 1 + 2 * turn, gy), device_id_type=MESH)

    def partial_copy(parity):
        return far_copy(SA, AH.at[parity], send_a.at[parity], recv_a.at[parity])

    def moduli_copy():
        return far_copy(MET.at[3:5, pl.ds(6 * turn, 2)], MH, moduli_sem.at[0], moduli_sem.at[1])

    def u_start(cur, part):
        if part == ON:
            u_copy(cur, part).start()
        else:
            @pl.when(has_off)
            def _():
                u_copy(cur, part).start()

    def u_wait(cur, part):
        if part == ON:
            u_copy(cur, part).wait()
        else:
            @pl.when(has_off)
            def _():
                u_copy(cur, part).wait()

    def y_copies(packed, halo, kind, part):
        return [
            pltpu.make_async_remote_copy(
                src_ref=packed.at[part], dst_ref=halo.at[part, 1 - d], send_sem=send_y.at[kind, part, d],
                recv_sem=recv_y.at[kind, part, d], device_id=peer, device_id_type=MESH)
            for d, peer in enumerate((down, up))
        ]

    def y_send(values, packed, halo, kind, part):
        for c in range(3):
            packed[part, c] = values[c]
        for copy in y_copies(packed, halo, kind, part):
            copy.start()

    def y_wait(packed, halo, kind, part):
        for copy in y_copies(packed, halo, kind, part):
            copy.wait()
        result = []
        for c in range(3):
            lo = jnp.where(gy == 0, zero8, halo[part, 0, c])
            hi = jnp.where(gy == ny - 1, zero8, halo[part, 1, c])
            result.append(jnp.where(low_part, lo, hi))
        return result

    turn = core
    outermost, second, inward = 7 * turn, 1 + 5 * turn, 1 - 2 * turn
    sign = jnp.where(turn == 0, 1.0, -1.0).astype(F32)

    def plane(part, i):
        if part == OFF:
            return second if i == 1 else outermost
        return i + 2 if part == INNER else i + 6 * side(part)

    loads[0].wait()

    def load_u(part):
        def body(i, carry):
            x = plane(part, i)
            packed = list(carry)
            for zb in range(4):
                rows = pl.ds(zb * 64 + x, 8, stride=8)
                k = x * 4 + zb
                for c in range(3):
                    d = disp[c, rows, :]
                    U[0, c, x + 2, zb * 8 + 8:zb * 8 + 16, :] = d
                    packed[c] = jnp.where((lane >> 2) == k, pltpu.roll(d, 4 * k + 2, 1), packed[c])
            return tuple(packed)

        if part == OFF:
            return body(1, body(0, (zero8,) * 3))
        return lax.fori_loop(0, 4 if part == INNER else 2, body, (zero8,) * 3)

    first = [load_u(INNER), load_u(ON), load_u(OFF)]
    pl.semaphore_wait(barrier, 32)
    for part in (OFF, ON):
        u_start(0, part)
    for part in (INNER, OFF, ON):
        y_send(first[part], PU, HU, 0, part)

    for copy in loads[1:]:
        copy.wait()

    @pl.loop(0, 8)
    def _(x):
        for zb in range(4):
            rows = pl.ds(zb * 64 + x, 8, stride=8)
            zs = slice(zb * 8, zb * 8 + 8)
            zu = slice(zb * 8 + 8, zb * 8 + 16)
            MET[0, x, zs, :] = slopes[0, rows, :]
            MET[1, x, zs, :] = slopes[1, rows, :]
            MET[2, x, zs, :] = stretch[rows, :]
            MET[3, x, zs, :] = moduli[0, rows, :] * (1.0 / 12.0)
            MET[4, x, zs, :] = moduli[1, rows, :] * (1.0 / 12.0)
            MET[5, x, zs, :] = buoy[rows, :] * (DT * DT / 12.0)
            for c in range(3):
                U[1, c, x + 2, zu, :] = U[0, c, x + 2, zu, :] - DT * vel[c, rows, :]

    @pl.when(has_off)
    def _():
        moduli_copy().start()

    spread[...] = jnp.zeros((128, 128), F32)
    for n in range(STEPS):
        spread[pl.ds(0, 64, stride=2), :] = probes[n] * (1.0 / (2.0 * DT))
        hi, mid, lo = split(spread[...])
        for i, term in enumerate((hi, mid, hi, lo, mid, hi)):
            PE[n, 128 * i:128 * i + 128, :] = term
    SK[...] = jnp.zeros_like(SK)

    def sketch(n, outer):
        where = (0, 3) if outer else (1, 2)
        hi, mid, lo = split(jnp.concatenate(
            [RATE[c, 2 * xh, pl.ds(0, 16, stride=2), :] for xh in where for c in range(3)], axis=0))
        term = jnp.dot(
            jnp.concatenate([hi, hi, mid, hi, mid, lo], axis=1), PE[n], preferred_element_type=F32)
        for i, xh in enumerate(where):
            SK[48 * xh:48 * xh + 48, :] += term[48 * i:48 * i + 48, :]

    def over_planes(part, planes, cell, put):
        def body(i, packed):
            cells = [(plane(part, i * planes + j), zb, j) for j in range(planes) for zb in range(4)]
            values = [cell(*where) for where in cells]
            packed = list(packed)
            for (x, zb, j), value in zip(cells, values):
                edge = put(x, zb, value, j)
                if edge is None:
                    continue
                k = x * 4 + zb
                here = (lane >> 2) == k
                for c in range(3):
                    packed[c] = jnp.where(here, pltpu.roll(edge[c], 4 * k + 2, 1), packed[c])
            return tuple(packed)

        if part != INNER:
            return body(0, (zero8,) * 3)
        return lax.fori_loop(0, 4 // planes, body, (zero8,) * 3)

    def stress(cur, part, halos):
        def d_x(c, x, zu, j):
            if part != OFF:
                return combine(U[cur, c, x, zu, :], U[cur, c, x + 1, zu, :],
                               U[cur, c, x + 3, zu, :], U[cur, c, x + 4, zu, :])
            ahead, second_ahead = U[cur, c, x + 2 + inward, zu, :], U[cur, c, x + 2 + 2 * inward, zu, :]
            if j == 1:
                ahead = ahead - U[cur, c, x + 2 - inward, zu, :]
            return sign * (8.0 * ahead - second_ahead)

        def cell(x, zb, j):
            z0 = zb * 8
            zs, zu = slice(z0, z0 + 8), slice(z0 + 8, z0 + 16)
            k = x * 4 + zb
            sx, sy, st = MET[0, x, zs, :], MET[1, x, zs, :], MET[2, x, zs, :]
            lam, mu = MET[3, x, zs, :], MET[4, x, zs, :]
            g = []
            for c in range(3):
                f = U[cur, c, x + 2, zu, :]
                dx = d_x(c, x, zu, j)
                dr = combine(*[U[cur, c, x + 2, z0 + o:z0 + o + 8, :] for o in (6, 7, 9, 10)])
                dy = combine(*shifted(f, pltpu.roll(halos[c], 126 - 4 * k, 1), lane))
                g.append((dx + sx * dr, dy + sy * dr, st * dr))
            pressure = lam * (g[0][0] + g[1][1] + g[2][2])
            mu2 = mu + mu
            return (pressure + mu2 * g[0][0], mu * (g[0][1] + g[1][0]), mu * (g[0][2] + g[2][0]),
                    pressure + mu2 * g[1][1], mu * (g[1][2] + g[2][1]), pressure + mu2 * g[2][2])

        def put(x, zb, value, j):
            for i in range(6):
                S[i, x + 2, zb * 8 + 8:zb * 8 + 16, :] = value[i]
            if part == OFF:
                for i in range(3):
                    SA[i, x - 6 * turn, zb * 8:zb * 8 + 8, :] = value[i]
                return None
            return value[1], value[3], value[4]

        return over_planes(part, 2, cell, put)

    def added(first, near, j):
        return first - 8.0 * near if j == 0 else near

    def complete(cur):
        def cell(x, zb, j):
            zs, zu = slice(zb * 8, zb * 8 + 8), slice(zb * 8 + 8, zb * 8 + 16)
            lam, mu = MET[3, x, zs, :], MET[4, x, zs, :]
            at = outermost + 2 - inward
            dx = [sign * added(U[cur, c, at - inward, zu, :], U[cur, c, at, zu, :], j) for c in range(3)]
            side_pressure = lam * dx[0]
            return (S[0, x + 2, zu, :] + (side_pressure + (mu + mu) * dx[0]), S[1, x + 2, zu, :] + mu * dx[1],
                    S[2, x + 2, zu, :] + mu * dx[2], S[3, x + 2, zu, :] + side_pressure,
                    S[5, x + 2, zu, :] + side_pressure, S[4, x + 2, zu, :])

        def put(x, zb, value, j):
            zu = slice(zb * 8 + 8, zb * 8 + 16)
            for i, row in enumerate((0, 1, 2, 3, 5)):
                S[row, x + 2, zu, :] = value[i]
            return value[1], value[3], value[5]

        return over_planes(OFF, 2, cell, put)

    def complete_beyond(cur, parity):
        for j in range(2):
            at = 1 - turn if j == 0 else turn
            for zb in range(4):
                zs, zu = slice(zb * 8, zb * 8 + 8), slice(zb * 8 + 8, zb * 8 + 16)
                lam, mu = MH[0, at, zs, :], MH[1, at, zs, :]
                dx = [-sign * added(U[cur, c, second + 2, zu, :], U[cur, c, outermost + 2, zu, :], j)
                      for c in range(3)]
                scale = (lam + (mu + mu), mu, mu)
                for c in range(3):
                    S[c, outermost + 2 - (1 + j) * inward, zu, :] = AH[parity, c, at, zs, :] + scale[c] * dx[c]

    def forces(cur, part, halos):
        old = 1 - cur

        def cell(x, zb, _):
            z0 = zb * 8
            zs, zu = slice(z0, z0 + 8), slice(z0 + 8, z0 + 16)
            k = x * 4 + zb
            sx, sy, st, b = (MET[j, x, zs, :] for j in (0, 1, 2, 5))

            def d_x(j):
                return combine(S[j, x, zu, :], S[j, x + 1, zu, :], S[j, x + 3, zu, :], S[j, x + 4, zu, :])

            def d_y(j, h):
                return combine(*shifted(S[j, x + 2, zu, :], pltpu.roll(h, 126 - 4 * k, 1), lane))

            dr = [combine(*[S[j, x + 2, z0 + o:z0 + o + 8, :] for o in (6, 7, 9, 10)]) for j in range(6)]
            acc = (
                d_x(0) + sx * dr[0] + d_y(1, halos[0]) + sy * dr[1] + st * dr[2],
                d_x(1) + sx * dr[1] + d_y(3, halos[1]) + sy * dr[3] + st * dr[4],
                d_x(2) + sx * dr[2] + d_y(4, halos[2]) + sy * dr[4] + st * dr[5],
            )
            moved = []
            for c in range(3):
                u, p = U[cur, c, x + 2, zu, :], U[old, c, x + 2, zu, :]
                fol = (u + u - p) + b * acc[c]
                moved.append((fol, fol - p))
            return moved

        def put(x, zb, value, _):
            z0 = zb * 8
            for c in range(3):
                U[old, c, x + 2, z0 + 8:z0 + 16, :] = value[c][0]
                RATE[c, x, z0:z0 + 8, :] = value[c][1]
            return [v[0] for v in value]

        return over_planes(part, 2, cell, put)

    def step(n, carry):
        cur = lax.rem(n, 2)
        more = n < STEPS - 1
        packed = stress(cur, INNER, y_wait(PU, HU, 0, INNER))
        y_send(packed, PS, HS, 1, INNER)
        stress(cur, OFF, y_wait(PU, HU, 0, OFF))

        @pl.when(has_off)
        def _():
            partial_copy(cur).start()

        halos = y_wait(PU, HU, 0, ON)
        u_wait(cur, ON)
        packed = stress(cur, ON, halos)
        s_copy().start()
        y_send(packed, PS, HS, 1, ON)

        @pl.when(n > 0)
        def _():
            sketch(n - 1, True)

        u_wait(cur, OFF)
        packed = complete(cur)
        y_send(packed, PS, HS, 1, OFF)

        packed = forces(cur, INNER, y_wait(PS, HS, 1, INNER))

        @pl.when(more)
        def _():
            y_send(packed, PU, HU, 0, INNER)

        sketch(n, False)
        for part in (ON, OFF):
            halos = y_wait(PS, HS, 1, part)
            if part == ON:
                s_copy().wait()
            else:
                @pl.when(has_off)
                def _():
                    partial_copy(cur).wait()

                @pl.when(has_off & (n == 0))
                def _():
                    moduli_copy().wait()

                complete_beyond(cur, cur)
            packed = forces(cur, part, halos)

            @pl.when(more)
            def _():
                u_start(1 - cur, part)
                y_send(packed, PU, HU, 0, part)

        return carry

    lax.fori_loop(0, STEPS, step, 0)
    sketch(STEPS - 1, True)
    for g in range(8):
        for xh in range(4):
            PIECES[g, 6 * xh:6 * xh + 6, :] = SK[xh * 48 + 6 * g:xh * 48 + 6 * g + 6, :]

    def piece(g, slot):
        return pltpu.make_async_remote_copy(
            src_ref=PIECES.at[g], dst_ref=RB.at[slot], send_sem=s0.at[g], recv_sem=r0.at[slot],
            device_id=(gx, g), device_id_type=MESH)

    @pl.loop(0, 7)
    def _(i):
        piece(lax.rem(gy + far_first(i, 4), 8), gy).start()

    RB[gy] = PIECES[gy]

    final = STEPS % 2

    @pl.loop(0, 8)
    def _(x):
        for zb in range(4):
            for c in range(3):
                out[c, pl.ds(zb * 64 + x, 8, stride=8), :] = U[final, c, x + 2, zb * 8 + 8:zb * 8 + 16, :]

    @pl.loop(1, 8)
    def _(d):
        g = lax.rem(gy + d, 8)
        piece(g, g).wait()

    total = RB[0]
    for g in range(1, 8):
        total = total + RB[g]
    tall[...] = total
    hi, mid, lo = (term.astype(F32) for term in split(total))
    GL[...] = lax.dot_general(
        jnp.concatenate([hi, hi, mid, hi, mid, lo], axis=0).astype(BF16),
        jnp.concatenate([hi, mid, hi, lo, mid, hi], axis=0).astype(BF16),
        (((0,), (0,)), ((), ())), preferred_element_type=F32).reshape(16, 8, 128)

    def group(dev, me, src, dst, send, recv):
        def make(slot, peer):
            return pltpu.make_async_remote_copy(
                src_ref=src(peer), dst_ref=dst.at[slot], send_sem=send.at[peer], recv_sem=recv.at[slot],
                device_id=dev(peer), device_id_type=MESH)

        @pl.loop(0, 15)
        def _(i):
            make(me, lax.rem(me + far_first(i, 8), 16)).start()

        def finish():
            @pl.loop(1, 16)
            def _(d):
                peer = lax.rem(me + d, 16)
                make(peer, peer).wait()

        return finish

    def summed(ref):
        parts = [ref[i] for i in range(16)]
        while len(parts) > 1:
            parts = [parts[i] + parts[i + 1] for i in range(0, len(parts), 2)]
        return parts[0]

    finish = group(b_dev, b_me, lambda p: GL.at[p], RA, s1, r1)
    RA[b_me] = GL[b_me]
    finish()
    part = summed(RA)
    PA[...] = part
    finish = group(a_dev, a_me, lambda p: PA, RBB, s2, r2)
    RBB[a_me] = part
    finish()
    whole = summed(RBB)
    GS[...] = whole
    finish = group(b_dev, b_me, lambda p: GS, gram, s3, r3)
    gram[b_me] = whole
    finish()


def wave(disp, vel, slopes, stretch, moduli, buoy, probes):
    sem = pltpu.SemaphoreType.DMA
    buffers = [
        (3, 256, 128), (3, 256, 128), (2, 256, 128), (256, 128), (2, 256, 128), (256, 128), (STEPS, 64, 128),
        (128, 128), (2, 3, 12, ZP, 128), (6, 12, ZP, 128), (6, 8, 32, 128), (3, 8, 32, 128), (192, 128),
        (3, 3, 8, 128), (3, 3, 8, 128), (3, 2, 3, 8, 128), (3, 2, 3, 8, 128),
        (3, 2, 32, 128), (2, 3, 2, 32, 128), (2, 2, 32, 128), (8, 24, 128), (8, 24, 128), (16, 8, 128), (16, 8, 128), (8, 128), (16, 8, 128), (8, 128),
    ]
    sems = [(7,), (4,), (4,), (), (), (2, 3, 2), (2, 3, 2), (2,), (2,), (2,)] + [(8,)] * 2 + [(16,)] * 6
    return pl.pallas_call(
        wave_kernel,
        name="wave",
        out_shape=(
            jax.ShapeDtypeStruct((24, 128), F32),
            jax.ShapeDtypeStruct((16, 8, 128), F32),
            jax.ShapeDtypeStruct((3, 256, 128), F32),
        ),
        in_specs=[pl.BlockSpec(memory_space=pltpu.MemorySpace.HBM)] * 7,
        out_specs=[pl.BlockSpec(memory_space=VMEM)] * 3,
        scratch_shapes=[pltpu.VMEM(shape, F32) for shape in buffers[:7]]
        + [pltpu.VMEM((STEPS, 768, 128), BF16)]
        + [pltpu.VMEM(shape, F32) for shape in buffers[7:]] + [sem(shape) for shape in sems],
        compiler_params=pltpu.CompilerParams(
            collective_id=0, has_side_effects=True, vmem_limit_bytes=VMEM_LIMIT),
    )(*[pltpu.with_memory_space_constraint(x, pltpu.MemorySpace.HBM)
        for x in (disp, vel, slopes, stretch, moduli, buoy, probes)])


def factor_kernel(scale, gram, tall, disp, basis, factor, out, sem):
    leave = pltpu.make_async_copy(disp, out, sem)
    leave.start()
    lane = lanes()
    sub = lax.broadcasted_iota(jnp.int32, (8, 128), 0)
    a = [gram[i] for i in range(16)]
    for b in range(16):
        j0 = 8 * b
        inside = (lane >= j0) & (lane < j0 + 8)
        cols = [jnp.broadcast_to(a[b][:, j0 + t:j0 + t + 1], (8, 128)) for t in range(8)]
        d = [[jnp.broadcast_to(cols[t][s:s + 1, :], (8, 128)) if t >= s else None for t in range(8)]
             for s in range(8)]
        inv = [None] * 8
        m = [[None] * 8 for _ in range(8)]
        for s in range(8):
            inv[s] = 1.0 / d[s][s]
            for t in range(s + 1, 8):
                m[s][t] = d[s][t] * inv[s]
                for q in range(t, 8):
                    d[t][q] = d[t][q] - m[s][t] * d[s][q]
        unit = [None] * 8
        fresh = a[b]
        for t in range(8):
            x = jnp.broadcast_to(a[b][t:t + 1, :], (8, 128))
            for s in range(t):
                x = jnp.where(lane == j0 + s, 0.0, x) - m[s][t] * unit[s]
            unit[t] = jnp.where(lane == j0 + t, 1.0, x)
            fresh = jnp.where(sub == t, x, fresh)
        a[b] = fresh
        below = [jnp.where((lane > j0 + t) & inside, 0.0, unit[t]) for t in range(8)]
        for i in range(b + 1, 16):
            c = [jnp.broadcast_to(a[i][:, j0 + s:j0 + s + 1], (8, 128)) for s in range(8)]
            x = jnp.where(inside, 0.0, a[i])
            for s in range(8):
                ms = c[s] * inv[s]
                for t in range(s + 1, 8):
                    c[t] = c[t] - ms * d[s][t]
                x = x - ms * below[s]
            a[i] = x
    inverse = []
    for i in range(16):
        rows = sub + 8 * i
        diag = jnp.sum(jnp.where(lane == rows, a[i], 0.0), axis=1, keepdims=True)
        root = lax.rsqrt(diag)
        factor[8 * i:8 * i + 8, :] = jnp.where(lane >= rows, a[i], 0.0) * root
        inverse.append(jnp.where(lane == rows, 1.0, jnp.where(lane < rows, a[i], 0.0)) * (root * scale))
    inverse = jnp.concatenate(inverse, axis=0)
    q = lax.dot_general(
        tall[...], inverse, (((1,), (1,)), ((), ())), precision=HIGH, preferred_element_type=F32)
    for xh in range(4):
        for r in range(6):
            basis[r, xh:xh + 1, :] = q[6 * xh + r:6 * xh + r + 1, :]
    leave.wait()


def finish(gram, tall, disp, scale):
    return pl.pallas_call(
        functools.partial(factor_kernel, scale),
        name="factor",
        out_shape=(
            jax.ShapeDtypeStruct((6, 4, 128), F32),
            jax.ShapeDtypeStruct((128, 128), F32),
            jax.ShapeDtypeStruct((3, 256, 128), F32),
        ),
        in_specs=[pl.BlockSpec(memory_space=VMEM)] * 3,
        out_specs=[pl.BlockSpec(memory_space=VMEM)] * 2 + [pl.BlockSpec(memory_space=pltpu.MemorySpace.HBM)],
        scratch_shapes=[pltpu.SemaphoreType.DMA],
        compiler_params=pltpu.CompilerParams(vmem_limit_bytes=VMEM_LIMIT),
    )(gram, tall, disp)


def shards(displacement, velocity, slopes, stretch, moduli, buoyancy, probes):
    tall, gram, moved = wave(
        displacement.reshape(3, 256, 128), velocity.reshape(3, 256, 128), slopes.reshape(2, 256, 128),
        stretch.reshape(256, 128), moduli.reshape(2, 256, 128), buoyancy.reshape(256, 128), probes)
    rows = tall.shape[0] * lax.axis_size("gx") * lax.axis_size("gy")
    basis, factor, moved = finish(gram, tall, moved, math.sqrt(rows))
    return moved.reshape(3, 32, 8, 128), jnp.transpose(basis, (1, 0, 2)), factor


def solution(mesh):
    in_specs = (
        P(None, None, "gx", "gy"),
        P(None, None, "gx", "gy"),
        P(None, None, "gx", "gy"),
        P(None, "gx", "gy"),
        P(None, None, "gx", "gy"),
        P(None, "gx", "gy"),
        P(None, "gy", None),
    )
    out_specs = (P(None, None, "gx", "gy"), P("gx", "gy", None), P())
    return jax.shard_map(shards, mesh=mesh, in_specs=in_specs, out_specs=out_specs, check_vma=False)
```

```python
import functools
import math

import jax
import jax.numpy as jnp
from jax import lax
from jax.experimental import pallas as pl
from jax.experimental.pallas import tpu as pltpu
from jax.sharding import PartitionSpec as P

STEPS = 4
DT = 0.12
MESH = pl.DeviceIdType.MESH
HIGH = lax.Precision.HIGHEST
F32 = jnp.float32
BF16 = jnp.bfloat16
ZP = 48
VMEM = pltpu.MemorySpace.VMEM
VMEM_LIMIT = 24 * 1024 * 1024


def lanes():
    return lax.broadcasted_iota(jnp.int32, (8, 128), 1)


def shifted(f, h, lane):
    m2 = pltpu.roll(jnp.where(lane >= 126, h, f), 2, 1)
    m1 = pltpu.roll(jnp.where(lane >= 127, h, f), 1, 1)
    p1 = pltpu.roll(jnp.where(lane < 1, h, f), 127, 1)
    p2 = pltpu.roll(jnp.where(lane < 2, h, f), 126, 1)
    return m2, m1, p1, p2


def combine(m2, m1, p1, p2):
    return (m2 - p2) + 8.0 * (p1 - m1)


def split(x):
    hi = x.astype(BF16)
    rest = x - hi.astype(F32)
    mid = rest.astype(BF16)
    return hi, mid, (rest - mid.astype(F32)).astype(BF16)


def wave_kernel(
    disp_hbm, vel_hbm, slopes_hbm, stretch_hbm, moduli_hbm, buoy_hbm, probes_hbm,
    tall, gram, out,
    disp, vel, slopes, stretch, moduli, buoy, probes,
    PE, spread, U, S, MET, RATE, SK, PU, PS, HU, HS,
    SA, AH, MH, PIECES, RB, GL, RA, PA, RBB, GS,
    load_sem, send_u, recv_u, send_s, recv_s, send_y, recv_y, send_a, recv_a, moduli_sem,
    s0, r0, s1, r1, s2, r2, s3, r3,
):
    gx, gy = lax.axis_index("gx"), lax.axis_index("gy")
    nx, ny = lax.axis_size("gx"), lax.axis_size("gy")
    left = (lax.rem(gx + nx - 1, nx), gy)
    right = (lax.rem(gx + 1, nx), gy)
    down = (gx, lax.rem(gy + ny - 1, ny))
    up = (gx, lax.rem(gy + 1, ny))
    core = lax.rem(gx, 2)
    has_off = (gx > 0) & (gx < nx - 1)
    pair = gx - core
    a_me = gy * 2 + core
    b_me = gx // 2

    def a_dev(a):
        return (pair + lax.rem(a, 2), a // 2)

    def b_dev(b):
        return (b * 2 + core, gy)

    def far_first(i, half):
        step = (i + 1) // 2
        return half + step * (2 * lax.rem(i, 2) - 1)

    loads = [
        pltpu.make_async_copy(src, dst, load_sem.at[i])
        for i, (src, dst) in enumerate((
            (disp_hbm, disp), (vel_hbm, vel), (slopes_hbm, slopes), (stretch_hbm, stretch),
            (moduli_hbm, moduli), (buoy_hbm, buoy), (probes_hbm, probes)))
    ]
    for copy in loads:
        copy.start()

    barrier = pltpu.get_barrier_semaphore()

    @pl.loop(0, 15)
    def _(i):
        d = far_first(i, 8)
        pl.semaphore_signal(barrier, inc=1, device_id=a_dev(lax.rem(a_me + d, 16)), device_id_type=MESH)
        pl.semaphore_signal(barrier, inc=1, device_id=b_dev(lax.rem(b_me + d, 16)), device_id_type=MESH)

    for peer in (left, right):
        pl.semaphore_signal(barrier, inc=1, device_id=peer, device_id_type=MESH)

    lane = lanes()
    zero8 = jnp.zeros((8, 128), F32)
    low_part = (lane & 3) < 2

    @pl.loop(0, 12)
    def _(x):
        for s in range(2):
            for c in range(3):
                U[s, c, x, 0:8, :] = zero8
                U[s, c, x, 40:48, :] = zero8
        for c in range(6):
            S[c, x, 0:8, :] = zero8
            S[c, x, 40:48, :] = zero8

    @pl.when(jnp.logical_not(has_off))
    def _():
        for i in range(2):
            for z0 in range(0, 32, 8):
                for c in range(3):
                    AH[0, c, i, z0:z0 + 8, :] = zero8
                    AH[1, c, i, z0:z0 + 8, :] = zero8
                for c in range(2):
                    MH[c, i, z0:z0 + 8, :] = zero8

    def clear(x):
        for c in range(3):
            for z0 in range(8, 40, 8):
                U[0, c, x, z0:z0 + 8, :] = zero8
                U[1, c, x, z0:z0 + 8, :] = zero8
                S[c, x, z0:z0 + 8, :] = zero8

    @pl.when(gx == 0)
    def _():
        clear(0)
        clear(1)

    @pl.when(gx == nx - 1)
    def _():
        clear(10)
        clear(11)

    INNER, ON, OFF = 0, 1, 2

    def side(part):
        return core if part == OFF else 1 - core

    def u_copy(cur, part):
        s = side(part)
        index = 2 * cur + part - 1
        return pltpu.make_async_remote_copy(
            src_ref=U.at[cur, :, pl.ds(2 + 6 * s, 2), 8:40, :], dst_ref=U.at[cur, :, pl.ds(10 - 10 * s, 2), 8:40, :],
            send_sem=send_u.at[index], recv_sem=recv_u.at[index],
            device_id=(gx - 1 + 2 * s, gy), device_id_type=MESH)

    def s_copy():
        s = side(ON)
        return pltpu.make_async_remote_copy(
            src_ref=S.at[0:3, pl.ds(2 + 6 * s, 2), 8:40, :], dst_ref=S.at[0:3, pl.ds(10 - 10 * s, 2), 8:40, :],
            send_sem=send_s, recv_sem=recv_s, device_id=(gx - 1 + 2 * s, gy), device_id_type=MESH)

    def far_copy(src, dst, send, recv):
        return pltpu.make_async_remote_copy(
            src_ref=src, dst_ref=dst, send_sem=send, recv_sem=recv,
            device_id=(gx - 1 + 2 * turn, gy), device_id_type=MESH)

    def partial_copy(parity):
        return far_copy(SA, AH.at[parity], send_a.at[parity], recv_a.at[parity])

    def moduli_copy():
        return far_copy(MET.at[3:5, pl.ds(6 * turn, 2)], MH, moduli_sem.at[0], moduli_sem.at[1])

    def u_start(cur, part):
        if part == ON:
            u_copy(cur, part).start()
        else:
            @pl.when(has_off)
            def _():
                u_copy(cur, part).start()

    def u_wait(cur, part):
        if part == ON:
            u_copy(cur, part).wait()
        else:
            @pl.when(has_off)
            def _():
                u_copy(cur, part).wait()

    def y_copies(packed, halo, kind, part):
        return [
            pltpu.make_async_remote_copy(
                src_ref=packed.at[part], dst_ref=halo.at[part, 1 - d], send_sem=send_y.at[kind, part, d],
                recv_sem=recv_y.at[kind, part, d], device_id=peer, device_id_type=MESH)
            for d, peer in enumerate((down, up))
        ]

    def y_send(values, packed, halo, kind, part):
        for c in range(3):
            packed[part, c] = values[c]
        for copy in y_copies(packed, halo, kind, part):
            copy.start()

    def y_wait(packed, halo, kind, part):
        for copy in y_copies(packed, halo, kind, part):
            copy.wait()
        result = []
        for c in range(3):
            lo = jnp.where(gy == 0, zero8, halo[part, 0, c])
            hi = jnp.where(gy == ny - 1, zero8, halo[part, 1, c])
            result.append(jnp.where(low_part, lo, hi))
        return result

    turn = core
    outermost, second, inward = 7 * turn, 1 + 5 * turn, 1 - 2 * turn
    sign = jnp.where(turn == 0, 1.0, -1.0).astype(F32)

    def plane(part, i):
        if part == OFF:
            return second if i == 1 else outermost
        return i + 2 if part == INNER else i + 6 * side(part)

    loads[0].wait()

    def load_u(part):
        def body(i, carry):
            x = plane(part, i)
            packed = list(carry)
            for zb in range(4):
                rows = pl.ds(zb * 64 + x, 8, stride=8)
                k = x * 4 + zb
                for c in range(3):
                    d = disp[c, rows, :]
                    U[0, c, x + 2, zb * 8 + 8:zb * 8 + 16, :] = d
                    packed[c] = jnp.where((lane >> 2) == k, pltpu.roll(d, 4 * k + 2, 1), packed[c])
            return tuple(packed)

        if part == OFF:
            return body(1, body(0, (zero8,) * 3))
        return lax.fori_loop(0, 4 if part == INNER else 2, body, (zero8,) * 3)

    first = [load_u(INNER), load_u(ON), load_u(OFF)]
    pl.semaphore_wait(barrier, 32)
    for part in (OFF, ON):
        u_start(0, part)
    for part in (INNER, OFF, ON):
        y_send(first[part], PU, HU, 0, part)

    for copy in loads[1:]:
        copy.wait()

    @pl.loop(0, 8)
    def _(x):
        for zb in range(4):
            rows = pl.ds(zb * 64 + x, 8, stride=8)
            zs = slice(zb * 8, zb * 8 + 8)
            zu = slice(zb * 8 + 8, zb * 8 + 16)
            MET[0, x, zs, :] = slopes[0, rows, :]
            MET[1, x, zs, :] = slopes[1, rows, :]
            MET[2, x, zs, :] = stretch[rows, :]
            MET[3, x, zs, :] = moduli[0, rows, :] * (1.0 / 12.0)
            MET[4, x, zs, :] = moduli[1, rows, :] * (1.0 / 12.0)
            MET[5, x, zs, :] = buoy[rows, :] * (DT * DT / 12.0)
            for c in range(3):
                U[1, c, x + 2, zu, :] = U[0, c, x + 2, zu, :] - DT * vel[c, rows, :]

    @pl.when(has_off)
    def _():
        moduli_copy().start()

    spread[...] = jnp.zeros((128, 128), F32)
    for n in range(STEPS):
        spread[pl.ds(0, 64, stride=2), :] = probes[n] * (1.0 / (2.0 * DT))
        hi, mid, lo = split(spread[...])
        for i, term in enumerate((hi, mid, hi, lo, mid, hi)):
            PE[n, 128 * i:128 * i + 128, :] = term
    SK[...] = jnp.zeros_like(SK)

    def sketch(n, outer):
        where = (0, 3) if outer else (1, 2)
        hi, mid, lo = split(jnp.concatenate(
            [RATE[c, 2 * xh, pl.ds(0, 16, stride=2), :] for xh in where for c in range(3)], axis=0))
        term = jnp.dot(
            jnp.concatenate([hi, hi, mid, hi, mid, lo], axis=1), PE[n], preferred_element_type=F32)
        for i, xh in enumerate(where):
            SK[48 * xh:48 * xh + 48, :] += term[48 * i:48 * i + 48, :]

    def over_planes(part, planes, cell, put):
        def body(i, packed):
            cells = [(plane(part, i * planes + j), zb, j) for j in range(planes) for zb in range(4)]
            values = [cell(*where) for where in cells]
            packed = list(packed)
            for (x, zb, j), value in zip(cells, values):
                edge = put(x, zb, value, j)
                if edge is None:
                    continue
                k = x * 4 + zb
                here = (lane >> 2) == k
                for c in range(3):
                    packed[c] = jnp.where(here, pltpu.roll(edge[c], 4 * k + 2, 1), packed[c])
            return tuple(packed)

        if part != INNER:
            return body(0, (zero8,) * 3)
        return lax.fori_loop(0, 4 // planes, body, (zero8,) * 3)

    def stress(cur, part, halos):
        def d_x(c, x, zu, j):
            if part != OFF:
                return combine(U[cur, c, x, zu, :], U[cur, c, x + 1, zu, :],
                               U[cur, c, x + 3, zu, :], U[cur, c, x + 4, zu, :])
            ahead, second_ahead = U[cur, c, x + 2 + inward, zu, :], U[cur, c, x + 2 + 2 * inward, zu, :]
            if j == 1:
                ahead = ahead - U[cur, c, x + 2 - inward, zu, :]
            return sign * (8.0 * ahead - second_ahead)

        def cell(x, zb, j):
            z0 = zb * 8
            zs, zu = slice(z0, z0 + 8), slice(z0 + 8, z0 + 16)
            k = x * 4 + zb
            sx, sy, st = MET[0, x, zs, :], MET[1, x, zs, :], MET[2, x, zs, :]
            lam, mu = MET[3, x, zs, :], MET[4, x, zs, :]
            g = []
            for c in range(3):
                f = U[cur, c, x + 2, zu, :]
                dx = d_x(c, x, zu, j)
                dr = combine(*[U[cur, c, x + 2, z0 + o:z0 + o + 8, :] for o in (6, 7, 9, 10)])
                dy = combine(*shifted(f, pltpu.roll(halos[c], 126 - 4 * k, 1), lane))
                g.append((dx + sx * dr, dy + sy * dr, st * dr))
            pressure = lam * (g[0][0] + g[1][1] + g[2][2])
            mu2 = mu + mu
            return (pressure + mu2 * g[0][0], mu * (g[0][1] + g[1][0]), mu * (g[0][2] + g[2][0]),
                    pressure + mu2 * g[1][1], mu * (g[1][2] + g[2][1]), pressure + mu2 * g[2][2])

        def put(x, zb, value, j):
            for i in range(6):
                S[i, x + 2, zb * 8 + 8:zb * 8 + 16, :] = value[i]
            if part == OFF:
                for i in range(3):
                    SA[i, x - 6 * turn, zb * 8:zb * 8 + 8, :] = value[i]
                return None
            return value[1], value[3], value[4]

        return over_planes(part, 2, cell, put)

    def added(first, near, j):
        return first - 8.0 * near if j == 0 else near

    def complete(cur):
        def cell(x, zb, j):
            zs, zu = slice(zb * 8, zb * 8 + 8), slice(zb * 8 + 8, zb * 8 + 16)
            lam, mu = MET[3, x, zs, :], MET[4, x, zs, :]
            at = outermost + 2 - inward
            dx = [sign * added(U[cur, c, at - inward, zu, :], U[cur, c, at, zu, :], j) for c in range(3)]
            side_pressure = lam * dx[0]
            return (S[0, x + 2, zu, :] + (side_pressure + (mu + mu) * dx[0]), S[1, x + 2, zu, :] + mu * dx[1],
                    S[2, x + 2, zu, :] + mu * dx[2], S[3, x + 2, zu, :] + side_pressure,
                    S[5, x + 2, zu, :] + side_pressure, S[4, x + 2, zu, :])

        def put(x, zb, value, j):
            zu = slice(zb * 8 + 8, zb * 8 + 16)
            for i, row in enumerate((0, 1, 2, 3, 5)):
                S[row, x + 2, zu, :] = value[i]
            return value[1], value[3], value[5]

        return over_planes(OFF, 2, cell, put)

    def complete_beyond(cur, parity):
        for j in range(2):
            at = 1 - turn if j == 0 else turn
            for zb in range(4):
                zs, zu = slice(zb * 8, zb * 8 + 8), slice(zb * 8 + 8, zb * 8 + 16)
                lam, mu = MH[0, at, zs, :], MH[1, at, zs, :]
                dx = [-sign * added(U[cur, c, second + 2, zu, :], U[cur, c, outermost + 2, zu, :], j)
                      for c in range(3)]
                scale = (lam + (mu + mu), mu, mu)
                for c in range(3):
                    S[c, outermost + 2 - (1 + j) * inward, zu, :] = AH[parity, c, at, zs, :] + scale[c] * dx[c]

    def forces(cur, part, halos):
        old = 1 - cur

        def cell(x, zb, _):
            z0 = zb * 8
            zs, zu = slice(z0, z0 + 8), slice(z0 + 8, z0 + 16)
            k = x * 4 + zb
            sx, sy, st, b = (MET[j, x, zs, :] for j in (0, 1, 2, 5))

            def d_x(j):
                return combine(S[j, x, zu, :], S[j, x + 1, zu, :], S[j, x + 3, zu, :], S[j, x + 4, zu, :])

            def d_y(j, h):
                return combine(*shifted(S[j, x + 2, zu, :], pltpu.roll(h, 126 - 4 * k, 1), lane))

            dr = [combine(*[S[j, x + 2, z0 + o:z0 + o + 8, :] for o in (6, 7, 9, 10)]) for j in range(6)]
            acc = (
                d_x(0) + sx * dr[0] + d_y(1, halos[0]) + sy * dr[1] + st * dr[2],
                d_x(1) + sx * dr[1] + d_y(3, halos[1]) + sy * dr[3] + st * dr[4],
                d_x(2) + sx * dr[2] + d_y(4, halos[2]) + sy * dr[4] + st * dr[5],
            )
            moved = []
            for c in range(3):
                u, p = U[cur, c, x + 2, zu, :], U[old, c, x + 2, zu, :]
                fol = (u + u - p) + b * acc[c]
                moved.append((fol, fol - p))
            return moved

        def put(x, zb, value, _):
            z0 = zb * 8
            for c in range(3):
                U[old, c, x + 2, z0 + 8:z0 + 16, :] = value[c][0]
                RATE[c, x, z0:z0 + 8, :] = value[c][1]
            return [v[0] for v in value]

        return over_planes(part, 2, cell, put)

    def step(n, carry):
        cur = lax.rem(n, 2)
        more = n < STEPS - 1
        packed = stress(cur, INNER, y_wait(PU, HU, 0, INNER))
        y_send(packed, PS, HS, 1, INNER)
        stress(cur, OFF, y_wait(PU, HU, 0, OFF))

        @pl.when(has_off)
        def _():
            partial_copy(cur).start()

        halos = y_wait(PU, HU, 0, ON)
        u_wait(cur, ON)
        packed = stress(cur, ON, halos)
        s_copy().start()
        y_send(packed, PS, HS, 1, ON)

        @pl.when(n > 0)
        def _():
            sketch(n - 1, True)

        u_wait(cur, OFF)
        packed = complete(cur)
        y_send(packed, PS, HS, 1, OFF)

        packed = forces(cur, INNER, y_wait(PS, HS, 1, INNER))

        @pl.when(more)
        def _():
            y_send(packed, PU, HU, 0, INNER)

        sketch(n, False)
        moved = []
        for part in (ON, OFF):
            halos = y_wait(PS, HS, 1, part)
            if part == ON:
                s_copy().wait()
            else:
                @pl.when(has_off)
                def _():
                    partial_copy(cur).wait()

                @pl.when(has_off & (n == 0))
                def _():
                    moduli_copy().wait()

                complete_beyond(cur, cur)
            packed = forces(cur, part, halos)

            moved.append(packed)

        @pl.when(more)
        def _():
            for part in (OFF, ON):
                y_send(moved[part - 1], PU, HU, 0, part)
                u_start(1 - cur, part)

        return carry

    lax.fori_loop(0, STEPS, step, 0)
    sketch(STEPS - 1, True)
    for g in range(8):
        for xh in range(4):
            PIECES[g, 6 * xh:6 * xh + 6, :] = SK[xh * 48 + 6 * g:xh * 48 + 6 * g + 6, :]

    def piece(g, slot):
        return pltpu.make_async_remote_copy(
            src_ref=PIECES.at[g], dst_ref=RB.at[slot], send_sem=s0.at[g], recv_sem=r0.at[slot],
            device_id=(gx, g), device_id_type=MESH)

    @pl.loop(0, 7)
    def _(i):
        piece(lax.rem(gy + far_first(i, 4), 8), gy).start()

    RB[gy] = PIECES[gy]

    final = STEPS % 2

    @pl.loop(0, 8)
    def _(x):
        for zb in range(4):
            for c in range(3):
                out[c, pl.ds(zb * 64 + x, 8, stride=8), :] = U[final, c, x + 2, zb * 8 + 8:zb * 8 + 16, :]

    @pl.loop(1, 8)
    def _(d):
        g = lax.rem(gy + d, 8)
        piece(g, g).wait()

    total = RB[0]
    for g in range(1, 8):
        total = total + RB[g]
    tall[...] = total
    hi, mid, lo = (term.astype(F32) for term in split(total))
    GL[...] = lax.dot_general(
        jnp.concatenate([hi, hi, mid, hi, mid, lo], axis=0).astype(BF16),
        jnp.concatenate([hi, mid, hi, lo, mid, hi], axis=0).astype(BF16),
        (((0,), (0,)), ((), ())), preferred_element_type=F32).reshape(16, 8, 128)

    def group(dev, me, src, dst, send, recv):
        def make(slot, peer):
            return pltpu.make_async_remote_copy(
                src_ref=src(peer), dst_ref=dst.at[slot], send_sem=send.at[peer], recv_sem=recv.at[slot],
                device_id=dev(peer), device_id_type=MESH)

        @pl.loop(0, 15, unroll=5)
        def _(i):
            make(me, lax.rem(me + far_first(i, 8), 16)).start()

        def finish():
            @pl.loop(1, 16, unroll=5)
            def _(d):
                peer = lax.rem(me + d, 16)
                make(peer, peer).wait_recv()

        def sent():
            @pl.loop(1, 16, unroll=5)
            def _(d):
                peer = lax.rem(me + d, 16)
                make(peer, peer).wait_send()

        return finish, sent

    def summed(ref):
        parts = [ref[i] for i in range(16)]
        while len(parts) > 1:
            parts = [parts[i] + parts[i + 1] for i in range(0, len(parts), 2)]
        return parts[0]

    finish, sent_a = group(b_dev, b_me, lambda p: GL.at[p], RA, s1, r1)
    RA[b_me] = GL[b_me]
    finish()
    part = summed(RA)
    PA[...] = part
    finish, sent_b = group(a_dev, a_me, lambda p: PA, RBB, s2, r2)
    RBB[a_me] = part
    finish()
    whole = summed(RBB)
    GS[...] = whole
    finish, sent_c = group(b_dev, b_me, lambda p: GS, gram, s3, r3)
    gram[b_me] = whole
    sent_a()
    sent_b()
    finish()
    sent_c()


def wave(disp, vel, slopes, stretch, moduli, buoy, probes):
    sem = pltpu.SemaphoreType.DMA
    buffers = [
        (3, 256, 128), (3, 256, 128), (2, 256, 128), (256, 128), (2, 256, 128), (256, 128), (STEPS, 64, 128),
        (128, 128), (2, 3, 12, ZP, 128), (6, 12, ZP, 128), (6, 8, 32, 128), (3, 8, 32, 128), (192, 128),
        (3, 3, 8, 128), (3, 3, 8, 128), (3, 2, 3, 8, 128), (3, 2, 3, 8, 128),
        (3, 2, 32, 128), (2, 3, 2, 32, 128), (2, 2, 32, 128), (8, 24, 128), (8, 24, 128), (16, 8, 128), (16, 8, 128), (8, 128), (16, 8, 128), (8, 128),
    ]
    sems = [(7,), (4,), (4,), (), (), (2, 3, 2), (2, 3, 2), (2,), (2,), (2,)] + [(8,)] * 2 + [(16,)] * 6
    return pl.pallas_call(
        wave_kernel,
        name="wave",
        out_shape=(
            jax.ShapeDtypeStruct((24, 128), F32),
            jax.ShapeDtypeStruct((16, 8, 128), F32),
            jax.ShapeDtypeStruct((3, 256, 128), F32),
        ),
        in_specs=[pl.BlockSpec(memory_space=pltpu.MemorySpace.HBM)] * 7,
        out_specs=[pl.BlockSpec(memory_space=VMEM)] * 3,
        scratch_shapes=[pltpu.VMEM(shape, F32) for shape in buffers[:7]]
        + [pltpu.VMEM((STEPS, 768, 128), BF16)]
        + [pltpu.VMEM(shape, F32) for shape in buffers[7:]] + [sem(shape) for shape in sems],
        compiler_params=pltpu.CompilerParams(
            collective_id=0, has_side_effects=True, vmem_limit_bytes=VMEM_LIMIT),
    )(*[pltpu.with_memory_space_constraint(x, pltpu.MemorySpace.HBM)
        for x in (disp, vel, slopes, stretch, moduli, buoy, probes)])


def factor_kernel(scale, gram, tall, disp, basis, factor, out, sem):
    leave = pltpu.make_async_copy(disp, out, sem)
    leave.start()
    lane = lanes()
    sub = lax.broadcasted_iota(jnp.int32, (8, 128), 0)
    a = [gram[i] for i in range(16)]
    for b in range(16):
        j0 = 8 * b
        inside = (lane >= j0) & (lane < j0 + 8)
        cols = [jnp.broadcast_to(a[b][:, j0 + t:j0 + t + 1], (8, 128)) for t in range(8)]
        d = [[jnp.broadcast_to(cols[t][s:s + 1, :], (8, 128)) if t >= s else None for t in range(8)]
             for s in range(8)]
        inv = [None] * 8
        m = [[None] * 8 for _ in range(8)]
        for s in range(8):
            inv[s] = 1.0 / d[s][s]
            for t in range(s + 1, 8):
                m[s][t] = d[s][t] * inv[s]
                for q in range(t, 8):
                    d[t][q] = d[t][q] - m[s][t] * d[s][q]
        unit = [None] * 8
        fresh = a[b]
        for t in range(8):
            x = jnp.broadcast_to(a[b][t:t + 1, :], (8, 128))
            for s in range(t):
                x = jnp.where(lane == j0 + s, 0.0, x) - m[s][t] * unit[s]
            unit[t] = jnp.where(lane == j0 + t, 1.0, x)
            fresh = jnp.where(sub == t, x, fresh)
        a[b] = fresh
        below = [jnp.where((lane > j0 + t) & inside, 0.0, unit[t]) for t in range(8)]
        for i in range(b + 1, 16):
            c = [jnp.broadcast_to(a[i][:, j0 + s:j0 + s + 1], (8, 128)) for s in range(8)]
            x = jnp.where(inside, 0.0, a[i])
            for s in range(8):
                ms = c[s] * inv[s]
                for t in range(s + 1, 8):
                    c[t] = c[t] - ms * d[s][t]
                x = x - ms * below[s]
            a[i] = x
    inverse = []
    for i in range(16):
        rows = sub + 8 * i
        diag = jnp.sum(jnp.where(lane == rows, a[i], 0.0), axis=1, keepdims=True)
        root = lax.rsqrt(diag)
        factor[8 * i:8 * i + 8, :] = jnp.where(lane >= rows, a[i], 0.0) * root
        inverse.append(jnp.where(lane == rows, 1.0, jnp.where(lane < rows, a[i], 0.0)) * (root * scale))
    inverse = jnp.concatenate(inverse, axis=0)
    q = lax.dot_general(
        tall[...], inverse, (((1,), (1,)), ((), ())), precision=HIGH, preferred_element_type=F32)
    for xh in range(4):
        for r in range(6):
            basis[r, xh:xh + 1, :] = q[6 * xh + r:6 * xh + r + 1, :]
    leave.wait()


def finish(gram, tall, disp, scale):
    return pl.pallas_call(
        functools.partial(factor_kernel, scale),
        name="factor",
        out_shape=(
            jax.ShapeDtypeStruct((6, 4, 128), F32),
            jax.ShapeDtypeStruct((128, 128), F32),
            jax.ShapeDtypeStruct((3, 256, 128), F32),
        ),
        in_specs=[pl.BlockSpec(memory_space=VMEM)] * 3,
        out_specs=[pl.BlockSpec(memory_space=VMEM)] * 2 + [pl.BlockSpec(memory_space=pltpu.MemorySpace.HBM)],
        scratch_shapes=[pltpu.SemaphoreType.DMA],
        compiler_params=pltpu.CompilerParams(vmem_limit_bytes=VMEM_LIMIT),
    )(gram, tall, disp)


def shards(displacement, velocity, slopes, stretch, moduli, buoyancy, probes):
    tall, gram, moved = wave(
        displacement.reshape(3, 256, 128), velocity.reshape(3, 256, 128), slopes.reshape(2, 256, 128),
        stretch.reshape(256, 128), moduli.reshape(2, 256, 128), buoyancy.reshape(256, 128), probes)
    rows = tall.shape[0] * lax.axis_size("gx") * lax.axis_size("gy")
    basis, factor, moved = finish(gram, tall, moved, math.sqrt(rows))
    return moved.reshape(3, 32, 8, 128), jnp.transpose(basis, (1, 0, 2)), factor


def solution(mesh):
    in_specs = (
        P(None, None, "gx", "gy"),
        P(None, None, "gx", "gy"),
        P(None, None, "gx", "gy"),
        P(None, "gx", "gy"),
        P(None, None, "gx", "gy"),
        P(None, "gx", "gy"),
        P(None, "gy", None),
    )
    out_specs = (P(None, None, "gx", "gy"), P("gx", "gy", None), P())
    return jax.shard_map(shards, mesh=mesh, in_specs=in_specs, out_specs=out_specs, check_vma=False)
```

```python
import functools
import math

import jax
import jax.numpy as jnp
from jax import lax
from jax.experimental import pallas as pl
from jax.experimental.pallas import tpu as pltpu
from jax.sharding import PartitionSpec as P

STEPS = 4
DT = 0.12
MESH = pl.DeviceIdType.MESH
HIGH = lax.Precision.HIGHEST
F32 = jnp.float32
BF16 = jnp.bfloat16
ZP = 48
VMEM = pltpu.MemorySpace.VMEM
VMEM_LIMIT = 24 * 1024 * 1024


def lanes():
    return lax.broadcasted_iota(jnp.int32, (8, 128), 1)


def shifted(f, h, lane):
    m2 = pltpu.roll(jnp.where(lane >= 126, h, f), 2, 1)
    m1 = pltpu.roll(jnp.where(lane >= 127, h, f), 1, 1)
    p1 = pltpu.roll(jnp.where(lane < 1, h, f), 127, 1)
    p2 = pltpu.roll(jnp.where(lane < 2, h, f), 126, 1)
    return m2, m1, p1, p2


def combine(m2, m1, p1, p2):
    return (m2 - p2) + 8.0 * (p1 - m1)


def split(x):
    hi = x.astype(BF16)
    rest = x - hi.astype(F32)
    mid = rest.astype(BF16)
    return hi, mid, (rest - mid.astype(F32)).astype(BF16)


def wave_kernel(
    disp_hbm, vel_hbm, slopes_hbm, stretch_hbm, moduli_hbm, buoy_hbm, probes_hbm,
    tall, gram, out,
    disp, vel, slopes, stretch, moduli, buoy, probes,
    PE, spread, U, S, MET, RATE, SK, PU, PS, HU, HS,
    SA, AH, MH, PIECES, RB, GL, RA, PA, RBB, GS,
    load_sem, send_u, recv_u, send_s, recv_s, send_y, recv_y, send_a, recv_a, moduli_sem,
    s0, r0, s1, r1, s2, r2, s3, r3,
):
    gx, gy = lax.axis_index("gx"), lax.axis_index("gy")
    nx, ny = lax.axis_size("gx"), lax.axis_size("gy")
    left = (lax.rem(gx + nx - 1, nx), gy)
    right = (lax.rem(gx + 1, nx), gy)
    down = (gx, lax.rem(gy + ny - 1, ny))
    up = (gx, lax.rem(gy + 1, ny))
    core = lax.rem(gx, 2)
    has_off = (gx > 0) & (gx < nx - 1)
    pair = gx - core
    a_me = gy * 2 + core
    b_me = gx // 2

    def a_dev(a):
        return (pair + lax.rem(a, 2), a // 2)

    def b_dev(b):
        return (b * 2 + core, gy)

    def far_first(i, half):
        step = (i + 1) // 2
        return half + step * (2 * lax.rem(i, 2) - 1)

    loads = [
        pltpu.make_async_copy(src, dst, load_sem.at[i])
        for i, (src, dst) in enumerate((
            (disp_hbm, disp), (vel_hbm, vel), (slopes_hbm, slopes), (stretch_hbm, stretch),
            (moduli_hbm, moduli), (buoy_hbm, buoy), (probes_hbm, probes)))
    ]
    for copy in loads:
        copy.start()

    barrier = pltpu.get_barrier_semaphore()

    @pl.loop(0, 15, unroll=5)
    def _(i):
        d = far_first(i, 8)
        pl.semaphore_signal(barrier, inc=1, device_id=a_dev(lax.rem(a_me + d, 16)), device_id_type=MESH)
        pl.semaphore_signal(barrier, inc=1, device_id=b_dev(lax.rem(b_me + d, 16)), device_id_type=MESH)

    for peer in (left, right):
        pl.semaphore_signal(barrier, inc=1, device_id=peer, device_id_type=MESH)

    lane = lanes()
    zero8 = jnp.zeros((8, 128), F32)
    low_part = (lane & 3) < 2

    @pl.loop(0, 12)
    def _(x):
        for s in range(2):
            for c in range(3):
                U[s, c, x, 0:8, :] = zero8
                U[s, c, x, 40:48, :] = zero8
        for c in range(6):
            S[c, x, 0:8, :] = zero8
            S[c, x, 40:48, :] = zero8

    @pl.when(jnp.logical_not(has_off))
    def _():
        for i in range(2):
            for z0 in range(0, 32, 8):
                for c in range(3):
                    AH[0, c, i, z0:z0 + 8, :] = zero8
                    AH[1, c, i, z0:z0 + 8, :] = zero8
                for c in range(2):
                    MH[c, i, z0:z0 + 8, :] = zero8

    def clear(x):
        for c in range(3):
            for z0 in range(8, 40, 8):
                U[0, c, x, z0:z0 + 8, :] = zero8
                U[1, c, x, z0:z0 + 8, :] = zero8
                S[c, x, z0:z0 + 8, :] = zero8

    @pl.when(gx == 0)
    def _():
        clear(0)
        clear(1)

    @pl.when(gx == nx - 1)
    def _():
        clear(10)
        clear(11)

    INNER, ON, OFF = 0, 1, 2

    def side(part):
        return core if part == OFF else 1 - core

    def u_copy(cur, part):
        s = side(part)
        index = 2 * cur + part - 1
        return pltpu.make_async_remote_copy(
            src_ref=U.at[cur, :, pl.ds(2 + 6 * s, 2), 8:40, :], dst_ref=U.at[cur, :, pl.ds(10 - 10 * s, 2), 8:40, :],
            send_sem=send_u.at[index], recv_sem=recv_u.at[index],
            device_id=(gx - 1 + 2 * s, gy), device_id_type=MESH)

    def s_copy():
        s = side(ON)
        return pltpu.make_async_remote_copy(
            src_ref=S.at[0:3, pl.ds(2 + 6 * s, 2), 8:40, :], dst_ref=S.at[0:3, pl.ds(10 - 10 * s, 2), 8:40, :],
            send_sem=send_s, recv_sem=recv_s, device_id=(gx - 1 + 2 * s, gy), device_id_type=MESH)

    def far_copy(src, dst, send, recv):
        return pltpu.make_async_remote_copy(
            src_ref=src, dst_ref=dst, send_sem=send, recv_sem=recv,
            device_id=(gx - 1 + 2 * turn, gy), device_id_type=MESH)

    def partial_copy(parity):
        return far_copy(SA, AH.at[parity], send_a.at[parity], recv_a.at[parity])

    def moduli_copy():
        return far_copy(MET.at[3:5, pl.ds(6 * turn, 2)], MH, moduli_sem.at[0], moduli_sem.at[1])

    def u_start(cur, part):
        if part == ON:
            u_copy(cur, part).start()
        else:
            @pl.when(has_off)
            def _():
                u_copy(cur, part).start()

    def u_wait(cur, part):
        if part == ON:
            u_copy(cur, part).wait()
        else:
            @pl.when(has_off)
            def _():
                u_copy(cur, part).wait()

    def y_copies(packed, halo, kind, part):
        return [
            pltpu.make_async_remote_copy(
                src_ref=packed.at[part], dst_ref=halo.at[part, 1 - d], send_sem=send_y.at[kind, part, d],
                recv_sem=recv_y.at[kind, part, d], device_id=peer, device_id_type=MESH)
            for d, peer in enumerate((down, up))
        ]

    def y_send(values, packed, halo, kind, part):
        for c in range(3):
            packed[part, c] = values[c]
        for copy in y_copies(packed, halo, kind, part):
            copy.start()

    def y_wait(packed, halo, kind, part):
        for copy in y_copies(packed, halo, kind, part):
            copy.wait()
        result = []
        for c in range(3):
            lo = jnp.where(gy == 0, zero8, halo[part, 0, c])
            hi = jnp.where(gy == ny - 1, zero8, halo[part, 1, c])
            result.append(jnp.where(low_part, lo, hi))
        return result

    turn = core
    outermost, second, inward = 7 * turn, 1 + 5 * turn, 1 - 2 * turn
    sign = jnp.where(turn == 0, 1.0, -1.0).astype(F32)

    def plane(part, i):
        if part == OFF:
            return second if i == 1 else outermost
        return i + 2 if part == INNER else i + 6 * side(part)

    loads[0].wait()

    def load_u(part):
        def body(i, carry):
            x = plane(part, i)
            packed = list(carry)
            for zb in range(4):
                rows = pl.ds(zb * 64 + x, 8, stride=8)
                k = x * 4 + zb
                for c in range(3):
                    d = disp[c, rows, :]
                    U[0, c, x + 2, zb * 8 + 8:zb * 8 + 16, :] = d
                    packed[c] = jnp.where((lane >> 2) == k, pltpu.roll(d, 4 * k + 2, 1), packed[c])
            return tuple(packed)

        if part == OFF:
            return body(1, body(0, (zero8,) * 3))
        return lax.fori_loop(0, 4 if part == INNER else 2, body, (zero8,) * 3)

    first = [load_u(INNER), load_u(ON), load_u(OFF)]
    pl.semaphore_wait(barrier, 32)
    for part in (OFF, ON):
        u_start(0, part)
    for part in (INNER, OFF, ON):
        y_send(first[part], PU, HU, 0, part)

    for copy in loads[1:]:
        copy.wait()

    @pl.loop(0, 8)
    def _(x):
        for zb in range(4):
            rows = pl.ds(zb * 64 + x, 8, stride=8)
            zs = slice(zb * 8, zb * 8 + 8)
            zu = slice(zb * 8 + 8, zb * 8 + 16)
            MET[0, x, zs, :] = slopes[0, rows, :]
            MET[1, x, zs, :] = slopes[1, rows, :]
            MET[2, x, zs, :] = stretch[rows, :]
            MET[3, x, zs, :] = moduli[0, rows, :] * (1.0 / 12.0)
            MET[4, x, zs, :] = moduli[1, rows, :] * (1.0 / 12.0)
            MET[5, x, zs, :] = buoy[rows, :] * (DT * DT / 12.0)
            for c in range(3):
                U[1, c, x + 2, zu, :] = U[0, c, x + 2, zu, :] - DT * vel[c, rows, :]

    @pl.when(has_off)
    def _():
        moduli_copy().start()

    spread[...] = jnp.zeros((128, 128), F32)
    for n in range(STEPS):
        spread[pl.ds(0, 64, stride=2), :] = probes[n] * (1.0 / (2.0 * DT))
        hi, mid, lo = split(spread[...])
        for i, term in enumerate((hi, mid, hi, lo, mid, hi)):
            PE[n, 128 * i:128 * i + 128, :] = term
    SK[...] = jnp.zeros_like(SK)

    def sketch(n, outer):
        where = (0, 3) if outer else (1, 2)
        hi, mid, lo = split(jnp.concatenate(
            [RATE[c, 2 * xh, pl.ds(0, 16, stride=2), :] for xh in where for c in range(3)], axis=0))
        term = jnp.dot(
            jnp.concatenate([hi, hi, mid, hi, mid, lo], axis=1), PE[n], preferred_element_type=F32)
        for i, xh in enumerate(where):
            SK[48 * xh:48 * xh + 48, :] += term[48 * i:48 * i + 48, :]

    def over_planes(part, planes, cell, put):
        def body(i, packed):
            cells = [(plane(part, i * planes + j), zb, j) for j in range(planes) for zb in range(4)]
            values = [cell(*where) for where in cells]
            packed = list(packed)
            for (x, zb, j), value in zip(cells, values):
                edge = put(x, zb, value, j)
                if edge is None:
                    continue
                k = x * 4 + zb
                here = (lane >> 2) == k
                for c in range(3):
                    packed[c] = jnp.where(here, pltpu.roll(edge[c], 4 * k + 2, 1), packed[c])
            return tuple(packed)

        if part != INNER:
            return body(0, (zero8,) * 3)
        return lax.fori_loop(0, 4 // planes, body, (zero8,) * 3)

    def stress(cur, part, halos):
        def d_x(c, x, zu, j):
            if part != OFF:
                return combine(U[cur, c, x, zu, :], U[cur, c, x + 1, zu, :],
                               U[cur, c, x + 3, zu, :], U[cur, c, x + 4, zu, :])
            ahead, second_ahead = U[cur, c, x + 2 + inward, zu, :], U[cur, c, x + 2 + 2 * inward, zu, :]
            if j == 1:
                ahead = ahead - U[cur, c, x + 2 - inward, zu, :]
            return sign * (8.0 * ahead - second_ahead)

        def cell(x, zb, j):
            z0 = zb * 8
            zs, zu = slice(z0, z0 + 8), slice(z0 + 8, z0 + 16)
            k = x * 4 + zb
            sx, sy, st = MET[0, x, zs, :], MET[1, x, zs, :], MET[2, x, zs, :]
            lam, mu = MET[3, x, zs, :], MET[4, x, zs, :]
            g = []
            for c in range(3):
                f = U[cur, c, x + 2, zu, :]
                dx = d_x(c, x, zu, j)
                dr = combine(*[U[cur, c, x + 2, z0 + o:z0 + o + 8, :] for o in (6, 7, 9, 10)])
                dy = combine(*shifted(f, pltpu.roll(halos[c], 126 - 4 * k, 1), lane))
                g.append((dx + sx * dr, dy + sy * dr, st * dr))
            pressure = lam * (g[0][0] + g[1][1] + g[2][2])
            mu2 = mu + mu
            return (pressure + mu2 * g[0][0], mu * (g[0][1] + g[1][0]), mu * (g[0][2] + g[2][0]),
                    pressure + mu2 * g[1][1], mu * (g[1][2] + g[2][1]), pressure + mu2 * g[2][2])

        def put(x, zb, value, j):
            for i in range(6):
                S[i, x + 2, zb * 8 + 8:zb * 8 + 16, :] = value[i]
            if part == OFF:
                for i in range(3):
                    SA[i, x - 6 * turn, zb * 8:zb * 8 + 8, :] = value[i]
                return None
            return value[1], value[3], value[4]

        return over_planes(part, 2, cell, put)

    def added(first, near, j):
        return first - 8.0 * near if j == 0 else near

    def complete(cur):
        def cell(x, zb, j):
            zs, zu = slice(zb * 8, zb * 8 + 8), slice(zb * 8 + 8, zb * 8 + 16)
            lam, mu = MET[3, x, zs, :], MET[4, x, zs, :]
            at = outermost + 2 - inward
            dx = [sign * added(U[cur, c, at - inward, zu, :], U[cur, c, at, zu, :], j) for c in range(3)]
            side_pressure = lam * dx[0]
            return (S[0, x + 2, zu, :] + (side_pressure + (mu + mu) * dx[0]), S[1, x + 2, zu, :] + mu * dx[1],
                    S[2, x + 2, zu, :] + mu * dx[2], S[3, x + 2, zu, :] + side_pressure,
                    S[5, x + 2, zu, :] + side_pressure, S[4, x + 2, zu, :])

        def put(x, zb, value, j):
            zu = slice(zb * 8 + 8, zb * 8 + 16)
            for i, row in enumerate((0, 1, 2, 3, 5)):
                S[row, x + 2, zu, :] = value[i]
            return value[1], value[3], value[5]

        return over_planes(OFF, 2, cell, put)

    def complete_beyond(cur, parity):
        for j in range(2):
            at = 1 - turn if j == 0 else turn
            for zb in range(4):
                zs, zu = slice(zb * 8, zb * 8 + 8), slice(zb * 8 + 8, zb * 8 + 16)
                lam, mu = MH[0, at, zs, :], MH[1, at, zs, :]
                dx = [-sign * added(U[cur, c, second + 2, zu, :], U[cur, c, outermost + 2, zu, :], j)
                      for c in range(3)]
                scale = (lam + (mu + mu), mu, mu)
                for c in range(3):
                    S[c, outermost + 2 - (1 + j) * inward, zu, :] = AH[parity, c, at, zs, :] + scale[c] * dx[c]

    def forces(cur, part, halos):
        old = 1 - cur

        def cell(x, zb, _):
            z0 = zb * 8
            zs, zu = slice(z0, z0 + 8), slice(z0 + 8, z0 + 16)
            k = x * 4 + zb
            sx, sy, st, b = (MET[j, x, zs, :] for j in (0, 1, 2, 5))

            def d_x(j):
                return combine(S[j, x, zu, :], S[j, x + 1, zu, :], S[j, x + 3, zu, :], S[j, x + 4, zu, :])

            def d_y(j, h):
                return combine(*shifted(S[j, x + 2, zu, :], pltpu.roll(h, 126 - 4 * k, 1), lane))

            dr = [combine(*[S[j, x + 2, z0 + o:z0 + o + 8, :] for o in (6, 7, 9, 10)]) for j in range(6)]
            acc = (
                d_x(0) + sx * dr[0] + d_y(1, halos[0]) + sy * dr[1] + st * dr[2],
                d_x(1) + sx * dr[1] + d_y(3, halos[1]) + sy * dr[3] + st * dr[4],
                d_x(2) + sx * dr[2] + d_y(4, halos[2]) + sy * dr[4] + st * dr[5],
            )
            moved = []
            for c in range(3):
                u, p = U[cur, c, x + 2, zu, :], U[old, c, x + 2, zu, :]
                fol = (u + u - p) + b * acc[c]
                moved.append((fol, fol - p))
            return moved

        def put(x, zb, value, _):
            z0 = zb * 8
            for c in range(3):
                U[old, c, x + 2, z0 + 8:z0 + 16, :] = value[c][0]
                RATE[c, x, z0:z0 + 8, :] = value[c][1]
            return [v[0] for v in value]

        return over_planes(part, 2, cell, put)

    def step(n, carry):
        cur = lax.rem(n, 2)
        more = n < STEPS - 1
        packed = stress(cur, INNER, y_wait(PU, HU, 0, INNER))
        y_send(packed, PS, HS, 1, INNER)
        stress(cur, OFF, y_wait(PU, HU, 0, OFF))

        @pl.when(has_off)
        def _():
            partial_copy(cur).start()

        halos = y_wait(PU, HU, 0, ON)
        u_wait(cur, ON)
        packed = stress(cur, ON, halos)
        s_copy().start()
        y_send(packed, PS, HS, 1, ON)

        @pl.when(n > 0)
        def _():
            sketch(n - 1, True)

        u_wait(cur, OFF)
        packed = complete(cur)
        y_send(packed, PS, HS, 1, OFF)

        packed = forces(cur, INNER, y_wait(PS, HS, 1, INNER))

        @pl.when(more)
        def _():
            y_send(packed, PU, HU, 0, INNER)

        sketch(n, False)
        moved = []
        for part in (ON, OFF):
            halos = y_wait(PS, HS, 1, part)
            if part == ON:
                s_copy().wait()
            else:
                @pl.when(has_off)
                def _():
                    partial_copy(cur).wait()

                @pl.when(has_off & (n == 0))
                def _():
                    moduli_copy().wait()

                complete_beyond(cur, cur)
            packed = forces(cur, part, halos)

            moved.append(packed)

        @pl.when(more)
        def _():
            for part in (OFF, ON):
                y_send(moved[part - 1], PU, HU, 0, part)
                u_start(1 - cur, part)

        return carry

    lax.fori_loop(0, STEPS, step, 0)
    sketch(STEPS - 1, True)
    for g in range(8):
        for xh in range(4):
            PIECES[g, 6 * xh:6 * xh + 6, :] = SK[xh * 48 + 6 * g:xh * 48 + 6 * g + 6, :]

    def piece(g, slot):
        return pltpu.make_async_remote_copy(
            src_ref=PIECES.at[g], dst_ref=RB.at[slot], send_sem=s0.at[g], recv_sem=r0.at[slot],
            device_id=(gx, g), device_id_type=MESH)

    @pl.loop(0, 7, unroll=7)
    def _(i):
        piece(lax.rem(gy + far_first(i, 4), 8), gy).start()

    RB[gy] = PIECES[gy]

    final = STEPS % 2

    @pl.loop(0, 8)
    def _(x):
        for zb in range(4):
            for c in range(3):
                out[c, pl.ds(zb * 64 + x, 8, stride=8), :] = U[final, c, x + 2, zb * 8 + 8:zb * 8 + 16, :]

    @pl.loop(1, 8, unroll=7)
    def _(d):
        g = lax.rem(gy + d, 8)
        piece(g, g).wait()

    total = RB[0]
    for g in range(1, 8):
        total = total + RB[g]
    tall[...] = total
    hi, mid, lo = (term.astype(F32) for term in split(total))
    GL[...] = lax.dot_general(
        jnp.concatenate([hi, hi, mid, hi, mid, lo], axis=0).astype(BF16),
        jnp.concatenate([hi, mid, hi, lo, mid, hi], axis=0).astype(BF16),
        (((0,), (0,)), ((), ())), preferred_element_type=F32).reshape(16, 8, 128)

    def group(dev, me, src, dst, send, recv):
        def make(slot, peer):
            return pltpu.make_async_remote_copy(
                src_ref=src(peer), dst_ref=dst.at[slot], send_sem=send.at[peer], recv_sem=recv.at[slot],
                device_id=dev(peer), device_id_type=MESH)

        @pl.loop(0, 15, unroll=5)
        def _(i):
            make(me, lax.rem(me + far_first(i, 8), 16)).start()

        def finish():
            @pl.loop(1, 16, unroll=5)
            def _(d):
                peer = lax.rem(me + d, 16)
                make(peer, peer).wait_recv()

        def sent():
            @pl.loop(1, 16, unroll=5)
            def _(d):
                peer = lax.rem(me + d, 16)
                make(peer, peer).wait_send()

        return finish, sent

    def summed(ref):
        parts = [ref[i] for i in range(16)]
        while len(parts) > 1:
            parts = [parts[i] + parts[i + 1] for i in range(0, len(parts), 2)]
        return parts[0]

    finish, sent_a = group(b_dev, b_me, lambda p: GL.at[p], RA, s1, r1)
    RA[b_me] = GL[b_me]
    finish()
    part = summed(RA)
    PA[...] = part
    finish, sent_b = group(a_dev, a_me, lambda p: PA, RBB, s2, r2)
    RBB[a_me] = part
    finish()
    whole = summed(RBB)
    GS[...] = whole
    finish, sent_c = group(b_dev, b_me, lambda p: GS, gram, s3, r3)
    gram[b_me] = whole
    sent_a()
    sent_b()
    finish()
    sent_c()


def wave(disp, vel, slopes, stretch, moduli, buoy, probes):
    sem = pltpu.SemaphoreType.DMA
    buffers = [
        (3, 256, 128), (3, 256, 128), (2, 256, 128), (256, 128), (2, 256, 128), (256, 128), (STEPS, 64, 128),
        (128, 128), (2, 3, 12, ZP, 128), (6, 12, ZP, 128), (6, 8, 32, 128), (3, 8, 32, 128), (192, 128),
        (3, 3, 8, 128), (3, 3, 8, 128), (3, 2, 3, 8, 128), (3, 2, 3, 8, 128),
        (3, 2, 32, 128), (2, 3, 2, 32, 128), (2, 2, 32, 128), (8, 24, 128), (8, 24, 128), (16, 8, 128), (16, 8, 128), (8, 128), (16, 8, 128), (8, 128),
    ]
    sems = [(7,), (4,), (4,), (), (), (2, 3, 2), (2, 3, 2), (2,), (2,), (2,)] + [(8,)] * 2 + [(16,)] * 6
    return pl.pallas_call(
        wave_kernel,
        name="wave",
        out_shape=(
            jax.ShapeDtypeStruct((24, 128), F32),
            jax.ShapeDtypeStruct((16, 8, 128), F32),
            jax.ShapeDtypeStruct((3, 256, 128), F32),
        ),
        in_specs=[pl.BlockSpec(memory_space=pltpu.MemorySpace.HBM)] * 7,
        out_specs=[pl.BlockSpec(memory_space=VMEM)] * 3,
        scratch_shapes=[pltpu.VMEM(shape, F32) for shape in buffers[:7]]
        + [pltpu.VMEM((STEPS, 768, 128), BF16)]
        + [pltpu.VMEM(shape, F32) for shape in buffers[7:]] + [sem(shape) for shape in sems],
        compiler_params=pltpu.CompilerParams(
            collective_id=0, has_side_effects=True, vmem_limit_bytes=VMEM_LIMIT),
    )(*[pltpu.with_memory_space_constraint(x, pltpu.MemorySpace.HBM)
        for x in (disp, vel, slopes, stretch, moduli, buoy, probes)])


def factor_kernel(scale, gram, tall, disp, basis, factor, out, sem):
    leave = pltpu.make_async_copy(disp, out, sem)
    leave.start()
    lane = lanes()
    sub = lax.broadcasted_iota(jnp.int32, (8, 128), 0)
    a = [gram[i] for i in range(16)]
    for b in range(16):
        j0 = 8 * b
        inside = (lane >= j0) & (lane < j0 + 8)
        cols = [jnp.broadcast_to(a[b][:, j0 + t:j0 + t + 1], (8, 128)) for t in range(8)]
        d = [[jnp.broadcast_to(cols[t][s:s + 1, :], (8, 128)) if t >= s else None for t in range(8)]
             for s in range(8)]
        inv = [None] * 8
        m = [[None] * 8 for _ in range(8)]
        for s in range(8):
            inv[s] = 1.0 / d[s][s]
            for t in range(s + 1, 8):
                m[s][t] = d[s][t] * inv[s]
                for q in range(t, 8):
                    d[t][q] = d[t][q] - m[s][t] * d[s][q]
        unit = [None] * 8
        fresh = a[b]
        for t in range(8):
            x = jnp.broadcast_to(a[b][t:t + 1, :], (8, 128))
            for s in range(t):
                x = jnp.where(lane == j0 + s, 0.0, x) - m[s][t] * unit[s]
            unit[t] = jnp.where(lane == j0 + t, 1.0, x)
            fresh = jnp.where(sub == t, x, fresh)
        a[b] = fresh
        below = [jnp.where((lane > j0 + t) & inside, 0.0, unit[t]) for t in range(8)]
        for i in range(b + 1, 16):
            c = [jnp.broadcast_to(a[i][:, j0 + s:j0 + s + 1], (8, 128)) for s in range(8)]
            x = jnp.where(inside, 0.0, a[i])
            for s in range(8):
                ms = c[s] * inv[s]
                for t in range(s + 1, 8):
                    c[t] = c[t] - ms * d[s][t]
                x = x - ms * below[s]
            a[i] = x
    inverse = []
    for i in range(16):
        rows = sub + 8 * i
        diag = jnp.sum(jnp.where(lane == rows, a[i], 0.0), axis=1, keepdims=True)
        root = lax.rsqrt(diag)
        factor[8 * i:8 * i + 8, :] = jnp.where(lane >= rows, a[i], 0.0) * root
        inverse.append(jnp.where(lane == rows, 1.0, jnp.where(lane < rows, a[i], 0.0)) * (root * scale))
    inverse = jnp.concatenate(inverse, axis=0)
    q = lax.dot_general(
        tall[...], inverse, (((1,), (1,)), ((), ())), precision=HIGH, preferred_element_type=F32)
    for xh in range(4):
        for r in range(6):
            basis[r, xh:xh + 1, :] = q[6 * xh + r:6 * xh + r + 1, :]
    leave.wait()


def finish(gram, tall, disp, scale):
    return pl.pallas_call(
        functools.partial(factor_kernel, scale),
        name="factor",
        out_shape=(
            jax.ShapeDtypeStruct((6, 4, 128), F32),
            jax.ShapeDtypeStruct((128, 128), F32),
            jax.ShapeDtypeStruct((3, 256, 128), F32),
        ),
        in_specs=[pl.BlockSpec(memory_space=VMEM)] * 3,
        out_specs=[pl.BlockSpec(memory_space=VMEM)] * 2 + [pl.BlockSpec(memory_space=pltpu.MemorySpace.HBM)],
        scratch_shapes=[pltpu.SemaphoreType.DMA],
        compiler_params=pltpu.CompilerParams(vmem_limit_bytes=VMEM_LIMIT),
    )(gram, tall, disp)


def shards(displacement, velocity, slopes, stretch, moduli, buoyancy, probes):
    tall, gram, moved = wave(
        displacement.reshape(3, 256, 128), velocity.reshape(3, 256, 128), slopes.reshape(2, 256, 128),
        stretch.reshape(256, 128), moduli.reshape(2, 256, 128), buoyancy.reshape(256, 128), probes)
    rows = tall.shape[0] * lax.axis_size("gx") * lax.axis_size("gy")
    basis, factor, moved = finish(gram, tall, moved, math.sqrt(rows))
    return moved.reshape(3, 32, 8, 128), jnp.transpose(basis, (1, 0, 2)), factor


def solution(mesh):
    in_specs = (
        P(None, None, "gx", "gy"),
        P(None, None, "gx", "gy"),
        P(None, None, "gx", "gy"),
        P(None, "gx", "gy"),
        P(None, None, "gx", "gy"),
        P(None, "gx", "gy"),
        P(None, "gy", None),
    )
    out_specs = (P(None, None, "gx", "gy"), P("gx", "gy", None), P())
    return jax.shard_map(shards, mesh=mesh, in_specs=in_specs, out_specs=out_specs, check_vma=False)
```
